32 devices in a mesh: wide: 8 (over z, x), narrow: 4 (over y, core).
Axes of the slice: x: 2, y: 2, z: 4, core: 2. Of those that a mesh axis runs over, the one named last changes fastest.
Arguments:
- hidden_in: bfloat16 [16384, 768], P(('wide', 'narrow')), may hold values from -6 to 6
- out_grad: bfloat16 [16384, 768], P(('wide', 'narrow')), may hold values from -6 to 6
- pair_lengths: int32 [32, 4], P(('wide', 'narrow')), may hold values from 1 to 256, 512 in all within a row
- params: float32 [4, 1772544], P('narrow', 'wide'), may hold values from -4 to 4, as said below
- momentum: float32 [4, 1772544], P('narrow', 'wide'), may hold values from -2 to 2, as said below
- average: float32 [4, 1772544], P('narrow', 'wide'), may hold values from -4 to 4, as said below
Outputs:
- block_out: bfloat16 [16384, 768], P(('wide', 'narrow'))
- in_grad: float32 [16384, 768], P(('wide', 'narrow'))
- grads: float32 [4, 1772544], P('narrow', 'wide')
- new_params: float32 [4, 1772544], P('narrow', 'wide')
- new_momentum: float32 [4, 1772544], P('narrow', 'wide')
- new_average: float32 [4, 1772544], P('narrow', 'wide')
- params_bf16: bfloat16 [4, 1772544], P('narrow', 'wide')
The draws below stay inside these ranges and needn't reach their ends.
Inputs may be any that keep to these rules, and one draw needn't show every extreme that they name: `pair_lengths`: each row's 4 lengths sum to 512, and some pair of each row has exactly 256 tokens. `params`: independent entries. `momentum`: independent entries. `average`: independent entries.
All inputs are finite; a program needn't handle non-finite values.
Results may differ from the reference program's by a relative error of at most 0.015.
Values may be sent and summed in bfloat16 or wider, within the bound.
No kernel may reach another device: no remote copies, remote signals or barrier semaphores. Data moves between devices by JAX's collectives and lax.ppermute only.
A program may use at most 128 MiB of HBM per device.

```python
import math
import jax
import jax.numpy as jnp
import numpy as np
from jax import lax

D = 768
HEADS = 12
FF = 3072
HD = 64
BUCKETS = 256
L = 512
PAIRS = 4
MOSTLEN = 256
ROWS_DEV = 1
ROWS = 32
TOKENS = 16384
P_SIZE = 7090176
PN = 1772544
N_NARROW = 4


def layout_scales():
    ranks = P_SIZE // PN
    width_part = D // ranks
    position = jnp.arange(PN)
    bounds = [3 * D * width_part, width_part * D, D * (FF // ranks), FF // ranks * D, 2 * width_part, FF // ranks, BUCKETS * (HEADS // ranks)]
    spreads = [D ** (-0.5), 4.0 * D ** (-0.5), D ** (-0.5), FF ** (-0.5), 0.3, 0.3, 1.0]
    spread = jnp.zeros((PN,), jnp.float32)
    low_edge = 0
    for extent, deviation in zip(bounds, spreads):
        inside = (position >= low_edge) & (position < low_edge + extent)
        spread = jnp.where(inside, deviation, spread)
        low_edge += extent
    rank_index = jnp.arange(ranks)[:, None]
    global_vec = rank_index * (6 * D // ranks) + (position[None, :] - low_edge)
    vec_row = global_vec // D
    in_vec = position[None, :] >= low_edge
    is_gain = in_vec & ((vec_row == 2) | (vec_row == 4))
    spread_grid = jnp.where(in_vec, jnp.where(is_gain, 0.18, 0.3), spread[None, :] + jnp.zeros((ranks, 1), jnp.float32))
    center_grid = jnp.where(is_gain, 1.0, 0.0).astype(jnp.float32)
    return (spread_grid.astype(jnp.float32), center_grid)


def unit_draw(key):
    ranks = P_SIZE // PN
    return jnp.clip(jax.random.normal(key, (ranks, PN), jnp.float32), -4.0, 4.0)


def draw_params(key, part):
    spread, center = layout_scales()
    return center + spread * unit_draw(jax.random.fold_in(key, 11))


def draw_momentum(key, part):
    spread, center = layout_scales()
    return 0.5 * spread * unit_draw(jax.random.fold_in(key, 23))


def draw_average(key, part):
    spread, center = layout_scales()
    return center + spread * unit_draw(jax.random.fold_in(key, 37))


def level_of(rng, shape, shards, least, high):
    gain, own = 1.0, jax.random.fold_in(rng, 6)
    for dim, parts in shards:
        draws = jnp.exp(jax.random.uniform(jax.random.fold_in(own, dim), (parts,), jnp.float32, least / len(shards), high / len(shards)))
        gain = gain * jnp.repeat(draws, shape[dim] // parts).reshape([-1 if axis == dim else 1 for axis in range(len(shape))])
    return gain


def profile(number_of, total, limit, skew):
    loads = [(1 << 20) // math.isqrt(grade ** skew) + 1 for grade in range(2, number_of + 1)]
    spare, given = total - limit - (number_of - 1), [1] * (number_of - 1)
    while spare > 0:
        movable = [i for i in range(number_of - 1) if given[i] < limit]
        mass, remaining = sum([loads[i] for i in movable]), spare
        for i in movable:
            extra = min(limit - given[i], max(1, remaining * loads[i] // mass), spare)
            given[i] = given[i] + extra
            spare = spare - extra
    return np.array([limit] + given)


def uneven(stream_key, count, total, reach, skew):
    if count == 2:
        one = jax.random.randint(stream_key, (), max(1, total - reach), min(reach, total - 1) + 1)
        return jnp.stack([one, total - one])
    sizes = jnp.asarray(profile(count, total, reach, skew), jnp.int32)
    twos = (count - 1) // 2
    source_of, sink = sizes[1:1 + 2 * twos:2], sizes[2:2 + 2 * twos:2]
    margin = jnp.minimum(source_of - 1, reach - sink)
    passed = jax.random.randint(jax.random.fold_in(stream_key, 1), (twos,), 0, 1 << 20) % (margin + 1)
    sizes = sizes.at[1:1 + 2 * twos:2].set(source_of - passed).at[2:2 + 2 * twos:2].set(sink + passed)
    return sizes[jax.random.permutation(jax.random.fold_in(stream_key, 2), count)]


def bell_draw(key, dims, scale, reach, cuts=(), kind=jnp.bfloat16):
    values = scale * jax.random.normal(key, dims, jnp.float32)
    if cuts:
        values = values * level_of(key, dims, cuts, -0.22, 0.18)
    return jnp.clip(values, -reach, reach).astype(kind)


def setup_inputs(seed: int = 0) -> dict:
    key_list = jax.random.split(jax.random.key(seed), 7)
    hidden_in = bell_draw(key_list[0], (TOKENS, D), 1.0, 6.0, ((0, 32),))
    out_grad = bell_draw(key_list[1], (TOKENS, D), 1.0, 6.0, ((0, 32),))
    pair_lengths = jax.vmap(lambda own: uneven(own, PAIRS, L, MOSTLEN, 2))(jax.random.split(key_list[2], ROWS)).reshape((ROWS, PAIRS)).astype(jnp.int32)
    params = draw_params(jax.random.fold_in(key_list[6], 71), 0)
    momentum = draw_momentum(jax.random.fold_in(key_list[6], 71), 0)
    average = draw_average(jax.random.fold_in(key_list[6], 71), 0)
    return {"hidden_in": hidden_in, "out_grad": out_grad, "pair_lengths": pair_lengths, "params": params, "momentum": momentum, "average": average}


@jax.custom_vjp
def low(v):
    return lax.optimization_barrier(v.astype(jnp.bfloat16)).astype(jnp.float32)

@jax.custom_vjp
def low_back(v):
    return v

def low_keep(v):
    return (low(v), None)

def low_pass(kept, grad):
    return (grad,)

def back_keep(v):
    return (v, None)

def back_low(kept, grad):
    return (low(grad),)
low.defvjp(low_keep, low_pass)
low_back.defvjp(back_keep, back_low)

def matmul(first_op, second_op):
    return jnp.dot(first_op, second_op, precision=lax.Precision.HIGHEST, preferred_element_type=jnp.float32)

def unpack_rank(flat_rank):
    ranks = N_NARROW
    width_part = D // ranks
    extents = [(D, 3, width_part), (width_part, D), (D, FF // ranks), (FF // ranks, D), (2, width_part), (FF // ranks,), (BUCKETS, HEADS // ranks), (6 * D // ranks,)]
    pieces = []
    offset = 0
    for extent in extents:
        amount = math.prod(extent)
        pieces.append(lax.slice_in_dim(flat_rank, offset, offset + amount).reshape(extent))
        offset += amount
    return pieces

def assemble(params_grid):
    ranks = [unpack_rank(params_grid[index]) for index in range(N_NARROW)]
    w_qkv = jnp.concatenate([piece[0] for piece in ranks], axis=2).reshape(D, 3 * D)
    w_out = jnp.concatenate([piece[1] for piece in ranks], axis=0)
    w_up = jnp.concatenate([piece[2] for piece in ranks], axis=1)
    w_down = jnp.concatenate([piece[3] for piece in ranks], axis=0)
    qv_bias = jnp.concatenate([piece[4] for piece in ranks], axis=1)
    up_bias = jnp.concatenate([piece[5] for piece in ranks], axis=0)
    bias_table = jnp.concatenate([piece[6] for piece in ranks], axis=1)
    vectors = jnp.concatenate([piece[7] for piece in ranks], axis=0).reshape(6, D)
    return (w_qkv, w_out, w_up, w_down, qv_bias, up_bias, bias_table, vectors)

def packing(row_lengths):
    pair_ends = jnp.cumsum(row_lengths).astype(jnp.int32)
    pair_starts = (pair_ends - row_lengths).astype(jnp.int32)
    position = jnp.arange(L, dtype=jnp.int32)
    segment = lax.optimization_barrier(jnp.sum((position[:, None] >= pair_ends[None, :]).astype(jnp.int32), axis=1)).astype(jnp.int32)
    owner_mask = segment[:, None] == jnp.arange(PAIRS, dtype=jnp.int32)[None, :]
    restart = (position - lax.optimization_barrier(jnp.sum(jnp.where(owner_mask, pair_starts[None, :], 0), axis=1))).astype(jnp.int32)
    same_pair = segment[:, None] == segment[None, :]
    bucket = jnp.clip(restart[None, :] - restart[:, None] + BUCKETS // 2, 0, BUCKETS - 1).astype(jnp.int32)
    return (same_pair, bucket)

def layer_norm(values, gain_row, shift_row):
    centred = values - lax.optimization_barrier(jnp.mean(values, axis=-1, keepdims=True))
    normed = centred * lax.rsqrt(lax.optimization_barrier(jnp.mean(centred * centred, axis=-1, keepdims=True)) + 1e-05)
    return normed * gain_row + shift_row

def gelu_exact(values):
    return 0.5 * values * (1.0 + lax.erf(values * (1.0 / math.sqrt(2.0))))

def attend_row(qkv_row, bias_table, same_pair, bucket):
    head_scale = 1.0 / math.sqrt(HD)
    query_heads = qkv_row[:, :D].reshape(L, HEADS, HD)
    key_heads = qkv_row[:, D:2 * D].reshape(L, HEADS, HD)
    value_heads = qkv_row[:, 2 * D:].reshape(L, HEADS, HD)
    logits = jnp.einsum('ihd,jhd->hij', query_heads, key_heads, precision=lax.Precision.HIGHEST) * head_scale
    position_bias = jnp.transpose(jnp.take(bias_table, bucket, axis=0), (2, 0, 1))
    logits = low_back(logits + position_bias)
    logits = jnp.where(same_pair[None], logits, -1000000000.0)
    attn_probs = jax.nn.softmax(logits, axis=-1)
    mixed_heads = jnp.einsum('hij,jhd->ihd', low(attn_probs), value_heads, precision=lax.Precision.HIGHEST)
    return mixed_heads.reshape(L, D)

def block_forward(input_float, params_grid, same_pair, bucket):
    w_qkv, w_out, w_up, w_down, qv_bias, up_bias, bias_table, vectors = assemble(low(params_grid))
    qkv_bias = jnp.concatenate([qv_bias[0], jnp.zeros((D,), jnp.float32), qv_bias[1]])
    qkv_all = low(low_back(matmul(input_float, w_qkv) + qkv_bias))
    row_blocks = qkv_all.reshape(-1, L, 3 * D)
    attend = jax.checkpoint(attend_row)
    mixed_rows = lax.map(lambda element: attend(element[0], bias_table, element[1], element[2]), (row_blocks, same_pair, bucket))
    mixed_all = low(low_back(mixed_rows.reshape(-1, D)))
    attn_out = low_back(matmul(mixed_all, w_out) + vectors[0])
    first_norm = layer_norm(input_float + attn_out, vectors[2], vectors[3])
    up_proj = low_back(matmul(low(first_norm), w_up) + up_bias)
    activated = low(gelu_exact(up_proj))
    down_proj = low_back(matmul(activated, w_down) + vectors[1])
    return layer_norm(first_norm + down_proj, vectors[4], vectors[5])

def reference(hidden_in, out_grad, pair_lengths, params, momentum, average):
    group_rows = ROWS_DEV * N_NARROW
    group_tokens = group_rows * L
    inputs_all = hidden_in.astype(jnp.float32).reshape(-1, group_tokens, D)
    cotangents = out_grad.astype(jnp.float32).reshape(-1, group_tokens, D)
    lengths_all = pair_lengths.reshape(-1, group_rows, PAIRS)

    def group_step(summed, element):
        input_float, grad_float, row_lengths = element
        same_pair, bucket = jax.vmap(packing)(row_lengths)

        def forward(input_value, params_value):
            return block_forward(input_value, params_value, same_pair, bucket)
        block_out, pullback = jax.vjp(forward, input_float, params)
        input_grad, param_grad = pullback(grad_float)
        return (summed + param_grad, (block_out.astype(jnp.bfloat16), input_grad))
    grads, outputs = lax.scan(group_step, jnp.zeros_like(params), (inputs_all, cotangents, lengths_all))
    block_out, input_grad = outputs
    step_rate = 1.0 / (32.0 * math.sqrt(TOKENS))
    new_momentum = 0.5 * momentum + step_rate * grads
    new_params = params - (step_rate * grads + 0.5 * new_momentum)
    new_average = 0.5 * average + 0.5 * new_params
    return (block_out.reshape(-1, D), input_grad.reshape(-1, D), grads, new_params, new_momentum, new_average, new_params.astype(jnp.bfloat16))
```

```python
import functools
import math

import jax
import jax.numpy as jnp
from jax import lax
from jax.experimental import pallas as pl
from jax.experimental.pallas import tpu as pltpu
from jax.sharding import PartitionSpec as P

D = 768
HEADS = 12
FF = 3072
HD = 64
BUCKETS = 256
L = 512
RANKS = 4
PART = D // RANKS
HPR = HEADS // RANKS
QKV_ROWS = 3 * PART
TILE_ROWS = 16
MAT_ROWS = 3 * D
PAD_ROWS = MAT_ROWS + TILE_ROWS
BLK = 128
NBLK = L // BLK
NEG = -1000000000.0
VMEM_LIMIT = 60 * 1024 * 1024
BF = jnp.bfloat16
F32 = jnp.float32


def mm(a, b):
    return jnp.dot(a, b, preferred_element_type=F32)


def mm_nt(a, b):
    return lax.dot_general(a, b, (((1,), (1,)), ((), ())), preferred_element_type=F32)


def mm_tn(a, b):
    return lax.dot_general(a, b, (((0,), (0,)), ((), ())), preferred_element_type=F32)


def qkv_pieces():
    for b in range(2):
        for j in range(4):
            for c in range(3):
                t, q = divmod(3 * j + c, 4)
                yield 288 * b + 96 * t, PART * q, PART * j + 96 * b, PART * c


def column_order():
    d = lax.broadcasted_iota(jnp.int32, (D, D), 0)
    n = lax.broadcasted_iota(jnp.int32, (D, D), 1)
    j = (n >= PART).astype(jnp.int32) + (n >= 2 * PART).astype(jnp.int32) + (n >= 3 * PART).astype(jnp.int32)
    return (d == 4 * (n - PART * j) + j).astype(F32).astype(BF)


def vector_rows(tail_ref):
    chunks = []
    for r in range(RANKS):
        chunks.append(tail_ref[r, 2:3, 384:768])
        chunks.append(tail_ref[r, 3:4, 0:384])
        chunks.append(tail_ref[r, 3:4, 384:768])
    return [
        jnp.concatenate([chunks[2 * v], chunks[2 * v + 1]], axis=1).astype(F32) for v in range(6)
    ]


def normalize(values):
    centred = values - jnp.mean(values, axis=-1, keepdims=True)
    inv = lax.rsqrt(jnp.mean(centred * centred, axis=-1, keepdims=True) + 1e-05)
    return centred * inv, inv


def norm_backward(e, normed, inv):
    return inv * (
        e - jnp.mean(e, axis=-1, keepdims=True) - normed * jnp.mean(e * normed, axis=-1, keepdims=True)
    )


def col_sum(values):
    return jnp.sum(values, axis=0, keepdims=True)


def merge_kernel(wide, rows, g_ref, out_ref):
    for w in range(wide):
        out_ref[0, rows * w : rows * (w + 1), :] = g_ref[0, w, 0:rows, :]
    for w in range(1, wide + 1):
        at = rows * w
        edge = g_ref[0, w - 1, rows : rows + TILE_ROWS, :]
        if w < wide:
            edge = g_ref[0, w, 0:TILE_ROWS, :] + edge
        out_ref[0, at : at + TILE_ROWS, :] = edge


def merge_blocks(g):
    _, wide, cap, _ = g.shape
    return pl.pallas_call(
        functools.partial(merge_kernel, wide, cap - TILE_ROWS),
        grid=(RANKS,),
        in_specs=[pl.BlockSpec((1, wide, cap, D), lambda r: (r, 0, 0, 0))],
        out_specs=pl.BlockSpec((1, PAD_ROWS, D), lambda r: (r, 0, 0)),
        out_shape=jax.ShapeDtypeStruct((RANKS, PAD_ROWS, D), BF),
        compiler_params=pltpu.CompilerParams(vmem_limit_bytes=VMEM_LIMIT),
        name="merge_weights",
    )(g)


def segment_of(pos, len_ref):
    end0 = len_ref[0]
    end1 = end0 + len_ref[1]
    end2 = end1 + len_ref[2]
    return (
        (pos >= end0).astype(jnp.int32)
        + (pos >= end1).astype(jnp.int32)
        + (pos >= end2).astype(jnp.int32)
    )


def att_fwd_kernel(
    len_ref, x_ref, mq_ref, wo_ref, tail_ref,
    qkv_ref, wq_ref, xp_ref, mixed_ref, probs_ref, n1_ref, r1_ref,
    table_s, acc_s,
):
    r = pl.program_id(0)

    @pl.when(r == 0)
    def _():
        xp_ref[...] = mm(x_ref[...], column_order()).astype(BF)
        acc_s[...] = jnp.zeros_like(acc_s)
        src = lax.broadcasted_iota(jnp.int32, (3 * BUCKETS, 3 * BUCKETS), 0)
        dst = lax.broadcasted_iota(jnp.int32, (3 * BUCKETS, 3 * BUCKETS), 1)
        hh = (dst >= BUCKETS).astype(jnp.int32) + (dst >= 2 * BUCKETS).astype(jnp.int32)
        pick = (src == 3 * (dst - BUCKETS * hh) + hh).astype(F32).astype(BF)
        flat = jnp.concatenate(
            [
                jnp.concatenate([tail_ref[k, 1:2, 384:768], tail_ref[k, 2:3, 0:384]], axis=1).astype(F32)
                for k in range(RANKS)
            ]
            + [jnp.zeros((4, D), F32)],
            axis=0,
        ).astype(BF)
        tables = mm(flat, pick)
        for k in range(RANKS):
            for h in range(HPR):
                row = tables[k : k + 1, BUCKETS * h : BUCKETS * (h + 1)]
                table_s[k, h : h + 1, :] = jnp.concatenate(
                    [
                        row,
                        jnp.broadcast_to(row[:, 255:256], (1, BLK)),
                        jnp.broadcast_to(row[:, 0:1], (1, BLK)),
                    ],
                    axis=1,
                )

    for src_row, src_col, dst_row, dst_col in qkv_pieces():
        wq_ref[0, dst_row : dst_row + 96, dst_col : dst_col + PART] = mq_ref[
            0, src_row : src_row + 96, src_col : src_col + PART
        ]
    first = tail_ref[r, 0:1, :]
    bias = jnp.concatenate(
        [first[:, 0:PART], jnp.zeros((1, PART), BF), first[:, PART : 2 * PART]], axis=1
    ).astype(F32)
    qkv = (mm(xp_ref[...], wq_ref[0]) + bias).astype(BF)
    qkv_ref[0] = qkv

    seg_j = segment_of(lax.broadcasted_iota(jnp.int32, (1, L), 1), len_ref)
    table = table_s[r]
    heads = []
    for h in range(HPR):
        q = qkv[:, HD * h : HD * (h + 1)]
        k = qkv[:, PART + HD * h : PART + HD * (h + 1)]
        v = qkv[:, 2 * PART + HD * h : 2 * PART + HD * (h + 1)]
        row = table[h : h + 1, :]
        near = pltpu.roll(jnp.broadcast_to(row, (BLK, 4 * BLK)), 0, 1, stride=1, stride_axis=0)
        far_right = jnp.broadcast_to(row[:, 255:256], (BLK, BLK))
        far_left = jnp.broadcast_to(row[:, 511:512], (BLK, BLK))
        for i in range(NBLK):
            seg_i = segment_of(
                lax.broadcasted_iota(jnp.int32, (BLK, 1), 0) + BLK * i, len_ref
            )
            parts = []
            for jb in range(NBLK):
                delta = jb - i
                if abs(delta) <= 1:
                    parts.append(near[:, BLK * (delta + 1) : BLK * (delta + 2)])
                else:
                    parts.append(far_right if delta > 0 else far_left)
            logits = mm_nt(q[BLK * i : BLK * (i + 1)], k) * 0.125 + jnp.concatenate(parts, axis=1)
            logits = jnp.where(seg_i == seg_j, logits, NEG)
            top = jnp.max(logits, axis=-1, keepdims=True)
            expo = jnp.exp(logits - top)
            total = jnp.sum(expo, axis=-1, keepdims=True)
            probs_ref[0, h, BLK * i : BLK * (i + 1), :] = (expo * (1.0 / total)).astype(BF)
        heads.append(mm(probs_ref[0, h], v))
    mixed = jnp.concatenate(heads, axis=1).astype(BF)
    mixed_ref[0] = mixed
    acc_s[...] += mm(mixed, wo_ref[0])

    @pl.when(r == RANKS - 1)
    def _():
        vec = vector_rows(tail_ref)
        normed, inv = normalize(x_ref[...].astype(F32) + acc_s[...] + vec[0])
        n1_ref[...] = normed
        r1_ref[...] = jnp.broadcast_to(inv, (L, BLK))


def attention_forward(lengths, x, mats):
    whole = lambda *shape: pl.BlockSpec(shape, lambda r, n: (0,) * len(shape))
    per = lambda *shape: pl.BlockSpec((1, *shape), lambda r, n: (r,) + (0,) * len(shape))
    return pl.pallas_call(
        att_fwd_kernel,
        grid_spec=pltpu.PrefetchScalarGridSpec(
            num_scalar_prefetch=1,
            grid=(RANKS,),
            in_specs=[
                whole(L, D),
                pl.BlockSpec((1, QKV_ROWS, D), lambda r, n: (r, 0, 0)),
                pl.BlockSpec((1, PART, D), lambda r, n: (r, 3, 0)),
                pl.BlockSpec((RANKS, TILE_ROWS, D), lambda r, n: (0, MAT_ROWS // TILE_ROWS, 0)),
            ],
            out_specs=[
                per(L, QKV_ROWS),
                per(D, QKV_ROWS),
                whole(L, D),
                per(L, PART),
                per(HPR, L, L),
                whole(L, D),
                whole(L, BLK),
            ],
            scratch_shapes=[pltpu.VMEM((RANKS, 8, 512), F32), pltpu.VMEM((L, D), F32)],
        ),
        out_shape=[
            jax.ShapeDtypeStruct((RANKS, L, QKV_ROWS), BF),
            jax.ShapeDtypeStruct((RANKS, D, QKV_ROWS), BF),
            jax.ShapeDtypeStruct((L, D), BF),
            jax.ShapeDtypeStruct((RANKS, L, PART), BF),
            jax.ShapeDtypeStruct((RANKS, HPR, L, L), BF),
            jax.ShapeDtypeStruct((L, D), F32),
            jax.ShapeDtypeStruct((L, BLK), F32),
        ],
        compiler_params=pltpu.CompilerParams(vmem_limit_bytes=VMEM_LIMIT),
        name="attention_forward",
    )(lengths, x, mats, mats, mats)


def ffn_kernel(
    n1_ref, r1_ref, og_ref, up_ref, down_ref, tail_ref,
    block_ref, du_ref, dd_ref, grad_one_ref, ga_ref, vec_ref, bup_ref,
    fn_s, fl_s, up_s, act_s, down_s, gd_s, gf_s,
):
    step = pl.program_id(0)
    r = lax.rem(step, RANKS)
    inv_root2 = 1.0 / math.sqrt(2.0)

    @pl.when(step == 0)
    def _():
        vec = vector_rows(tail_ref)
        first = n1_ref[...] * vec[2] + vec[3]
        fn_s[...] = first
        fl_s[...] = first.astype(BF)

    @pl.when(step < RANKS)
    def _():
        bias = jnp.concatenate([tail_ref[r, 0:1, 384:768], tail_ref[r, 1:2, 0:384]], axis=1)
        up = mm(fl_s[...], up_ref[0]) + bias.astype(F32)
        up_s[r] = up
        act = (0.5 * up * (1.0 + lax.erf(up * inv_root2))).astype(BF)
        act_s[r] = act
        down = mm(act, down_ref[0])

        @pl.when(step == 0)
        def _():
            down_s[...] = down

        @pl.when(step > 0)
        def _():
            down_s[...] += down

    @pl.when(step == RANKS)
    def _():
        vec = vector_rows(tail_ref)
        normed, inv = normalize(fn_s[...] + down_s[...] + vec[1])
        block_ref[...] = (normed * vec[4] + vec[5]).astype(BF)
        og = og_ref[...].astype(F32)
        vec_ref[4:5, :] = col_sum(og * normed)
        vec_ref[5:6, :] = col_sum(og)
        grad_two = norm_backward(og * vec[4], normed, inv)
        low = grad_two.astype(BF)
        gd_s[...] = low
        vec_ref[1:2, :] = col_sum(low.astype(F32))
        vec_ref[6:8, :] = jnp.zeros((2, D), F32)
        gf_s[...] = grad_two

    @pl.when(step >= RANKS)
    def _():
        gd = gd_s[...]
        dd_ref[0] = mm_tn(act_s[r], gd).astype(BF)
        up = up_s[r]
        slope = 0.5 * (1.0 + lax.erf(up * inv_root2)) + up * jnp.exp(-0.5 * up * up) * (
            1.0 / math.sqrt(2.0 * math.pi)
        )
        gu = (mm_nt(gd, down_ref[0]) * slope).astype(BF)
        bup_ref[0, 0:1, :] = col_sum(gu.astype(F32))
        bup_ref[0, 1:8, :] = jnp.zeros((7, D), F32)
        du_ref[0] = mm_tn(fl_s[...], gu).astype(BF)
        gf_s[...] += mm_nt(gu, up_ref[0])

    @pl.when(step == 2 * RANKS - 1)
    def _():
        vec = vector_rows(tail_ref)
        f = gf_s[...]
        normed = n1_ref[...]
        vec_ref[2:3, :] = col_sum(f * normed)
        vec_ref[3:4, :] = col_sum(f)
        grad_one = norm_backward(f * vec[2], normed, r1_ref[:, 0:1])
        grad_one_ref[...] = grad_one
        low = grad_one.astype(BF)
        ga_ref[...] = low
        vec_ref[0:1, :] = col_sum(low.astype(F32))


def feed_forward(n1, r1, out_grad, mats):
    whole = lambda *shape: pl.BlockSpec(shape, lambda s: (0,) * len(shape))
    late = lambda *shape: pl.BlockSpec(
        (1, *shape), lambda s: (jnp.maximum(s - RANKS, 0),) + (0,) * len(shape)
    )
    return pl.pallas_call(
        ffn_kernel,
        grid=(2 * RANKS,),
        in_specs=[
            whole(L, D),
            whole(L, BLK),
            whole(L, D),
            pl.BlockSpec((1, D, D), lambda s: (lax.rem(s, RANKS), 1, 0)),
            pl.BlockSpec((1, D, D), lambda s: (lax.rem(s, RANKS), 2, 0)),
            pl.BlockSpec((RANKS, TILE_ROWS, D), lambda s: (0, MAT_ROWS // TILE_ROWS, 0)),
        ],
        out_specs=[
            whole(L, D),
            late(D, D),
            late(D, D),
            whole(L, D),
            whole(L, D),
            whole(8, D),
            late(8, D),
        ],
        out_shape=[
            jax.ShapeDtypeStruct((L, D), BF),
            jax.ShapeDtypeStruct((RANKS, D, D), BF),
            jax.ShapeDtypeStruct((RANKS, D, D), BF),
            jax.ShapeDtypeStruct((L, D), F32),
            jax.ShapeDtypeStruct((L, D), BF),
            jax.ShapeDtypeStruct((8, D), F32),
            jax.ShapeDtypeStruct((RANKS, 8, D), F32),
        ],
        scratch_shapes=[
            pltpu.VMEM((L, D), F32),
            pltpu.VMEM((L, D), BF),
            pltpu.VMEM((RANKS, L, D), F32),
            pltpu.VMEM((RANKS, L, D), BF),
            pltpu.VMEM((L, D), F32),
            pltpu.VMEM((L, D), BF),
            pltpu.VMEM((L, D), F32),
        ],
        compiler_params=pltpu.CompilerParams(vmem_limit_bytes=VMEM_LIMIT),
        name="feed_forward",
    )(n1, r1, out_grad, mats, mats, mats)


def att_bwd_kernel(
    ga_ref, wo_ref, qkv_ref, probs_ref, mixed_ref, wq_ref, xp_ref, grad_one_ref,
    da_ref, in_grad_ref, table_ref, qv_ref,
    ds_s, near_s, dx_s,
):
    r = pl.program_id(0)
    ga = ga_ref[...]
    da_ref[0, QKV_ROWS:D, :] = mm_tn(mixed_ref[0], ga).astype(BF)
    dm_all = mm_nt(ga, wo_ref[0]).astype(BF)
    qkv = qkv_ref[0]
    dq, dk, dv = [], [], []
    for h in range(HPR):
        q = qkv[:, HD * h : HD * (h + 1)]
        k = qkv[:, PART + HD * h : PART + HD * (h + 1)]
        v = qkv[:, 2 * PART + HD * h : 2 * PART + HD * (h + 1)]
        dm = dm_all[:, HD * h : HD * (h + 1)]
        far_left = jnp.zeros((BLK, BLK), F32)
        far_right = jnp.zeros((BLK, BLK), F32)
        for i in range(NBLK):
            rows = slice(BLK * i, BLK * (i + 1))
            p = probs_ref[0, h, rows, :].astype(F32)
            dp = mm_nt(dm[rows], v)
            ds = (p * (dp - jnp.sum(p * dp, axis=-1, keepdims=True))).astype(BF)
            ds_s[rows, :] = ds
            ds = ds.astype(F32)
            for jb in range(NBLK):
                piece = ds[:, BLK * jb : BLK * (jb + 1)]
                delta = jb - i
                if abs(delta) <= 1:
                    cols = slice(BLK * (delta + 1), BLK * (delta + 2))
                    if i == max(0, -delta):
                        near_s[:, cols] = piece
                    else:
                        near_s[:, cols] += piece
                elif delta > 0:
                    far_right += piece
                else:
                    far_left += piece
        near_s[:, 3 * BLK :] = jnp.zeros((BLK, BLK), F32)
        table_ref[0, h : h + 1, 0 : 4 * BLK] = diagonal_sums(near_s[...])
        table_ref[0, h : h + 1, 4 * BLK : 5 * BLK] = col_sum(far_left)
        table_ref[0, h : h + 1, 5 * BLK : 6 * BLK] = col_sum(far_right)
        dscore = ds_s[...]
        dq.append(mm(dscore, k) * 0.125)
        dk.append(mm_tn(dscore, q) * 0.125)
        dv.append(mm_tn(probs_ref[0, h], dm))
    table_ref[0, HPR:8, :] = jnp.zeros((8 - HPR, 6 * BLK), F32)
    dqkv = jnp.concatenate(dq + dk + dv, axis=1).astype(BF)
    qv_ref[0, 0:1, :] = col_sum(dqkv.astype(F32))
    qv_ref[0, 1:8, :] = jnp.zeros((7, QKV_ROWS), F32)
    dw = mm_tn(xp_ref[...], dqkv).astype(BF)
    for src_row, src_col, dst_row, dst_col in qkv_pieces():
        da_ref[0, src_row : src_row + 96, src_col : src_col + PART] = dw[
            dst_row : dst_row + 96, dst_col : dst_col + PART
        ]
    dx = mm_nt(dqkv, wq_ref[0])

    @pl.when(r == 0)
    def _():
        dx_s[...] = dx

    @pl.when(r > 0)
    def _():
        dx_s[...] += dx

    @pl.when(r == RANKS - 1)
    def _():
        in_grad_ref[...] = grad_one_ref[...] + mm_nt(dx_s[...].astype(BF), column_order())


def diagonal_sums(block):
    half = block.shape[0] // 2
    while half >= 8:
        block = block[:half] + pltpu.roll(block[half:], 4 * BLK - half, 1)
        half //= 2
    row = lax.broadcasted_iota(jnp.int32, (8, 1), 0)
    for bit in (4, 2, 1):
        block = jnp.where((row & bit) > 0, pltpu.roll(block, 4 * BLK - bit, 1), block)
    return col_sum(block)


def attention_backward(ga, mats, qkv, probs, mixed, wq, xp, grad_one):
    whole = lambda *shape: pl.BlockSpec(shape, lambda r: (0,) * len(shape))
    per = lambda *shape: pl.BlockSpec((1, *shape), lambda r: (r,) + (0,) * len(shape))
    return pl.pallas_call(
        att_bwd_kernel,
        grid=(RANKS,),
        in_specs=[
            whole(L, D),
            pl.BlockSpec((1, PART, D), lambda r: (r, 3, 0)),
            per(L, QKV_ROWS),
            per(HPR, L, L),
            per(L, PART),
            per(D, QKV_ROWS),
            whole(L, D),
            whole(L, D),
        ],
        out_specs=[per(D, D), whole(L, D), per(8, 6 * BLK), per(8, QKV_ROWS)],
        out_shape=[
            jax.ShapeDtypeStruct((RANKS, D, D), BF),
            jax.ShapeDtypeStruct((L, D), F32),
            jax.ShapeDtypeStruct((RANKS, 8, 6 * BLK), F32),
            jax.ShapeDtypeStruct((RANKS, 8, QKV_ROWS), F32),
        ],
        scratch_shapes=[
            pltpu.VMEM((L, L), BF),
            pltpu.VMEM((BLK, 4 * BLK), F32),
            pltpu.VMEM((L, D), F32),
        ],
        compiler_params=pltpu.CompilerParams(vmem_limit_bytes=VMEM_LIMIT),
        name="attention_backward",
    )(ga, mats, qkv, probs, mixed, wq, xp, grad_one)


def aligned_plan(shard, wide, ranks):
    unit = TILE_ROWS * D
    tiles, spare = divmod(shard, unit)
    rows = tiles * TILE_ROWS
    fits = (
        ranks == RANKS
        and spare * wide <= unit
        and rows * wide == MAT_ROWS
        and rows == QKV_ROWS // 2
    )
    return rows, spare, fits


def split_thirds(rows_96x3):
    shape = rows_96x3.shape
    return jnp.swapaxes(rows_96x3.reshape(*shape[:-2], 96, 3, D), -3, -2).reshape(shape)


def join_thirds(rows_3x96):
    shape = rows_3x96.shape
    return jnp.swapaxes(rows_3x96.reshape(*shape[:-2], 3, 96, D), -3, -2).reshape(shape)


def gather_weights(params, wide, ranks):
    shard = params.shape[1]
    rows, spare, fits = aligned_plan(shard, wide, ranks)
    if fits:
        at = lax.axis_index("wide")
        flat = jnp.zeros(((rows + TILE_ROWS) * D,), F32)
        flat = lax.dynamic_update_slice(flat, params[0], (at * spare,))
        block = flat.reshape(rows + TILE_ROWS, D)
        head = jnp.where(at < 2, split_thirds(block[:rows]), block[:rows])
        block = jnp.concatenate([head, block[rows:]], axis=0).astype(BF)
        gathered = lax.all_gather(block, ("narrow", "wide"), axis=0, tiled=True)
        return merge_blocks(gathered.reshape(ranks, wide, rows + TILE_ROWS, D))
    flat = lax.all_gather(params.astype(BF)[0], "wide", axis=0, tiled=True)
    flat = jnp.pad(flat, (0, PAD_ROWS * D - flat.shape[0])).reshape(PAD_ROWS, D)
    head = split_thirds(flat[:QKV_ROWS].reshape(2, QKV_ROWS // 2, D)).reshape(QKV_ROWS, D)
    flat = jnp.concatenate([head, flat[QKV_ROWS:]], axis=0)
    return lax.all_gather(flat, "narrow", axis=0, tiled=True).reshape(ranks, PAD_ROWS, D)


def scatter_grads(grads, shard, wide, ranks):
    rows, spare, fits = aligned_plan(shard, wide, ranks)
    if fits:
        windows = jnp.stack(
            [grads[:, rows * w : rows * (w + 1) + TILE_ROWS] for w in range(wide)], axis=1
        )
        mine = lax.psum_scatter(
            windows.reshape(-1, D), ("narrow", "wide"), scatter_dimension=0, tiled=True
        ).astype(F32)
        at = lax.axis_index("wide")
        head = jnp.where(at < 2, join_thirds(mine[:rows]), mine[:rows])
        flat = jnp.concatenate([head, mine[rows:]], axis=0).reshape(-1)
        return lax.dynamic_slice(flat, (at * spare,), (shard,)).reshape(1, shard)
    mine = lax.psum_scatter(grads.reshape(-1, D), "narrow", scatter_dimension=0, tiled=True)
    head = join_thirds(mine[:QKV_ROWS].reshape(2, QKV_ROWS // 2, D)).reshape(QKV_ROWS, D)
    flat = jnp.concatenate([head, mine[QKV_ROWS:]], axis=0).reshape(-1)[: shard * wide]
    return lax.psum_scatter(flat.astype(F32), "wide", scatter_dimension=0, tiled=True).reshape(1, shard)


def body(hidden_in, out_grad, pair_lengths, params, momentum, average):
    wide, ranks = lax.axis_size("wide"), lax.axis_size("narrow")
    shard = params.shape[1]
    mats = gather_weights(params, wide, ranks)
    qkv, wq, xp, mixed, probs, n1, r1 = attention_forward(pair_lengths[0], hidden_in, mats)
    block_out, d_up, d_down, grad_one, ga, vec_g, up_g = feed_forward(n1, r1, out_grad, mats)
    d_att, in_grad, table_g, qv_g = attention_backward(
        ga, mats, qkv, probs, mixed, wq, xp, grad_one
    )
    near = table_g[:, :HPR, : 4 * BLK]
    left = near[:, :, 0] + jnp.sum(near[:, :, 3 * BLK :], axis=-1) + jnp.sum(
        table_g[:, :HPR, 4 * BLK : 5 * BLK], axis=-1
    )
    right = jnp.sum(near[:, :, 255 : 3 * BLK], axis=-1) + jnp.sum(
        table_g[:, :HPR, 5 * BLK :], axis=-1
    )
    table = jnp.concatenate([left[:, :, None], near[:, :, 1:255], right[:, :, None]], axis=2)
    tail = jnp.concatenate(
        [
            qv_g[:, 0, :PART],
            qv_g[:, 0, 2 * PART :],
            up_g[:, 0],
            jnp.swapaxes(table, 1, 2).reshape(RANKS, -1),
            vec_g[:6].reshape(RANKS, -1),
        ],
        axis=1,
    ).reshape(RANKS, 4, D)
    tail = jnp.pad(tail, ((0, 0), (0, TILE_ROWS - 4), (0, 0))).astype(BF)
    grads = jnp.concatenate([d_att, d_up, d_down, tail], axis=1)
    grad_shard = scatter_grads(grads, shard, wide, ranks)
    device_count = wide * ranks
    step_rate = 1.0 / (32.0 * math.sqrt(hidden_in.shape[0] * device_count))
    new_momentum = 0.5 * momentum + step_rate * grad_shard
    new_params = params - (step_rate * grad_shard + 0.5 * new_momentum)
    new_average = 0.5 * average + 0.5 * new_params
    return (
        block_out,
        in_grad,
        grad_shard,
        new_params,
        new_momentum,
        new_average,
        new_params.astype(BF),
    )


def solution(mesh):
    rows = P(("wide", "narrow"), None)
    flat = P("narrow", "wide")
    return jax.shard_map(
        body,
        mesh=mesh,
        in_specs=(rows, rows, rows, flat, flat, flat),
        out_specs=(rows, rows, flat, flat, flat, flat, flat),
        check_vma=False,
    )
```

```python
import functools
import math

import jax
import jax.numpy as jnp
from jax import lax
from jax.experimental import pallas as pl
from jax.experimental.pallas import tpu as pltpu
from jax.sharding import PartitionSpec as P

D = 768
HEADS = 12
FF = 3072
HD = 64
BUCKETS = 256
L = 512
RANKS = 4
PART = D // RANKS
HPR = HEADS // RANKS
SLOTS = 2
QKV_ROWS = 3 * PART
TILE_ROWS = 16
MAT_ROWS = 3 * D
PAD_ROWS = MAT_ROWS + TILE_ROWS
ATT_ROWS = D + TILE_ROWS
FF_ROWS = 2 * D
BLK = 128
NBLK = L // BLK
NEG = -1000000000.0
VMEM_LIMIT = 60 * 1024 * 1024
BF = jnp.bfloat16
F32 = jnp.float32


def mm(a, b):
    return jnp.dot(a, b, preferred_element_type=F32)


def mm_nt(a, b):
    return lax.dot_general(a, b, (((1,), (1,)), ((), ())), preferred_element_type=F32)


def mm_tn(a, b):
    return lax.dot_general(a, b, (((0,), (0,)), ((), ())), preferred_element_type=F32)


def qkv_pieces():
    for b in range(2):
        for j in range(4):
            for c in range(3):
                t, q = divmod(3 * j + c, 4)
                yield 288 * b + 96 * t, PART * q, PART * j + 96 * b, PART * c


def column_order():
    d = lax.broadcasted_iota(jnp.int32, (D, D), 0)
    n = lax.broadcasted_iota(jnp.int32, (D, D), 1)
    j = (n >= PART).astype(jnp.int32) + (n >= 2 * PART).astype(jnp.int32) + (n >= 3 * PART).astype(jnp.int32)
    return (d == 4 * (n - PART * j) + j).astype(F32).astype(BF)


def slot_of(r, place_ref):
    return ((r // 2) ^ place_ref[1]) + 2 * ((r % 2) ^ place_ref[2])


def slice_of(slot, place_ref):
    return 2 * ((slot % 2) ^ place_ref[1]) + ((slot // 2) ^ place_ref[2])


def vector_rows(tails_ref, place_ref):
    chunks = []
    for r in range(RANKS):
        k = slot_of(r, place_ref)
        chunks.append(tails_ref[k, 2:3, 384:768])
        chunks.append(tails_ref[k, 3:4, 0:384])
        chunks.append(tails_ref[k, 3:4, 384:768])
    return [
        jnp.concatenate([chunks[2 * v], chunks[2 * v + 1]], axis=1).astype(F32) for v in range(6)
    ]


def table_order():
    src = lax.broadcasted_iota(jnp.int32, (D, D), 0)
    dst = lax.broadcasted_iota(jnp.int32, (D, D), 1)
    hh = (dst >= BUCKETS).astype(jnp.int32) + (dst >= 2 * BUCKETS).astype(jnp.int32)
    return (src == 3 * (dst - BUCKETS * hh) + hh).astype(F32).astype(BF)


def normalize(values):
    centred = values - jnp.mean(values, axis=-1, keepdims=True)
    inv = lax.rsqrt(jnp.mean(centred * centred, axis=-1, keepdims=True) + 1e-05)
    return centred * inv, inv


def norm_backward(e, normed, inv):
    return inv * (
        e - jnp.mean(e, axis=-1, keepdims=True) - normed * jnp.mean(e * normed, axis=-1, keepdims=True)
    )


def col_sum(values):
    return jnp.sum(values, axis=0, keepdims=True)


def call(kernel, name, grid, in_specs, out_specs, out_shape, scratch, args, vmem=VMEM_LIMIT, flops=0, moved=0):
    return pl.pallas_call(
        kernel,
        grid_spec=pltpu.PrefetchScalarGridSpec(
            num_scalar_prefetch=1,
            grid=grid,
            in_specs=in_specs,
            out_specs=out_specs,
            scratch_shapes=scratch,
        ),
        out_shape=out_shape,
        compiler_params=pltpu.CompilerParams(vmem_limit_bytes=vmem),
        cost_estimate=pl.CostEstimate(flops=flops, bytes_accessed=moved, transcendentals=0),
        name=name,
    )(*args)


def whole(*shape):
    return pl.BlockSpec(shape, lambda *_: (0,) * len(shape))


def shaped(dtype, *shape):
    return jax.ShapeDtypeStruct(shape, dtype)


def block_kernel(rows, lead, shift, place_ref, flat_ref, out_ref, rows_s):
    w = place_ref[0]
    count = flat_ref.shape[1] // 128
    rows_s[0:lead, :] = jnp.zeros((lead, 128), F32)
    rows_s[lead : lead + count, :] = flat_ref[...].reshape(count, 128)
    rows_s[lead + count :, :] = jnp.zeros((rows_s.shape[0] - lead - count, 128), F32)
    start = lead - shift * w
    third = rows // 3

    @pl.when(w < 2)
    def _():
        for t in range(3):
            for c in range(6):
                out_ref[third * t : third * (t + 1), 128 * c : 128 * (c + 1)] = rows_s[
                    pl.ds(start + 6 * t + c, third, stride=18), :
                ].astype(BF)

    @pl.when(w >= 2)
    def _():
        for c in range(6):
            out_ref[0:rows, 128 * c : 128 * (c + 1)] = rows_s[
                pl.ds(start + c, rows, stride=6), :
            ].astype(BF)

    for c in range(6):
        out_ref[rows : rows + TILE_ROWS, 128 * c : 128 * (c + 1)] = rows_s[
            pl.ds(start + 6 * rows + c, TILE_ROWS, stride=6), :
        ].astype(BF)


def own_block(place, params, rows, spare, wide):
    count = params.shape[1] // 128
    lead = spare // 128 * wide
    total = -(-(lead + 6 * (rows + TILE_ROWS)) // 8) * 8
    return call(
        functools.partial(block_kernel, rows, lead, spare // 128),
        "own_block", (1,),
        [whole(*params.shape)],
        whole(rows + TILE_ROWS, D),
        shaped(BF, rows + TILE_ROWS, D),
        [pltpu.VMEM((total, 128), F32)],
        (place, params),
        vmem=16 * 1024 * 1024,
    )


def update_kernel(
    rows, lead, shift, rate, place_ref, kept_ref, near_ref, second_ref, ring_ref, params_ref, momentum_ref, average_ref,
    grads_ref, new_params_ref, new_momentum_ref, new_average_ref, low_ref, rows_s,
):
    w = place_ref[0]
    count = params_ref.shape[1] // 128
    block = (
        kept_ref[...].astype(F32) + near_ref[0].astype(F32) + second_ref[...].astype(F32) + ring_ref[...].astype(F32)
    )
    start = lead - shift * w
    third = rows // 3

    @pl.when(w < 2)
    def _():
        for t in range(3):
            for c in range(6):
                rows_s[pl.ds(start + 6 * t + c, third, stride=18), :] = block[
                    third * t : third * (t + 1), 128 * c : 128 * (c + 1)
                ]

    @pl.when(w >= 2)
    def _():
        for c in range(6):
            rows_s[pl.ds(start + c, rows, stride=6), :] = block[0:rows, 128 * c : 128 * (c + 1)]

    for c in range(6):
        rows_s[pl.ds(start + 6 * rows + c, TILE_ROWS, stride=6), :] = block[
            rows : rows + TILE_ROWS, 128 * c : 128 * (c + 1)
        ]
    grads = rows_s[lead : lead + count, :].reshape(params_ref.shape)
    grads_ref[...] = grads
    params = params_ref[...]
    new_momentum = 0.5 * momentum_ref[...] + rate * grads
    new_params = params - (rate * grads + 0.5 * new_momentum)
    new_momentum_ref[...] = new_momentum
    new_params_ref[...] = new_params
    new_average_ref[...] = 0.5 * average_ref[...] + 0.5 * new_params
    low_ref[...] = new_params.astype(BF)


def update_shard(place, parts, params, momentum, average, rate, rows, spare, wide):
    count = params.shape[1] // 128
    lead = spare // 128 * wide
    total = -(-(lead + 6 * (rows + TILE_ROWS)) // 8) * 8
    kept, near, second, ring = parts
    cap = rows + TILE_ROWS
    flat = whole(*params.shape)
    return call(
        functools.partial(update_kernel, rows, lead, spare // 128, rate),
        "update_shard", (1,),
        [whole(cap, D), pl.BlockSpec((1, cap, D), lambda *_: (1, 0, 0)), whole(cap, D), whole(cap, D), flat, flat, flat],
        [flat] * 5,
        [shaped(F32, *params.shape)] * 4 + [shaped(BF, *params.shape)],
        [pltpu.VMEM((total, 128), F32)],
        (place, kept, near, second, ring, params, momentum, average),
        vmem=32 * 1024 * 1024,
    )


def merge_kernel(rows, at_ref, *refs):
    pieces, (att_ref, ff_ref), (mats, edges, in_sem, out_sem) = refs[:16], refs[16:18], refs[18:]
    copies = {}
    for slot in range(SLOTS):
        for i in range(8):
            w = at_ref[i]
            piece = pieces[8 * slot + i]
            main = pltpu.make_async_copy(
                piece.at[0:rows],
                mats.at[slot, pl.ds(pl.multiple_of(rows * w, TILE_ROWS), rows)],
                in_sem.at[slot, i, 0],
            )
            edge = pltpu.make_async_copy(
                piece.at[rows : rows + TILE_ROWS], edges.at[slot, w], in_sem.at[slot, i, 1]
            )
            main.start()
            edge.start()
            copies[slot, i] = (main, edge)
    outs = []
    for slot in range(SLOTS):
        for i in range(8):
            for c in copies[slot, i]:
                c.wait()
        for w in range(1, 8):
            at = rows * w
            mats[slot, at : at + TILE_ROWS, :] = mats[slot, at : at + TILE_ROWS, :] + edges[slot, w - 1]
        mats[slot, MAT_ROWS:PAD_ROWS, :] = edges[slot, 7]
        for n, (src, dst) in enumerate(
            (
                (mats.at[slot, 0:D], att_ref.at[slot, 0:D]),
                (mats.at[slot, MAT_ROWS:PAD_ROWS], att_ref.at[slot, D:ATT_ROWS]),
                (mats.at[slot, D:MAT_ROWS], ff_ref.at[slot]),
            )
        ):
            copy = pltpu.make_async_copy(src, dst, out_sem.at[slot, n])
            copy.start()
            outs.append(copy)
    for copy in outs:
        copy.wait()


def merge_blocks(at, pieces, rows):
    hbm = pl.BlockSpec(memory_space=pl.ANY)
    return call(
        functools.partial(merge_kernel, rows),
        "merge_weights", (1,),
        [hbm] * 16,
        [hbm] * 2,
        [shaped(BF, SLOTS, ATT_ROWS, D), shaped(BF, SLOTS, FF_ROWS, D)],
        [
            pltpu.VMEM((SLOTS, PAD_ROWS, D), BF),
            pltpu.VMEM((SLOTS, 8, TILE_ROWS, D), BF),
            pltpu.SemaphoreType.DMA((SLOTS, 8, 2)),
            pltpu.SemaphoreType.DMA((SLOTS, 3)),
        ],
        (at, *pieces),
    )


def window_kernel(rows, kinds, at_ref, own_att, own_ff, got_att, got_ff, *refs):
    outs, (own_s, got_s, own_sem, got_sem) = refs[:-4], refs[-4:]
    cap = rows + TILE_ROWS

    def fetch(w, slot, att, ff, buf, sem):
        @pl.when(w < 2)
        def _():
            src = att.at[slot, pl.ds(pl.multiple_of(rows * w, TILE_ROWS), cap)]
            pltpu.make_async_copy(src, buf, sem).start()

        @pl.when(w == 2)
        def _():
            pltpu.make_async_copy(att.at[slot, 2 * rows : D], buf.at[0 : D - 2 * rows], sem).start()
            pltpu.make_async_copy(ff.at[slot, 0 : 3 * rows + TILE_ROWS - D], buf.at[D - 2 * rows : cap], sem).start()

        @pl.when((w > 2) & (w < 7))
        def _():
            src = ff.at[slot, pl.ds(pl.multiple_of(rows * w - D, TILE_ROWS), cap)]
            pltpu.make_async_copy(src, buf, sem).start()

        @pl.when(w == 7)
        def _():
            pltpu.make_async_copy(ff.at[slot, 7 * rows - D : FF_ROWS], buf.at[0:rows], sem).start()
            pltpu.make_async_copy(att.at[slot, D:ATT_ROWS], buf.at[rows:cap], sem).start()

    windows = [(q, xo, slot) for q in range(len(kinds)) for xo in range(2) for slot in range(SLOTS)]
    for n, (q, xo, slot) in enumerate(windows):
        w = at_ref[2 * q + xo]
        fetch(w, slot, own_att, own_ff, own_s.at[n], own_sem.at[n])
        fetch(w, slot, got_att, got_ff, got_s.at[n], got_sem.at[n])
    for n, (q, xo, slot) in enumerate(windows):
        pltpu.make_async_copy(own_ff.at[0, 0:cap], own_s.at[n], own_sem.at[n]).wait()
        pltpu.make_async_copy(own_ff.at[0, 0:cap], got_s.at[n], got_sem.at[n]).wait()
        total = (own_s[n].astype(F32) + got_s[n].astype(F32)).astype(BF)
        send, pass_on, keep = outs[3 * q : 3 * q + 3]
        if xo == 0 and slot == 0:
            keep[...] = total
        elif xo == 1 and slot == 1:
            send[0] = total
        elif (slot == 1) == (kinds[q] == "y"):
            send[1] = total
        else:
            pass_on[...] = total


def split_windows(at, kinds, own, got, rows):
    hbm = pl.BlockSpec(memory_space=pl.ANY)
    cap = rows + TILE_ROWS
    n = 4 * len(kinds)
    outs = call(
        functools.partial(window_kernel, rows, kinds),
        "split_windows", (1,),
        [hbm] * 4,
        [whole(2, cap, D), whole(cap, D), whole(cap, D)] * len(kinds),
        [shaped(BF, 2, cap, D), shaped(BF, cap, D), shaped(BF, cap, D)] * len(kinds),
        [
            pltpu.VMEM((n, cap, D), BF),
            pltpu.VMEM((n, cap, D), BF),
            pltpu.SemaphoreType.DMA((n,)),
            pltpu.SemaphoreType.DMA((n,)),
        ],
        (at, *own, *got),
    )
    return [outs[3 * q : 3 * q + 3] for q in range(len(kinds))]


def segment_of(pos, len_ref):
    end0 = len_ref[0]
    end1 = end0 + len_ref[1]
    end2 = end1 + len_ref[2]
    return (
        (pos >= end0).astype(jnp.int32)
        + (pos >= end1).astype(jnp.int32)
        + (pos >= end2).astype(jnp.int32)
    )


def att_fwd_kernel(
    scal_ref, x_ref, mq0_ref, wo0_ref, mq1_ref, wo1_ref, tails_ref,
    qkv_ref, wq_ref, mixed_ref, probs_ref, xp_ref, n1_ref, r1_ref,
    table_s, acc_s, wo_s,
):
    s = pl.program_id(0)
    len_ref = scal_ref

    @pl.when(s == 0)
    def _():
        xp_ref[...] = mm(x_ref[...], column_order()).astype(BF)
        acc_s[...] = jnp.zeros_like(acc_s)
        flat = jnp.concatenate(
            [
                jnp.concatenate([tails_ref[k, 1:2, 384:768], tails_ref[k, 2:3, 0:384]], axis=1).astype(F32)
                for k in range(RANKS)
            ]
            + [jnp.zeros((8 - RANKS, D), F32)],
            axis=0,
        ).astype(BF)
        tables = mm(flat, table_order())
        for k in range(RANKS):
            for h in range(HPR):
                row = tables[k : k + 1, BUCKETS * h : BUCKETS * (h + 1)]
                table_s[k, h : h + 1, :] = jnp.concatenate(
                    [
                        row,
                        jnp.broadcast_to(row[:, 255:256], (1, BLK)),
                        jnp.broadcast_to(row[:, 0:1], (1, BLK)),
                    ],
                    axis=1,
                )

    def load(mq_ref, wo_ref):
        for src_row, src_col, dst_row, dst_col in qkv_pieces():
            wq_ref[0, dst_row : dst_row + 96, dst_col : dst_col + PART] = mq_ref[
                0, src_row : src_row + 96, src_col : src_col + PART
            ]
        wo_s[...] = wo_ref[0]

    @pl.when(s < SLOTS)
    def _():
        load(mq0_ref, wo0_ref)

    @pl.when(s >= SLOTS)
    def _():
        load(mq1_ref, wo1_ref)

    first = tails_ref[s, 0:1, :]
    bias = jnp.concatenate(
        [first[:, 0:PART], jnp.zeros((1, PART), BF), first[:, PART : 2 * PART]], axis=1
    ).astype(F32)
    qkv = (mm(xp_ref[...], wq_ref[0]) + bias).astype(BF)
    qkv_ref[0] = qkv

    seg_j = segment_of(lax.broadcasted_iota(jnp.int32, (1, L), 1), len_ref)
    table = table_s[s]
    heads = []
    for h in range(HPR):
        q = qkv[:, HD * h : HD * (h + 1)]
        k = qkv[:, PART + HD * h : PART + HD * (h + 1)]
        v = qkv[:, 2 * PART + HD * h : 2 * PART + HD * (h + 1)]
        row = table[h : h + 1, :]
        near = pltpu.roll(jnp.broadcast_to(row, (BLK, 4 * BLK)), 0, 1, stride=1, stride_axis=0)
        far_right = jnp.broadcast_to(row[:, 255:256], (BLK, BLK))
        far_left = jnp.broadcast_to(row[:, 511:512], (BLK, BLK))
        for i in range(NBLK):
            seg_i = segment_of(
                lax.broadcasted_iota(jnp.int32, (BLK, 1), 0) + BLK * i, len_ref
            )
            parts = []
            for jb in range(NBLK):
                delta = jb - i
                if abs(delta) <= 1:
                    parts.append(near[:, BLK * (delta + 1) : BLK * (delta + 2)])
                else:
                    parts.append(far_right if delta > 0 else far_left)
            logits = mm_nt(q[BLK * i : BLK * (i + 1)], k) * 0.125 + jnp.concatenate(parts, axis=1)
            logits = jnp.where(seg_i == seg_j, logits, NEG)
            top = jnp.max(logits, axis=-1, keepdims=True)
            expo = jnp.exp(logits - top)
            total = jnp.sum(expo, axis=-1, keepdims=True)
            probs_ref[0, h, BLK * i : BLK * (i + 1), :] = (expo * (1.0 / total)).astype(BF)
        heads.append(mm(probs_ref[0, h], v))
    mixed = jnp.concatenate(heads, axis=1).astype(BF)
    mixed_ref[0] = mixed
    acc_s[...] += mm(mixed, wo_s[...])

    @pl.when(s == RANKS - 1)
    def _():
        vec = vector_rows(tails_ref, PlaceView(scal_ref))
        normed, inv = normalize(x_ref[...].astype(F32) + acc_s[...] + vec[0])
        n1_ref[...] = normed
        r1_ref[...] = jnp.broadcast_to(inv, (L, BLK))


class PlaceView:
    def __init__(self, ref):
        self.ref = ref

    def __getitem__(self, i):
        return self.ref[4 + i]


def attention_forward(scalars, x, own_att, got_att, tails):
    per = lambda *shape: pl.BlockSpec((1, *shape), lambda s, n: (s,) + (0,) * len(shape))
    own = lambda rows, at: pl.BlockSpec((1, rows, D), lambda s, n: (jnp.minimum(s, 1), at, 0))
    got = lambda rows, at: pl.BlockSpec((1, rows, D), lambda s, n: (jnp.maximum(s - 2, 0), at, 0))
    return call(
        att_fwd_kernel,
        "attention_forward", (RANKS,),
        [
            whole(L, D),
            own(QKV_ROWS, 0), own(PART, QKV_ROWS // PART),
            got(QKV_ROWS, 0), got(PART, QKV_ROWS // PART),
            whole(RANKS, TILE_ROWS, D),
        ],
        [per(L, QKV_ROWS), per(D, QKV_ROWS), per(L, PART), per(HPR, L, L), whole(L, D), whole(L, D), whole(L, BLK)],
        [
            shaped(BF, RANKS, L, QKV_ROWS),
            shaped(BF, RANKS, D, QKV_ROWS),
            shaped(BF, RANKS, L, PART),
            shaped(BF, RANKS, HPR, L, L),
            shaped(BF, L, D),
            shaped(F32, L, D),
            shaped(F32, L, BLK),
        ],
        [pltpu.VMEM((RANKS, 8, 512), F32), pltpu.VMEM((L, D), F32), pltpu.VMEM((PART, D), BF)],
        (scalars, x, own_att, own_att, got_att, got_att, tails),
        flops=6_000_000_000, moved=24_000_000,
    )


def ffn_kernel(
    place_ref, n1_ref, r1_ref, og_ref, up0_ref, down0_ref, up1_ref, down1_ref, tails_ref,
    block_ref, grad0_ref, grad1_ref, grad_one_ref, ga_ref, vec_ref, bup_ref,
    fn_s, fl_s, up_s, act_s, down_s, gd_s, gf_s,
):
    step = pl.program_id(0)
    inv_root2 = 1.0 / math.sqrt(2.0)

    @pl.when(step == 0)
    def _():
        vec = vector_rows(tails_ref, place_ref)
        first = n1_ref[...] * vec[2] + vec[3]
        fn_s[...] = first
        fl_s[...] = first.astype(BF)
        down_s[...] = jnp.zeros_like(down_s)

    def forward(slot, up_ref, down_ref):
        bias = jnp.concatenate([tails_ref[slot, 0:1, 384:768], tails_ref[slot, 1:2, 0:384]], axis=1)
        up = mm(fl_s[...], up_ref[0]) + bias.astype(F32)
        up_s[slot] = up
        act = (0.5 * up * (1.0 + lax.erf(up * inv_root2))).astype(BF)
        act_s[slot] = act
        down_s[...] += mm(act, down_ref[0])

    @pl.when(step < 2)
    def _():
        forward(step, up0_ref, down0_ref)

    @pl.when((step == 2) | (step == 3))
    def _():
        forward(step, up1_ref, down1_ref)

    @pl.when(step == RANKS)
    def _():
        vec = vector_rows(tails_ref, place_ref)
        normed, inv = normalize(fn_s[...] + down_s[...] + vec[1])
        block_ref[...] = (normed * vec[4] + vec[5]).astype(BF)
        og = og_ref[...].astype(F32)
        vec_ref[4:5, :] = col_sum(og * normed)
        vec_ref[5:6, :] = col_sum(og)
        grad_two = norm_backward(og * vec[4], normed, inv)
        low = grad_two.astype(BF)
        gd_s[...] = low
        vec_ref[1:2, :] = col_sum(low.astype(F32))
        vec_ref[6:8, :] = jnp.zeros((2, D), F32)
        gf_s[...] = grad_two

    def backward(slot, up_ref, down_ref, grad_ref):
        gd = gd_s[...]
        grad_ref[0, D:FF_ROWS, :] = mm_tn(act_s[slot], gd).astype(BF)
        up = up_s[slot]
        slope = 0.5 * (1.0 + lax.erf(up * inv_root2)) + up * jnp.exp(-0.5 * up * up) * (
            1.0 / math.sqrt(2.0 * math.pi)
        )
        gu = (mm_nt(gd, down_ref[0]) * slope).astype(BF)
        bup_ref[0, 0:1, :] = col_sum(gu.astype(F32))
        bup_ref[0, 1:8, :] = jnp.zeros((7, D), F32)
        grad_ref[0, 0:D, :] = mm_tn(fl_s[...], gu).astype(BF)
        gf_s[...] += mm_nt(gu, up_ref[0])

    @pl.when((step == 4) | (step == 5))
    def _():
        backward(step - 2, up1_ref, down1_ref, grad1_ref)

    @pl.when(step >= 6)
    def _():
        backward(step - 6, up0_ref, down0_ref, grad0_ref)

    @pl.when(step == 2 * RANKS - 1)
    def _():
        vec = vector_rows(tails_ref, place_ref)
        f = gf_s[...]
        normed = n1_ref[...]
        vec_ref[2:3, :] = col_sum(f * normed)
        vec_ref[3:4, :] = col_sum(f)
        grad_one = norm_backward(f * vec[2], normed, r1_ref[:, 0:1])
        grad_one_ref[...] = grad_one
        low = grad_one.astype(BF)
        ga_ref[...] = low
        vec_ref[0:1, :] = col_sum(low.astype(F32))


def feed_forward(place, n1, r1, out_grad, own_ff, got_ff, tails):
    def own_at(half):
        return lambda s, n: ((((s >= 1) & (s <= 3)) | (s == 7)).astype(jnp.int32), half, 0)

    def got_at(half):
        return lambda s, n: (((s == 3) | (s >= 5)).astype(jnp.int32), half, 0)

    wt = lambda index: pl.BlockSpec((1, D, D), index)
    return call(
        ffn_kernel,
        "feed_forward", (2 * RANKS,),
        [
            whole(L, D), whole(L, BLK), whole(L, D),
            wt(own_at(0)), wt(own_at(1)), wt(got_at(0)), wt(got_at(1)),
            whole(RANKS, TILE_ROWS, D),
        ],
        [
            whole(L, D),
            pl.BlockSpec((1, FF_ROWS, D), lambda s, n: ((s >= 7).astype(jnp.int32), 0, 0)),
            pl.BlockSpec((1, FF_ROWS, D), lambda s, n: ((s >= 5).astype(jnp.int32), 0, 0)),
            whole(L, D), whole(L, D), whole(8, D),
            pl.BlockSpec((1, 8, D), lambda s, n: (lax.rem(jnp.maximum(s, 4) - 2, 4), 0, 0)),
        ],
        [
            shaped(BF, L, D),
            shaped(BF, SLOTS, FF_ROWS, D),
            shaped(BF, SLOTS, FF_ROWS, D),
            shaped(F32, L, D),
            shaped(BF, L, D),
            shaped(F32, 8, D),
            shaped(F32, RANKS, 8, D),
        ],
        [
            pltpu.VMEM((L, D), F32),
            pltpu.VMEM((L, D), BF),
            pltpu.VMEM((RANKS, L, D), F32),
            pltpu.VMEM((RANKS, L, D), BF),
            pltpu.VMEM((L, D), F32),
            pltpu.VMEM((L, D), BF),
            pltpu.VMEM((L, D), F32),
        ],
        (place, n1, r1, out_grad, own_ff, own_ff, got_ff, got_ff, tails),
        flops=14_500_000_000, moved=36_000_000,
    )


def diagonal_sums(block):
    half = block.shape[0] // 2
    while half >= 8:
        block = block[:half] + pltpu.roll(block[half:], 4 * BLK - half, 1)
        half //= 2
    row = lax.broadcasted_iota(jnp.int32, (8, 1), 0)
    for bit in (4, 2, 1):
        block = jnp.where((row & bit) > 0, pltpu.roll(block, 4 * BLK - bit, 1), block)
    return col_sum(block)


def att_bwd_kernel(
    place_ref, ga_ref, wo0_ref, wo1_ref, qkv_ref, probs_ref, mixed_ref, wq_ref, xp_ref, vec_ref, bup_ref, grad_one_ref,
    da0_ref, da1_ref, in_grad_ref,
    ds_s, near_s, sums_s, dx_s, order_s, wo_s, da_s,
):
    s = pl.program_id(0)
    slot = lax.rem(s + SLOTS, RANKS)

    @pl.when(s == 0)
    def _():
        order_s[...] = table_order()
        dx_s[...] = jnp.zeros_like(dx_s)
        sums_s[...] = jnp.zeros_like(sums_s)
        da_s[D:ATT_ROWS, :] = jnp.zeros((TILE_ROWS, D), BF)

    @pl.when(slot < SLOTS)
    def _():
        wo_s[...] = wo0_ref[0]

    @pl.when(slot >= SLOTS)
    def _():
        wo_s[...] = wo1_ref[0]

    ga = ga_ref[...]
    da_s[QKV_ROWS:D, :] = mm_tn(mixed_ref[0], ga).astype(BF)
    dm_all = mm_nt(ga, wo_s[...]).astype(BF)
    qkv = qkv_ref[0]
    dq, dk, dv = [], [], []
    for h in range(HPR):
        q = qkv[:, HD * h : HD * (h + 1)]
        k = qkv[:, PART + HD * h : PART + HD * (h + 1)]
        v = qkv[:, 2 * PART + HD * h : 2 * PART + HD * (h + 1)]
        dm = dm_all[:, HD * h : HD * (h + 1)]
        far_left = jnp.zeros((BLK, BLK), F32)
        far_right = jnp.zeros((BLK, BLK), F32)
        for i in range(NBLK):
            rows = slice(BLK * i, BLK * (i + 1))
            p = probs_ref[0, h, rows, :].astype(F32)
            dp = mm_nt(dm[rows], v)
            ds = (p * (dp - jnp.sum(p * dp, axis=-1, keepdims=True))).astype(BF)
            ds_s[rows, :] = ds
            ds = ds.astype(F32)
            for jb in range(NBLK):
                piece = ds[:, BLK * jb : BLK * (jb + 1)]
                delta = jb - i
                if abs(delta) <= 1:
                    cols = slice(BLK * (delta + 1), BLK * (delta + 2))
                    if i == max(0, -delta):
                        near_s[:, cols] = piece
                    else:
                        near_s[:, cols] += piece
                elif delta > 0:
                    far_right += piece
                else:
                    far_left += piece
        near_s[:, 3 * BLK :] = jnp.zeros((BLK, BLK), F32)
        sums_s[h : h + 1, 0 : 4 * BLK] = diagonal_sums(near_s[...])
        sums_s[h : h + 1, 4 * BLK : 5 * BLK] = col_sum(far_left)
        sums_s[h : h + 1, 5 * BLK : 6 * BLK] = col_sum(far_right)
        dscore = ds_s[...]
        dq.append(mm(dscore, k) * 0.125)
        dk.append(mm_tn(dscore, q) * 0.125)
        dv.append(mm_tn(probs_ref[0, h], dm))
    dqkv = jnp.concatenate(dq + dk + dv, axis=1).astype(BF)

    qv = col_sum(dqkv.astype(F32))
    sums = sums_s[...]
    lane = lax.broadcasted_iota(jnp.int32, (1, 6 * BLK), 1)
    is_left = (lane == 0) | ((lane >= 3 * BLK) & (lane < 5 * BLK))
    is_right = ((lane >= BUCKETS - 1) & (lane < 3 * BLK)) | (lane >= 5 * BLK)
    left = jnp.sum(jnp.where(is_left, sums, 0.0), axis=-1, keepdims=True)
    right = jnp.sum(jnp.where(is_right, sums, 0.0), axis=-1, keepdims=True)
    sums = jnp.where(lane == 0, left, jnp.where(lane == BUCKETS - 1, right, sums))
    table = jnp.concatenate([sums[h : h + 1, :BUCKETS] for h in range(HPR)], axis=1)
    table = jnp.broadcast_to(table, (8, D)).astype(BF)
    table = mm_nt(table, order_s[...])[0:1]
    r = slice_of(slot, place_ref)
    vecs = []
    for i in range(3):
        m = 3 * r + i
        row = vec_ref[pl.ds(m // 2, 1), :]
        vecs.append(jnp.where(m % 2 == 0, row[:, 0:384], row[:, 384:768]))
    bup = bup_ref[0, 0:1, :]
    tail = jnp.concatenate(
        [
            jnp.concatenate([qv[:, 0:PART], qv[:, 2 * PART :], bup[:, 0:384]], axis=1),
            jnp.concatenate([bup[:, 384:768], table[:, 0:384]], axis=1),
            jnp.concatenate([table[:, 384:768], vecs[0]], axis=1),
            jnp.concatenate([vecs[1], vecs[2]], axis=1),
            jnp.zeros((TILE_ROWS - 4, D), F32),
        ],
        axis=0,
    )
    da_s[D:ATT_ROWS, :] = tail.astype(BF)

    dw = mm_tn(xp_ref[...], dqkv).astype(BF)
    for src_row, src_col, dst_row, dst_col in qkv_pieces():
        da_s[src_row : src_row + 96, src_col : src_col + PART] = dw[
            dst_row : dst_row + 96, dst_col : dst_col + PART
        ]
    dx_s[...] += mm_nt(dqkv, wq_ref[0])

    @pl.when(slot < SLOTS)
    def _():
        da0_ref[0] = da_s[...]

    @pl.when(slot >= SLOTS)
    def _():
        da1_ref[0] = da_s[...]

    @pl.when(s == RANKS - 1)
    def _():
        in_grad_ref[...] = grad_one_ref[...] + mm_nt(dx_s[...].astype(BF), column_order())


def attention_backward(place, ga, own_att, got_att, qkv, wq, mixed, probs, xp, vec_g, up_g, grad_one):
    per = lambda *shape: pl.BlockSpec(
        (1, *shape), lambda s, n: (lax.rem(s + SLOTS, RANKS),) + (0,) * len(shape)
    )
    own = lambda s: jnp.maximum(s - 2, 0)
    got = lambda s: jnp.minimum(s, 1)
    return call(
        att_bwd_kernel,
        "attention_backward", (RANKS,),
        [
            whole(L, D),
            pl.BlockSpec((1, PART, D), lambda s, n: (own(s), QKV_ROWS // PART, 0)),
            pl.BlockSpec((1, PART, D), lambda s, n: (got(s), QKV_ROWS // PART, 0)),
            per(L, QKV_ROWS), per(HPR, L, L), per(L, PART), per(D, QKV_ROWS),
            whole(L, D), whole(8, D), per(8, D), whole(L, D),
        ],
        [
            pl.BlockSpec((1, ATT_ROWS, D), lambda s, n: (own(s), 0, 0)),
            pl.BlockSpec((1, ATT_ROWS, D), lambda s, n: (got(s), 0, 0)),
            whole(L, D),
        ],
        [shaped(BF, SLOTS, ATT_ROWS, D), shaped(BF, SLOTS, ATT_ROWS, D), shaped(F32, L, D)],
        [
            pltpu.VMEM((L, L), BF),
            pltpu.VMEM((BLK, 4 * BLK), F32),
            pltpu.VMEM((8, 6 * BLK), F32),
            pltpu.VMEM((L, D), F32),
            pltpu.VMEM((D, D), BF),
            pltpu.VMEM((PART, D), BF),
            pltpu.VMEM((ATT_ROWS, D), BF),
        ],
        (place, ga, own_att, got_att, qkv, probs, mixed, wq, xp, vec_g, up_g, grad_one),
        flops=12_000_000_000, moved=30_000_000,
    )


X_SWAP = [(w, w ^ 1) for w in range(8)]
Z_RING = [(w, (w + 2) % 8) for w in range(8)]
Y_SWAP = [(n, n ^ 2) for n in range(4)]
CORE_SWAP = [(n, n ^ 1) for n in range(4)]


def swap_x(a):
    return lax.ppermute(a, "wide", X_SWAP)


def swap_y(a):
    return lax.ppermute(a, "narrow", Y_SWAP)


def ring_z(a):
    return lax.ppermute(a, "wide", Z_RING)


def swap_core(a):
    return lax.ppermute(a, "narrow", CORE_SWAP)


together = lax.optimization_barrier


def aligned_plan(shard, wide, ranks):
    unit = TILE_ROWS * D
    tiles, spare = divmod(shard, unit)
    rows = tiles * TILE_ROWS
    fits = (
        wide == 8
        and ranks == RANKS
        and spare * wide <= unit
        and spare % 128 == 0
        and rows * wide == MAT_ROWS
        and rows == QKV_ROWS // 2
    )
    return rows, spare, fits


def gather_blocks(block, z, x, rows):
    ring, by_x, by_y, corner = [block], [], [], [None] * 4
    r1, x0, y0 = together((ring_z(block), swap_x(block), swap_y(block)))
    r2, x1, y1 = together((ring_z(r1), swap_x(r1), swap_y(r1)))
    r3, x2, y2, d0, d1 = together((ring_z(r2), swap_x(r2), swap_y(r2), swap_y(x0), swap_x(y1)))
    x3, y3, d2 = swap_x(r3), swap_y(r3), swap_y(x2)
    d3 = swap_x(y3)
    planes = jnp.mod(z - jnp.arange(4, dtype=jnp.int32), 4)
    at = jnp.concatenate([2 * planes + x, 2 * planes + 1 - x])
    pieces = [block, r1, r2, r3, x0, x1, x2, x3, y0, y1, y2, y3, d0, d1, d2, d3]
    return merge_blocks(at, pieces, rows)


def add_low(*terms):
    total = terms[0].astype(F32)
    for term in terms[1:]:
        total = total + term.astype(F32)
    return total.astype(BF)


def reduce_windows(own, got, z, x, rows):
    kinds = ("y", "x", "y", "x")
    planes = jnp.mod(z - jnp.array([1, 2, 3, 0], jnp.int32), 4)
    at = jnp.stack([2 * planes + x, 2 * planes + 1 - x], axis=1).reshape(-1)
    parts = split_windows(at[:4], kinds[:2], own, got, rows) + split_windows(
        at[4:], kinds[2:], own, got, rows
    )
    first, second = [], []
    for kind, (send, pass_on, keep) in zip(kinds, parts):
        one, two = (swap_y, swap_x) if kind == "y" else (swap_x, swap_y)
        first.append(one(send))
        second.append(two(add_low(pass_on, first[-1][0])))
    ring = None
    for q in range(3):
        terms = [parts[q][2], first[q][1], second[q]] + ([] if ring is None else [ring])
        ring = ring_z(add_low(*terms))
    return parts[3][2], first[3], second[3], ring


def gather_plain(params):
    flat = lax.all_gather(params.astype(BF)[0], "wide", axis=0, tiled=True)
    flat = jnp.pad(flat, (0, PAD_ROWS * D - flat.shape[0])).reshape(PAD_ROWS, D)
    head = jnp.swapaxes(flat[:QKV_ROWS].reshape(2, 96, 3, D), 1, 2).reshape(QKV_ROWS, D)
    flat = jnp.concatenate([head, flat[QKV_ROWS:]], axis=0)
    mats = lax.all_gather(flat, "narrow", axis=0, tiled=True).reshape(2, 2, PAD_ROWS, D)
    pairs = []
    for core in range(2):
        pair = mats[:, core]
        pairs.append((jnp.concatenate([pair[:, :D], pair[:, MAT_ROWS:]], axis=1), pair[:, D:MAT_ROWS]))
    return pairs


def scatter_plain(pairs, shard, wide):
    mats = [jnp.concatenate([att[:, :D], ff, att[:, D:]], axis=1) for att, ff in pairs]
    grads = jnp.stack(mats, axis=1).reshape(-1, D)
    mine = lax.psum_scatter(grads, "narrow", scatter_dimension=0, tiled=True)
    head = jnp.swapaxes(mine[:QKV_ROWS].reshape(2, 3, 96, D), 1, 2).reshape(QKV_ROWS, D)
    flat = jnp.concatenate([head, mine[QKV_ROWS:]], axis=0).reshape(-1)[: shard * wide]
    return lax.psum_scatter(flat.astype(F32), "wide", scatter_dimension=0, tiled=True).reshape(1, shard)


def body(hidden_in, out_grad, pair_lengths, params, momentum, average):
    wide, ranks = lax.axis_size("wide"), lax.axis_size("narrow")
    shard = params.shape[1]
    rows, spare, fits = aligned_plan(shard, wide, ranks)
    at_wide, at_narrow = lax.axis_index("wide"), lax.axis_index("narrow")
    if fits:
        place = jnp.stack([at_wide, at_narrow // 2, at_narrow % 2]).astype(jnp.int32)
        block = own_block(place, params, rows, spare, wide)
        own_att, own_ff = gather_blocks(block, at_wide // 2, at_wide % 2, rows)
        got_att, got_ff = swap_core(own_att), swap_core(own_ff)
    else:
        place = jnp.zeros((3,), jnp.int32)
        (own_att, own_ff), (got_att, got_ff) = gather_plain(params)
    scalars = jnp.concatenate([pair_lengths[0], place])
    tails = jnp.concatenate([own_att[:, D:], got_att[:, D:]], axis=0)

    qkv, wq, mixed, probs, xp, n1, r1 = attention_forward(scalars, hidden_in, own_att, got_att, tails)
    block_out, own_ffg, got_ffg, grad_one, ga, vec_g, up_g = feed_forward(
        place, n1, r1, out_grad, own_ff, got_ff, tails
    )
    own_attg, got_attg, in_grad = attention_backward(
        place, ga, own_att, got_att, qkv, wq, mixed, probs, xp, vec_g, up_g, grad_one
    )

    device_count = wide * ranks
    rate = 1.0 / (32.0 * math.sqrt(hidden_in.shape[0] * device_count))
    if fits:
        got = swap_core(got_attg), swap_core(got_ffg)
        parts = reduce_windows((own_attg, own_ffg), got, at_wide // 2, at_wide % 2, rows)
        grads, new_params, new_momentum, new_average, low = update_shard(
            place, parts, params, momentum, average, rate, rows, spare, wide
        )
    else:
        grads = scatter_plain(((own_attg, own_ffg), (got_attg, got_ffg)), shard, wide)
        new_momentum = 0.5 * momentum + rate * grads
        new_params = params - (rate * grads + 0.5 * new_momentum)
        new_average = 0.5 * average + 0.5 * new_params
        low = new_params.astype(BF)
    return (
        block_out,
        in_grad,
        grads,
        new_params,
        new_momentum,
        new_average,
        low,
    )


def solution(mesh):
    rows = P(("wide", "narrow"), None)
    flat = P("narrow", "wide")
    return jax.shard_map(
        body,
        mesh=mesh,
        in_specs=(rows, rows, rows, flat, flat, flat),
        out_specs=(rows, rows, flat, flat, flat, flat, flat),
        check_vma=False,
    )
```

```python
import functools
import math

import jax
import jax.numpy as jnp
from jax import lax
from jax.experimental import pallas as pl
from jax.experimental.pallas import tpu as pltpu
from jax.sharding import PartitionSpec as P

D = 768
HEADS = 12
FF = 3072
HD = 64
BUCKETS = 256
L = 512
RANKS = 4
PART = D // RANKS
HPR = HEADS // RANKS
SLOTS = 2
QKV_ROWS = 3 * PART
TILE_ROWS = 16
MAT_ROWS = 3 * D
PAD_ROWS = MAT_ROWS + TILE_ROWS
ATT_ROWS = D + TILE_ROWS
FF_ROWS = 2 * D
BLK = 128
NBLK = L // BLK
NEG = -1000000000.0
VMEM_LIMIT = 60 * 1024 * 1024
BF = jnp.bfloat16
F32 = jnp.float32


def mm(a, b):
    return jnp.dot(a, b, preferred_element_type=F32)


def mm_nt(a, b):
    return lax.dot_general(a, b, (((1,), (1,)), ((), ())), preferred_element_type=F32)


def mm_tn(a, b):
    return lax.dot_general(a, b, (((0,), (0,)), ((), ())), preferred_element_type=F32)


def qkv_pieces():
    for b in range(2):
        for j in range(4):
            for c in range(3):
                t, q = divmod(3 * j + c, 4)
                yield 288 * b + 96 * t, PART * q, PART * j + 96 * b, PART * c


def column_order():
    d = lax.broadcasted_iota(jnp.int32, (D, D), 0)
    n = lax.broadcasted_iota(jnp.int32, (D, D), 1)
    j = (n >= PART).astype(jnp.int32) + (n >= 2 * PART).astype(jnp.int32) + (n >= 3 * PART).astype(jnp.int32)
    return (d == 4 * (n - PART * j) + j).astype(F32).astype(BF)


def slot_of(r, place_ref):
    return ((r // 2) ^ place_ref[1]) + 2 * ((r % 2) ^ place_ref[2])


def slice_of(slot, place_ref):
    return 2 * ((slot % 2) ^ place_ref[1]) + ((slot // 2) ^ place_ref[2])


def vector_rows(tails_ref, place_ref):
    chunks = []
    for r in range(RANKS):
        k = slot_of(r, place_ref)
        chunks.append(tails_ref[k, 2:3, 384:768])
        chunks.append(tails_ref[k, 3:4, 0:384])
        chunks.append(tails_ref[k, 3:4, 384:768])
    return [
        jnp.concatenate([chunks[2 * v], chunks[2 * v + 1]], axis=1).astype(F32) for v in range(6)
    ]


def table_order():
    src = lax.broadcasted_iota(jnp.int32, (D, D), 0)
    dst = lax.broadcasted_iota(jnp.int32, (D, D), 1)
    hh = (dst >= BUCKETS).astype(jnp.int32) + (dst >= 2 * BUCKETS).astype(jnp.int32)
    return (src == 3 * (dst - BUCKETS * hh) + hh).astype(F32).astype(BF)


def normalize(values):
    centred = values - jnp.mean(values, axis=-1, keepdims=True)
    inv = lax.rsqrt(jnp.mean(centred * centred, axis=-1, keepdims=True) + 1e-05)
    return centred * inv, inv


def norm_backward(e, normed, inv):
    return inv * (
        e - jnp.mean(e, axis=-1, keepdims=True) - normed * jnp.mean(e * normed, axis=-1, keepdims=True)
    )


def col_sum(values):
    return jnp.sum(values, axis=0, keepdims=True)


def call(kernel, name, grid, in_specs, out_specs, out_shape, scratch, args, vmem=VMEM_LIMIT, flops=0, moved=0):
    return pl.pallas_call(
        kernel,
        grid_spec=pltpu.PrefetchScalarGridSpec(
            num_scalar_prefetch=1,
            grid=grid,
            in_specs=in_specs,
            out_specs=out_specs,
            scratch_shapes=scratch,
        ),
        out_shape=out_shape,
        compiler_params=pltpu.CompilerParams(vmem_limit_bytes=vmem),
        cost_estimate=pl.CostEstimate(flops=flops, bytes_accessed=moved, transcendentals=0),
        name=name,
    )(*args)


def whole(*shape):
    return pl.BlockSpec(shape, lambda *_: (0,) * len(shape))


def shaped(dtype, *shape):
    return jax.ShapeDtypeStruct(shape, dtype)


def block_kernel(rows, lead, shift, place_ref, flat_ref, out_ref, rows_s):
    w = place_ref[0]
    count = flat_ref.shape[1] // 128
    rows_s[0:lead, :] = jnp.zeros((lead, 128), F32)
    rows_s[lead : lead + count, :] = flat_ref[...].reshape(count, 128)
    rows_s[lead + count :, :] = jnp.zeros((rows_s.shape[0] - lead - count, 128), F32)
    start = lead - shift * w
    third = rows // 3

    @pl.when(w < 2)
    def _():
        for t in range(3):
            for c in range(6):
                out_ref[third * t : third * (t + 1), 128 * c : 128 * (c + 1)] = rows_s[
                    pl.ds(start + 6 * t + c, third, stride=18), :
                ].astype(BF)

    @pl.when(w >= 2)
    def _():
        for c in range(6):
            out_ref[0:rows, 128 * c : 128 * (c + 1)] = rows_s[
                pl.ds(start + c, rows, stride=6), :
            ].astype(BF)

    for c in range(6):
        out_ref[rows : rows + TILE_ROWS, 128 * c : 128 * (c + 1)] = rows_s[
            pl.ds(start + 6 * rows + c, TILE_ROWS, stride=6), :
        ].astype(BF)


def own_block(place, params, rows, spare, wide):
    count = params.shape[1] // 128
    lead = spare // 128 * wide
    total = -(-(lead + 6 * (rows + TILE_ROWS)) // 8) * 8
    return call(
        functools.partial(block_kernel, rows, lead, spare // 128),
        "own_block", (1,),
        [whole(*params.shape)],
        whole(rows + TILE_ROWS, D),
        shaped(BF, rows + TILE_ROWS, D),
        [pltpu.VMEM((total, 128), F32)],
        (place, params),
        vmem=16 * 1024 * 1024,
    )


def update_kernel(
    rows, lead, shift, rate, place_ref, kept_ref, near_ref, second_ref, ring_ref, params_ref, momentum_ref, average_ref,
    grads_ref, new_params_ref, new_momentum_ref, new_average_ref, low_ref, rows_s,
):
    w = place_ref[0]
    count = params_ref.shape[1] // 128
    block = (
        kept_ref[...].astype(F32) + near_ref[...].astype(F32) + second_ref[...].astype(F32) + ring_ref[...].astype(F32)
    )
    start = lead - shift * w
    third = rows // 3

    @pl.when(w < 2)
    def _():
        for t in range(3):
            for c in range(6):
                rows_s[pl.ds(start + 6 * t + c, third, stride=18), :] = block[
                    third * t : third * (t + 1), 128 * c : 128 * (c + 1)
                ]

    @pl.when(w >= 2)
    def _():
        for c in range(6):
            rows_s[pl.ds(start + c, rows, stride=6), :] = block[0:rows, 128 * c : 128 * (c + 1)]

    for c in range(6):
        rows_s[pl.ds(start + 6 * rows + c, TILE_ROWS, stride=6), :] = block[
            rows : rows + TILE_ROWS, 128 * c : 128 * (c + 1)
        ]
    grads = rows_s[lead : lead + count, :].reshape(params_ref.shape)
    grads_ref[...] = grads
    params = params_ref[...]
    new_momentum = 0.5 * momentum_ref[...] + rate * grads
    new_params = params - (rate * grads + 0.5 * new_momentum)
    new_momentum_ref[...] = new_momentum
    new_params_ref[...] = new_params
    new_average_ref[...] = 0.5 * average_ref[...] + 0.5 * new_params
    low_ref[...] = new_params.astype(BF)


def update_shard(place, parts, params, momentum, average, rate, rows, spare, wide):
    count = params.shape[1] // 128
    lead = spare // 128 * wide
    total = -(-(lead + 6 * (rows + TILE_ROWS)) // 8) * 8
    kept, near, second, ring = parts
    cap = rows + TILE_ROWS
    flat = whole(*params.shape)
    return call(
        functools.partial(update_kernel, rows, lead, spare // 128, rate),
        "update_shard", (1,),
        [whole(cap, D)] * 4 + [flat] * 3,
        [flat] * 5,
        [shaped(F32, *params.shape)] * 4 + [shaped(BF, *params.shape)],
        [pltpu.VMEM((total, 128), F32)],
        (place, kept, near, second, ring, params, momentum, average),
        vmem=32 * 1024 * 1024,
    )


def merge_kernel(rows, at_ref, *refs):
    pieces, (att_ref, ff_ref), (mats, edges, in_sem, out_sem) = refs[:16], refs[16:18], refs[18:]
    copies = {}
    for slot in range(SLOTS):
        for i in range(8):
            w = at_ref[i]
            piece = pieces[8 * slot + i]
            main = pltpu.make_async_copy(
                piece.at[0:rows],
                mats.at[slot, pl.ds(pl.multiple_of(rows * w, TILE_ROWS), rows)],
                in_sem.at[slot, i, 0],
            )
            edge = pltpu.make_async_copy(
                piece.at[rows : rows + TILE_ROWS], edges.at[slot, w], in_sem.at[slot, i, 1]
            )
            main.start()
            edge.start()
            copies[slot, i] = (main, edge)
    outs = []
    for slot in range(SLOTS):
        for i in range(8):
            for c in copies[slot, i]:
                c.wait()
        for w in range(1, 8):
            at = rows * w
            mats[slot, at : at + TILE_ROWS, :] = mats[slot, at : at + TILE_ROWS, :] + edges[slot, w - 1]
        mats[slot, MAT_ROWS:PAD_ROWS, :] = edges[slot, 7]
        for n, (src, dst) in enumerate(
            (
                (mats.at[slot, 0:D], att_ref.at[slot, 0:D]),
                (mats.at[slot, MAT_ROWS:PAD_ROWS], att_ref.at[slot, D:ATT_ROWS]),
                (mats.at[slot, D:MAT_ROWS], ff_ref.at[slot]),
            )
        ):
            copy = pltpu.make_async_copy(src, dst, out_sem.at[slot, n])
            copy.start()
            outs.append(copy)
    for copy in outs:
        copy.wait()


def merge_blocks(at, pieces, rows):
    hbm = pl.BlockSpec(memory_space=pl.ANY)
    return call(
        functools.partial(merge_kernel, rows),
        "merge_weights", (1,),
        [hbm] * 16,
        [hbm] * 2,
        [shaped(BF, SLOTS, ATT_ROWS, D), shaped(BF, SLOTS, FF_ROWS, D)],
        [
            pltpu.VMEM((SLOTS, PAD_ROWS, D), BF),
            pltpu.VMEM((SLOTS, 8, TILE_ROWS, D), BF),
            pltpu.SemaphoreType.DMA((SLOTS, 8, 2)),
            pltpu.SemaphoreType.DMA((SLOTS, 3)),
        ],
        (at, *pieces),
    )


def window_kernel(rows, windows, at_ref, own_att, own_ff, got_att, got_ff, *refs):
    outs, (own_s, got_s, own_sem, got_sem) = refs[:-4], refs[-4:]
    cap = rows + TILE_ROWS

    def fetch(w, slot, att, ff, buf, sem):
        @pl.when(w < 2)
        def _():
            src = att.at[slot, pl.ds(pl.multiple_of(rows * w, TILE_ROWS), cap)]
            pltpu.make_async_copy(src, buf, sem).start()

        @pl.when(w == 2)
        def _():
            pltpu.make_async_copy(att.at[slot, 2 * rows : D], buf.at[0 : D - 2 * rows], sem).start()
            pltpu.make_async_copy(ff.at[slot, 0 : 3 * rows + TILE_ROWS - D], buf.at[D - 2 * rows : cap], sem).start()

        @pl.when((w > 2) & (w < 7))
        def _():
            src = ff.at[slot, pl.ds(pl.multiple_of(rows * w - D, TILE_ROWS), cap)]
            pltpu.make_async_copy(src, buf, sem).start()

        @pl.when(w == 7)
        def _():
            pltpu.make_async_copy(ff.at[slot, 7 * rows - D : FF_ROWS], buf.at[0:rows], sem).start()
            pltpu.make_async_copy(att.at[slot, D:ATT_ROWS], buf.at[rows:cap], sem).start()

    for n, (slot, where) in enumerate(windows):
        w = at_ref[where]
        fetch(w, slot, own_att, own_ff, own_s.at[n], own_sem.at[n])
        fetch(w, slot, got_att, got_ff, got_s.at[n], got_sem.at[n])
    for n in range(len(windows)):
        pltpu.make_async_copy(own_ff.at[0, 0:cap], own_s.at[n], own_sem.at[n]).wait()
        pltpu.make_async_copy(own_ff.at[0, 0:cap], got_s.at[n], got_sem.at[n]).wait()
        outs[n][...] = (own_s[n].astype(F32) + got_s[n].astype(F32)).astype(BF)


def split_windows(at, names, own, got, rows):
    hbm = pl.BlockSpec(memory_space=pl.ANY)
    cap = rows + TILE_ROWS
    n = len(names)
    windows = [(int(name[0] in "YD"), int(name[1]) + 4 * int(name[0] in "XD")) for name in names]
    outs = call(
        functools.partial(window_kernel, rows, windows),
        "split_windows", (1,),
        [hbm] * 4,
        [whole(cap, D)] * n,
        [shaped(BF, cap, D)] * n,
        [
            pltpu.VMEM((n, cap, D), BF),
            pltpu.VMEM((n, cap, D), BF),
            pltpu.SemaphoreType.DMA((n,)),
            pltpu.SemaphoreType.DMA((n,)),
        ],
        (at, *own, *got),
    )
    return dict(zip(names, outs))


def segment_of(pos, len_ref):
    end0 = len_ref[0]
    end1 = end0 + len_ref[1]
    end2 = end1 + len_ref[2]
    return (
        (pos >= end0).astype(jnp.int32)
        + (pos >= end1).astype(jnp.int32)
        + (pos >= end2).astype(jnp.int32)
    )


def att_fwd_kernel(
    scal_ref, x_ref, mq0_ref, wo0_ref, mq1_ref, wo1_ref, tails_ref,
    qkv_ref, wq_ref, mixed_ref, probs_ref, xp_ref, n1_ref, r1_ref,
    table_s, acc_s, wo_s,
):
    s = pl.program_id(0)
    len_ref = scal_ref

    @pl.when(s == 0)
    def _():
        xp_ref[...] = mm(x_ref[...], column_order()).astype(BF)
        acc_s[...] = jnp.zeros_like(acc_s)
        flat = jnp.concatenate(
            [
                jnp.concatenate([tails_ref[k, 1:2, 384:768], tails_ref[k, 2:3, 0:384]], axis=1).astype(F32)
                for k in range(RANKS)
            ]
            + [jnp.zeros((8 - RANKS, D), F32)],
            axis=0,
        ).astype(BF)
        tables = mm(flat, table_order())
        for k in range(RANKS):
            for h in range(HPR):
                row = tables[k : k + 1, BUCKETS * h : BUCKETS * (h + 1)]
                table_s[k, h : h + 1, :] = jnp.concatenate(
                    [
                        row,
                        jnp.broadcast_to(row[:, 255:256], (1, BLK)),
                        jnp.broadcast_to(row[:, 0:1], (1, BLK)),
                    ],
                    axis=1,
                )

    def load(mq_ref, wo_ref):
        for src_row, src_col, dst_row, dst_col in qkv_pieces():
            wq_ref[0, dst_row : dst_row + 96, dst_col : dst_col + PART] = mq_ref[
                0, src_row : src_row + 96, src_col : src_col + PART
            ]
        wo_s[...] = wo_ref[0]

    @pl.when(s < SLOTS)
    def _():
        load(mq0_ref, wo0_ref)

    @pl.when(s >= SLOTS)
    def _():
        load(mq1_ref, wo1_ref)

    first = tails_ref[s, 0:1, :]
    bias = jnp.concatenate(
        [first[:, 0:PART], jnp.zeros((1, PART), BF), first[:, PART : 2 * PART]], axis=1
    ).astype(F32)
    qkv = (mm(xp_ref[...], wq_ref[0]) + bias).astype(BF)
    qkv_ref[0] = qkv

    seg_j = segment_of(lax.broadcasted_iota(jnp.int32, (1, L), 1), len_ref)
    table = table_s[s]
    heads = []
    for h in range(HPR):
        q = qkv[:, HD * h : HD * (h + 1)]
        k = qkv[:, PART + HD * h : PART + HD * (h + 1)]
        v = qkv[:, 2 * PART + HD * h : 2 * PART + HD * (h + 1)]
        row = table[h : h + 1, :]
        near = pltpu.roll(jnp.broadcast_to(row, (BLK, 4 * BLK)), 0, 1, stride=1, stride_axis=0)
        far_right = jnp.broadcast_to(row[:, 255:256], (BLK, BLK))
        far_left = jnp.broadcast_to(row[:, 511:512], (BLK, BLK))
        for i in range(NBLK):
            seg_i = segment_of(
                lax.broadcasted_iota(jnp.int32, (BLK, 1), 0) + BLK * i, len_ref
            )
            parts = []
            for jb in range(NBLK):
                delta = jb - i
                if abs(delta) <= 1:
                    parts.append(near[:, BLK * (delta + 1) : BLK * (delta + 2)])
                else:
                    parts.append(far_right if delta > 0 else far_left)
            logits = mm_nt(q[BLK * i : BLK * (i + 1)], k) * 0.125 + jnp.concatenate(parts, axis=1)
            logits = jnp.where(seg_i == seg_j, logits, NEG)
            top = jnp.max(logits, axis=-1, keepdims=True)
            expo = jnp.exp(logits - top)
            total = jnp.sum(expo, axis=-1, keepdims=True)
            probs_ref[0, h, BLK * i : BLK * (i + 1), :] = (expo * (1.0 / total)).astype(BF)
        heads.append(mm(probs_ref[0, h], v))
    mixed = jnp.concatenate(heads, axis=1).astype(BF)
    mixed_ref[0] = mixed
    acc_s[...] += mm(mixed, wo_s[...])

    @pl.when(s == RANKS - 1)
    def _():
        vec = vector_rows(tails_ref, PlaceView(scal_ref))
        normed, inv = normalize(x_ref[...].astype(F32) + acc_s[...] + vec[0])
        n1_ref[...] = normed
        r1_ref[...] = jnp.broadcast_to(inv, (L, BLK))


class PlaceView:
    def __init__(self, ref):
        self.ref = ref

    def __getitem__(self, i):
        return self.ref[4 + i]


def attention_forward(scalars, x, own_att, got_att, tails):
    per = lambda *shape: pl.BlockSpec((1, *shape), lambda s, n: (s,) + (0,) * len(shape))
    own = lambda rows, at: pl.BlockSpec((1, rows, D), lambda s, n: (jnp.minimum(s, 1), at, 0))
    got = lambda rows, at: pl.BlockSpec((1, rows, D), lambda s, n: (jnp.maximum(s - 2, 0), at, 0))
    return call(
        att_fwd_kernel,
        "attention_forward", (RANKS,),
        [
            whole(L, D),
            own(QKV_ROWS, 0), own(PART, QKV_ROWS // PART),
            got(QKV_ROWS, 0), got(PART, QKV_ROWS // PART),
            whole(RANKS, TILE_ROWS, D),
        ],
        [per(L, QKV_ROWS), per(D, QKV_ROWS), per(L, PART), per(HPR, L, L), whole(L, D), whole(L, D), whole(L, BLK)],
        [
            shaped(BF, RANKS, L, QKV_ROWS),
            shaped(BF, RANKS, D, QKV_ROWS),
            shaped(BF, RANKS, L, PART),
            shaped(BF, RANKS, HPR, L, L),
            shaped(BF, L, D),
            shaped(F32, L, D),
            shaped(F32, L, BLK),
        ],
        [pltpu.VMEM((RANKS, 8, 512), F32), pltpu.VMEM((L, D), F32), pltpu.VMEM((PART, D), BF)],
        (scalars, x, own_att, own_att, got_att, got_att, tails),
        flops=6_000_000_000, moved=24_000_000,
    )


def ffn_kernel(
    place_ref, n1_ref, r1_ref, og_ref, up0_ref, down0_ref, up1_ref, down1_ref, tails_ref,
    block_ref, grad0_ref, grad1_ref, grad_one_ref, ga_ref, vec_ref, bup_ref,
    fn_s, fl_s, up_s, act_s, down_s, gd_s, gf_s,
):
    step = pl.program_id(0)
    inv_root2 = 1.0 / math.sqrt(2.0)

    @pl.when(step == 0)
    def _():
        vec = vector_rows(tails_ref, place_ref)
        first = n1_ref[...] * vec[2] + vec[3]
        fn_s[...] = first
        fl_s[...] = first.astype(BF)
        down_s[...] = jnp.zeros_like(down_s)

    def forward(slot, up_ref, down_ref):
        bias = jnp.concatenate([tails_ref[slot, 0:1, 384:768], tails_ref[slot, 1:2, 0:384]], axis=1)
        up = mm(fl_s[...], up_ref[0]) + bias.astype(F32)
        up_s[slot] = up
        act = (0.5 * up * (1.0 + lax.erf(up * inv_root2))).astype(BF)
        act_s[slot] = act
        down_s[...] += mm(act, down_ref[0])

    @pl.when(step < 2)
    def _():
        forward(step, up0_ref, down0_ref)

    @pl.when((step == 2) | (step == 3))
    def _():
        forward(step, up1_ref, down1_ref)

    @pl.when(step == RANKS)
    def _():
        vec = vector_rows(tails_ref, place_ref)
        normed, inv = normalize(fn_s[...] + down_s[...] + vec[1])
        block_ref[...] = (normed * vec[4] + vec[5]).astype(BF)
        og = og_ref[...].astype(F32)
        vec_ref[4:5, :] = col_sum(og * normed)
        vec_ref[5:6, :] = col_sum(og)
        grad_two = norm_backward(og * vec[4], normed, inv)
        low = grad_two.astype(BF)
        gd_s[...] = low
        vec_ref[1:2, :] = col_sum(low.astype(F32))
        vec_ref[6:8, :] = jnp.zeros((2, D), F32)
        gf_s[...] = grad_two

    def backward(slot, up_ref, down_ref, grad_ref):
        gd = gd_s[...]
        grad_ref[0, D:FF_ROWS, :] = mm_tn(act_s[slot], gd).astype(BF)
        up = up_s[slot]
        slope = 0.5 * (1.0 + lax.erf(up * inv_root2)) + up * jnp.exp(-0.5 * up * up) * (
            1.0 / math.sqrt(2.0 * math.pi)
        )
        gu = (mm_nt(gd, down_ref[0]) * slope).astype(BF)
        bup_ref[0, 0:1, :] = col_sum(gu.astype(F32))
        bup_ref[0, 1:8, :] = jnp.zeros((7, D), F32)
        grad_ref[0, 0:D, :] = mm_tn(fl_s[...], gu).astype(BF)
        gf_s[...] += mm_nt(gu, up_ref[0])

    @pl.when((step == 4) | (step == 5))
    def _():
        backward(step - 2, up1_ref, down1_ref, grad1_ref)

    @pl.when(step >= 6)
    def _():
        backward(step - 6, up0_ref, down0_ref, grad0_ref)

    @pl.when(step == 2 * RANKS - 1)
    def _():
        vec = vector_rows(tails_ref, place_ref)
        f = gf_s[...]
        normed = n1_ref[...]
        vec_ref[2:3, :] = col_sum(f * normed)
        vec_ref[3:4, :] = col_sum(f)
        grad_one = norm_backward(f * vec[2], normed, r1_ref[:, 0:1])
        grad_one_ref[...] = grad_one
        low = grad_one.astype(BF)
        ga_ref[...] = low
        vec_ref[0:1, :] = col_sum(low.astype(F32))


def feed_forward(place, n1, r1, out_grad, own_ff, got_ff, tails):
    def own_at(half):
        return lambda s, n: ((((s >= 1) & (s <= 3)) | (s == 7)).astype(jnp.int32), half, 0)

    def got_at(half):
        return lambda s, n: (((s == 3) | (s >= 5)).astype(jnp.int32), half, 0)

    wt = lambda index: pl.BlockSpec((1, D, D), index)
    return call(
        ffn_kernel,
        "feed_forward", (2 * RANKS,),
        [
            whole(L, D), whole(L, BLK), whole(L, D),
            wt(own_at(0)), wt(own_at(1)), wt(got_at(0)), wt(got_at(1)),
            whole(RANKS, TILE_ROWS, D),
        ],
        [
            whole(L, D),
            pl.BlockSpec((1, FF_ROWS, D), lambda s, n: ((s >= 7).astype(jnp.int32), 0, 0)),
            pl.BlockSpec((1, FF_ROWS, D), lambda s, n: ((s >= 5).astype(jnp.int32), 0, 0)),
            whole(L, D), whole(L, D), whole(8, D),
            pl.BlockSpec((1, 8, D), lambda s, n: (lax.rem(jnp.maximum(s, 4) - 2, 4), 0, 0)),
        ],
        [
            shaped(BF, L, D),
            shaped(BF, SLOTS, FF_ROWS, D),
            shaped(BF, SLOTS, FF_ROWS, D),
            shaped(F32, L, D),
            shaped(BF, L, D),
            shaped(F32, 8, D),
            shaped(F32, RANKS, 8, D),
        ],
        [
            pltpu.VMEM((L, D), F32),
            pltpu.VMEM((L, D), BF),
            pltpu.VMEM((RANKS, L, D), F32),
            pltpu.VMEM((RANKS, L, D), BF),
            pltpu.VMEM((L, D), F32),
            pltpu.VMEM((L, D), BF),
            pltpu.VMEM((L, D), F32),
        ],
        (place, n1, r1, out_grad, own_ff, own_ff, got_ff, got_ff, tails),
        flops=14_500_000_000, moved=36_000_000,
    )


def diagonal_sums(block):
    half = block.shape[0] // 2
    while half >= 8:
        block = block[:half] + pltpu.roll(block[half:], 4 * BLK - half, 1)
        half //= 2
    row = lax.broadcasted_iota(jnp.int32, (8, 1), 0)
    for bit in (4, 2, 1):
        block = jnp.where((row & bit) > 0, pltpu.roll(block, 4 * BLK - bit, 1), block)
    return col_sum(block)


def att_bwd_kernel(
    place_ref, ga_ref, wo0_ref, wo1_ref, qkv_ref, probs_ref, mixed_ref, wq_ref, xp_ref, vec_ref, bup_ref, grad_one_ref,
    da0_ref, da1_ref, in_grad_ref,
    ds_s, near_s, sums_s, dx_s, order_s, wo_s, da_s,
):
    s = pl.program_id(0)
    slot = lax.rem(s + SLOTS, RANKS)

    @pl.when(s == 0)
    def _():
        order_s[...] = table_order()
        dx_s[...] = jnp.zeros_like(dx_s)
        sums_s[...] = jnp.zeros_like(sums_s)
        da_s[D:ATT_ROWS, :] = jnp.zeros((TILE_ROWS, D), BF)

    @pl.when(slot < SLOTS)
    def _():
        wo_s[...] = wo0_ref[0]

    @pl.when(slot >= SLOTS)
    def _():
        wo_s[...] = wo1_ref[0]

    ga = ga_ref[...]
    da_s[QKV_ROWS:D, :] = mm_tn(mixed_ref[0], ga).astype(BF)
    dm_all = mm_nt(ga, wo_s[...]).astype(BF)
    qkv = qkv_ref[0]
    dq, dk, dv = [], [], []
    for h in range(HPR):
        q = qkv[:, HD * h : HD * (h + 1)]
        k = qkv[:, PART + HD * h : PART + HD * (h + 1)]
        v = qkv[:, 2 * PART + HD * h : 2 * PART + HD * (h + 1)]
        dm = dm_all[:, HD * h : HD * (h + 1)]
        far_left = jnp.zeros((BLK, BLK), F32)
        far_right = jnp.zeros((BLK, BLK), F32)
        for i in range(NBLK):
            rows = slice(BLK * i, BLK * (i + 1))
            p = probs_ref[0, h, rows, :].astype(F32)
            dp = mm_nt(dm[rows], v)
            ds = (p * (dp - jnp.sum(p * dp, axis=-1, keepdims=True))).astype(BF)
            ds_s[rows, :] = ds
            ds = ds.astype(F32)
            for jb in range(NBLK):
                piece = ds[:, BLK * jb : BLK * (jb + 1)]
                delta = jb - i
                if abs(delta) <= 1:
                    cols = slice(BLK * (delta + 1), BLK * (delta + 2))
                    if i == max(0, -delta):
                        near_s[:, cols] = piece
                    else:
                        near_s[:, cols] += piece
                elif delta > 0:
                    far_right += piece
                else:
                    far_left += piece
        near_s[:, 3 * BLK :] = jnp.zeros((BLK, BLK), F32)
        sums_s[h : h + 1, 0 : 4 * BLK] = diagonal_sums(near_s[...])
        sums_s[h : h + 1, 4 * BLK : 5 * BLK] = col_sum(far_left)
        sums_s[h : h + 1, 5 * BLK : 6 * BLK] = col_sum(far_right)
        dscore = ds_s[...]
        dq.append(mm(dscore, k) * 0.125)
        dk.append(mm_tn(dscore, q) * 0.125)
        dv.append(mm_tn(probs_ref[0, h], dm))
    dqkv = jnp.concatenate(dq + dk + dv, axis=1).astype(BF)

    qv = col_sum(dqkv.astype(F32))
    sums = sums_s[...]
    lane = lax.broadcasted_iota(jnp.int32, (1, 6 * BLK), 1)
    is_left = (lane == 0) | ((lane >= 3 * BLK) & (lane < 5 * BLK))
    is_right = ((lane >= BUCKETS - 1) & (lane < 3 * BLK)) | (lane >= 5 * BLK)
    left = jnp.sum(jnp.where(is_left, sums, 0.0), axis=-1, keepdims=True)
    right = jnp.sum(jnp.where(is_right, sums, 0.0), axis=-1, keepdims=True)
    sums = jnp.where(lane == 0, left, jnp.where(lane == BUCKETS - 1, right, sums))
    table = jnp.concatenate([sums[h : h + 1, :BUCKETS] for h in range(HPR)], axis=1)
    table = jnp.broadcast_to(table, (8, D)).astype(BF)
    table = mm_nt(table, order_s[...])[0:1]
    r = slice_of(slot, place_ref)
    vecs = []
    for i in range(3):
        m = 3 * r + i
        row = vec_ref[pl.ds(m // 2, 1), :]
        vecs.append(jnp.where(m % 2 == 0, row[:, 0:384], row[:, 384:768]))
    bup = bup_ref[0, 0:1, :]
    tail = jnp.concatenate(
        [
            jnp.concatenate([qv[:, 0:PART], qv[:, 2 * PART :], bup[:, 0:384]], axis=1),
            jnp.concatenate([bup[:, 384:768], table[:, 0:384]], axis=1),
            jnp.concatenate([table[:, 384:768], vecs[0]], axis=1),
            jnp.concatenate([vecs[1], vecs[2]], axis=1),
            jnp.zeros((TILE_ROWS - 4, D), F32),
        ],
        axis=0,
    )
    da_s[D:ATT_ROWS, :] = tail.astype(BF)

    dw = mm_tn(xp_ref[...], dqkv).astype(BF)
    for src_row, src_col, dst_row, dst_col in qkv_pieces():
        da_s[src_row : src_row + 96, src_col : src_col + PART] = dw[
            dst_row : dst_row + 96, dst_col : dst_col + PART
        ]
    dx_s[...] += mm_nt(dqkv, wq_ref[0])

    @pl.when(slot < SLOTS)
    def _():
        da0_ref[0] = da_s[...]

    @pl.when(slot >= SLOTS)
    def _():
        da1_ref[0] = da_s[...]

    @pl.when(s == RANKS - 1)
    def _():
        in_grad_ref[...] = grad_one_ref[...] + mm_nt(dx_s[...].astype(BF), column_order())


def attention_backward(place, ga, own_att, got_att, qkv, wq, mixed, probs, xp, vec_g, up_g, grad_one):
    per = lambda *shape: pl.BlockSpec(
        (1, *shape), lambda s, n: (lax.rem(s + SLOTS, RANKS),) + (0,) * len(shape)
    )
    own = lambda s: jnp.maximum(s - 2, 0)
    got = lambda s: jnp.minimum(s, 1)
    return call(
        att_bwd_kernel,
        "attention_backward", (RANKS,),
        [
            whole(L, D),
            pl.BlockSpec((1, PART, D), lambda s, n: (own(s), QKV_ROWS // PART, 0)),
            pl.BlockSpec((1, PART, D), lambda s, n: (got(s), QKV_ROWS // PART, 0)),
            per(L, QKV_ROWS), per(HPR, L, L), per(L, PART), per(D, QKV_ROWS),
            whole(L, D), whole(8, D), per(8, D), whole(L, D),
        ],
        [
            pl.BlockSpec((1, ATT_ROWS, D), lambda s, n: (own(s), 0, 0)),
            pl.BlockSpec((1, ATT_ROWS, D), lambda s, n: (got(s), 0, 0)),
            whole(L, D),
        ],
        [shaped(BF, SLOTS, ATT_ROWS, D), shaped(BF, SLOTS, ATT_ROWS, D), shaped(F32, L, D)],
        [
            pltpu.VMEM((L, L), BF),
            pltpu.VMEM((BLK, 4 * BLK), F32),
            pltpu.VMEM((8, 6 * BLK), F32),
            pltpu.VMEM((L, D), F32),
            pltpu.VMEM((D, D), BF),
            pltpu.VMEM((PART, D), BF),
            pltpu.VMEM((ATT_ROWS, D), BF),
        ],
        (place, ga, own_att, got_att, qkv, probs, mixed, wq, xp, vec_g, up_g, grad_one),
        flops=12_000_000_000, moved=30_000_000,
    )


X_SWAP = [(w, w ^ 1) for w in range(8)]
Z_RING = [(w, (w + 2) % 8) for w in range(8)]
Y_SWAP = [(n, n ^ 2) for n in range(4)]
CORE_SWAP = [(n, n ^ 1) for n in range(4)]


def swap_x(a):
    return lax.ppermute(a, "wide", X_SWAP)


def swap_y(a):
    return lax.ppermute(a, "narrow", Y_SWAP)


def ring_z(a):
    return lax.ppermute(a, "wide", Z_RING)


def ring_back(a):
    return lax.ppermute(a, "wide", [(j, i) for i, j in Z_RING])


def swap_core(a):
    return lax.ppermute(a, "narrow", CORE_SWAP)


def after(value, earlier):
    return lax.optimization_barrier((value, earlier))[0]


def aligned_plan(shard, wide, ranks):
    unit = TILE_ROWS * D
    tiles, spare = divmod(shard, unit)
    rows = tiles * TILE_ROWS
    fits = (
        wide == 8
        and ranks == RANKS
        and spare * wide <= unit
        and spare % 128 == 0
        and rows * wide == MAT_ROWS
        and rows == QKV_ROWS // 2
    )
    return rows, spare, fits


def window_places(z, x):
    planes = jnp.mod(z - jnp.arange(4, dtype=jnp.int32), 4)
    return jnp.concatenate([2 * planes + x, 2 * planes + 1 - x])


def gather_blocks(r0, z, x, rows):
    r1, x0, y0 = ring_z(r0), swap_x(r0), swap_y(r0)
    r2, x1, d0 = ring_z(r1), swap_x(after(r1, x0)), swap_y(after(x0, y0))
    r3, x2, y1 = ring_z(r2), swap_x(after(r2, x1)), swap_y(after(r1, d0))
    d1, x3, y2 = ring_z(after(d0, r3)), swap_x(after(r3, x2)), swap_y(after(r2, y1))
    y3, d2, d3 = ring_z(after(y2, d1)), swap_x(after(y2, x3)), swap_y(after(x3, y2))
    pieces = [r0, r1, r2, r3, x0, x1, x2, x3, y0, y1, y2, y3, d0, d1, d2, d3]
    return merge_blocks(window_places(z, x), pieces, rows)


def add_low(*terms):
    total = terms[0].astype(F32)
    for term in terms[1:]:
        total = total + term.astype(F32)
    return total.astype(BF)


def reduce_windows(own, got, z, x, rows):
    at = window_places(z, x)
    a = split_windows(at, ("Y3", "D2", "D3", "Y2", "X3", "D1"), own, got, rows)
    a |= split_windows(
        at, ("X2", "Y1", "R3", "R2", "D0", "X1", "R1", "X0", "Y0", "R0"), own, got, rows
    )
    z1, x1, y1 = ring_back(a["Y3"]), swap_x(a["D2"]), swap_y(a["D3"])
    z2 = ring_back(after(a["D1"], z1))
    x2 = swap_x(add_low(a["X3"], y1))
    y2 = swap_y(add_low(a["Y2"], z1, x1))
    z3 = ring_back(add_low(a["R3"], x2))
    x3 = swap_x(after(a["X2"], x2))
    y3 = swap_y(after(a["Y1"], y2))
    z4 = ring_back(add_low(a["R2"], y2, z3, x3))
    x4 = swap_x(after(a["X1"], x3))
    y4 = swap_y(after(add_low(a["D0"], z2), y3))
    z5 = ring_back(add_low(a["R1"], y3, z4, x4))
    x5 = swap_x(add_low(a["X0"], y4))
    y5 = swap_y(after(a["Y0"], y4))
    return a["R0"], z5, x5, y5


def gather_plain(params):
    flat = lax.all_gather(params.astype(BF)[0], "wide", axis=0, tiled=True)
    flat = jnp.pad(flat, (0, PAD_ROWS * D - flat.shape[0])).reshape(PAD_ROWS, D)
    head = jnp.swapaxes(flat[:QKV_ROWS].reshape(2, 96, 3, D), 1, 2).reshape(QKV_ROWS, D)
    flat = jnp.concatenate([head, flat[QKV_ROWS:]], axis=0)
    mats = lax.all_gather(flat, "narrow", axis=0, tiled=True).reshape(2, 2, PAD_ROWS, D)
    pairs = []
    for core in range(2):
        pair = mats[:, core]
        pairs.append((jnp.concatenate([pair[:, :D], pair[:, MAT_ROWS:]], axis=1), pair[:, D:MAT_ROWS]))
    return pairs


def scatter_plain(pairs, shard, wide):
    mats = [jnp.concatenate([att[:, :D], ff, att[:, D:]], axis=1) for att, ff in pairs]
    grads = jnp.stack(mats, axis=1).reshape(-1, D)
    mine = lax.psum_scatter(grads, "narrow", scatter_dimension=0, tiled=True)
    head = jnp.swapaxes(mine[:QKV_ROWS].reshape(2, 3, 96, D), 1, 2).reshape(QKV_ROWS, D)
    flat = jnp.concatenate([head, mine[QKV_ROWS:]], axis=0).reshape(-1)[: shard * wide]
    return lax.psum_scatter(flat.astype(F32), "wide", scatter_dimension=0, tiled=True).reshape(1, shard)


def body(hidden_in, out_grad, pair_lengths, params, momentum, average):
    wide, ranks = lax.axis_size("wide"), lax.axis_size("narrow")
    shard = params.shape[1]
    rows, spare, fits = aligned_plan(shard, wide, ranks)
    at_wide, at_narrow = lax.axis_index("wide"), lax.axis_index("narrow")
    if fits:
        place = jnp.stack([at_wide, at_narrow // 2, at_narrow % 2]).astype(jnp.int32)
        block = own_block(place, params, rows, spare, wide)
        own_att, own_ff = gather_blocks(block, at_wide // 2, at_wide % 2, rows)
        got_att = swap_core(own_att)
        got_ff = swap_core(after(own_ff, got_att))
    else:
        place = jnp.zeros((3,), jnp.int32)
        (own_att, own_ff), (got_att, got_ff) = gather_plain(params)
    scalars = jnp.concatenate([pair_lengths[0], place])
    tails = jnp.concatenate([own_att[:, D:], got_att[:, D:]], axis=0)

    qkv, wq, mixed, probs, xp, n1, r1 = attention_forward(scalars, hidden_in, own_att, got_att, tails)
    block_out, own_ffg, got_ffg, grad_one, ga, vec_g, up_g = feed_forward(
        place, n1, r1, out_grad, own_ff, got_ff, tails
    )
    own_attg, got_attg, in_grad = attention_backward(
        place, ga, own_att, got_att, qkv, wq, mixed, probs, xp, vec_g, up_g, grad_one
    )

    device_count = wide * ranks
    rate = 1.0 / (32.0 * math.sqrt(hidden_in.shape[0] * device_count))
    if fits:
        got = swap_core(got_attg), swap_core(got_ffg)
        parts = reduce_windows((own_attg, own_ffg), got, at_wide // 2, at_wide % 2, rows)
        grads, new_params, new_momentum, new_average, low = update_shard(
            place, parts, params, momentum, average, rate, rows, spare, wide
        )
    else:
        grads = scatter_plain(((own_attg, own_ffg), (got_attg, got_ffg)), shard, wide)
        new_momentum = 0.5 * momentum + rate * grads
        new_params = params - (rate * grads + 0.5 * new_momentum)
        new_average = 0.5 * average + 0.5 * new_params
        low = new_params.astype(BF)
    return (
        block_out,
        in_grad,
        grads,
        new_params,
        new_momentum,
        new_average,
        low,
    )


def solution(mesh):
    rows = P(("wide", "narrow"), None)
    flat = P("narrow", "wide")
    return jax.shard_map(
        body,
        mesh=mesh,
        in_specs=(rows, rows, rows, flat, flat, flat),
        out_specs=(rows, rows, flat, flat, flat, flat, flat),
        check_vma=False,
    )
```

```python
import functools
import math

import jax
import jax.numpy as jnp
from jax import lax
from jax.experimental import pallas as pl
from jax.experimental.pallas import tpu as pltpu
from jax.sharding import PartitionSpec as P

D = 768
HEADS = 12
FF = 3072
HD = 64
BUCKETS = 256
L = 512
RANKS = 4
PART = D // RANKS
HPR = HEADS // RANKS
SLOTS = 2
QKV_ROWS = 3 * PART
TILE_ROWS = 8
MAT_ROWS = 3 * D
PAD_ROWS = MAT_ROWS + TILE_ROWS
ATT_ROWS = D + TILE_ROWS
FF_ROWS = 2 * D
BLK = 128
NBLK = L // BLK
NEG = -1000000000.0
VMEM_LIMIT = 60 * 1024 * 1024
BF = jnp.bfloat16
F32 = jnp.float32


def mm(a, b):
    return jnp.dot(a, b, preferred_element_type=F32)


def mm_nt(a, b):
    return lax.dot_general(a, b, (((1,), (1,)), ((), ())), preferred_element_type=F32)


def mm_tn(a, b):
    return lax.dot_general(a, b, (((0,), (0,)), ((), ())), preferred_element_type=F32)


def qkv_pieces():
    for b in range(2):
        for j in range(4):
            for c in range(3):
                t, q = divmod(3 * j + c, 4)
                yield 288 * b + 96 * t, PART * q, PART * j + 96 * b, PART * c


def column_order():
    d = lax.broadcasted_iota(jnp.int32, (D, D), 0)
    n = lax.broadcasted_iota(jnp.int32, (D, D), 1)
    j = (n >= PART).astype(jnp.int32) + (n >= 2 * PART).astype(jnp.int32) + (n >= 3 * PART).astype(jnp.int32)
    return (d == 4 * (n - PART * j) + j).astype(F32).astype(BF)


def slot_of(r, place_ref):
    return ((r // 2) ^ place_ref[1]) + 2 * ((r % 2) ^ place_ref[2])


def slice_of(slot, place_ref):
    return 2 * ((slot % 2) ^ place_ref[1]) + ((slot // 2) ^ place_ref[2])


def vector_rows(tails_ref, place_ref):
    chunks = []
    for r in range(RANKS):
        k = slot_of(r, place_ref)
        chunks.append(tails_ref[k, 2:3, 384:768])
        chunks.append(tails_ref[k, 3:4, 0:384])
        chunks.append(tails_ref[k, 3:4, 384:768])
    return [
        jnp.concatenate([chunks[2 * v], chunks[2 * v + 1]], axis=1).astype(F32) for v in range(6)
    ]


def table_order():
    src = lax.broadcasted_iota(jnp.int32, (D, D), 0)
    dst = lax.broadcasted_iota(jnp.int32, (D, D), 1)
    hh = (dst >= BUCKETS).astype(jnp.int32) + (dst >= 2 * BUCKETS).astype(jnp.int32)
    return (src == 3 * (dst - BUCKETS * hh) + hh).astype(F32).astype(BF)


def normalize(values):
    centred = values - jnp.mean(values, axis=-1, keepdims=True)
    inv = lax.rsqrt(jnp.mean(centred * centred, axis=-1, keepdims=True) + 1e-05)
    return centred * inv, inv


def norm_backward(e, normed, inv):
    return inv * (
        e - jnp.mean(e, axis=-1, keepdims=True) - normed * jnp.mean(e * normed, axis=-1, keepdims=True)
    )


def col_sum(values):
    return jnp.sum(values, axis=0, keepdims=True)


def call(kernel, name, grid, in_specs, out_specs, out_shape, scratch, args, vmem=VMEM_LIMIT, flops=0, moved=0):
    return pl.pallas_call(
        kernel,
        grid_spec=pltpu.PrefetchScalarGridSpec(
            num_scalar_prefetch=1,
            grid=grid,
            in_specs=in_specs,
            out_specs=out_specs,
            scratch_shapes=scratch,
        ),
        out_shape=out_shape,
        compiler_params=pltpu.CompilerParams(vmem_limit_bytes=vmem),
        cost_estimate=pl.CostEstimate(flops=flops, bytes_accessed=moved, transcendentals=0),
        name=name,
    )(*args)


def whole(*shape):
    return pl.BlockSpec(shape, lambda *_: (0,) * len(shape))


def shaped(dtype, *shape):
    return jax.ShapeDtypeStruct(shape, dtype)


def block_kernel(rows, lead, shift, place_ref, flat_ref, out_ref, rows_s):
    w = place_ref[0]
    count = flat_ref.shape[1] // 128
    rows_s[0:lead, :] = jnp.zeros((lead, 128), F32)
    rows_s[lead : lead + count, :] = flat_ref[...].reshape(count, 128)
    rows_s[lead + count :, :] = jnp.zeros((rows_s.shape[0] - lead - count, 128), F32)
    start = lead - shift * w
    third = rows // 3

    @pl.when(w < 2)
    def _():
        for t in range(3):
            for c in range(6):
                out_ref[third * t : third * (t + 1), 128 * c : 128 * (c + 1)] = rows_s[
                    pl.ds(start + 6 * t + c, third, stride=18), :
                ].astype(BF)

    @pl.when(w >= 2)
    def _():
        for c in range(6):
            out_ref[0:rows, 128 * c : 128 * (c + 1)] = rows_s[
                pl.ds(start + c, rows, stride=6), :
            ].astype(BF)

    for c in range(6):
        out_ref[rows : rows + TILE_ROWS, 128 * c : 128 * (c + 1)] = rows_s[
            pl.ds(start + 6 * rows + c, TILE_ROWS, stride=6), :
        ].astype(BF)


def own_block(place, params, rows, spare, wide):
    count = params.shape[1] // 128
    lead = spare // 128 * wide
    total = -(-(lead + 6 * (rows + TILE_ROWS)) // 8) * 8
    return call(
        functools.partial(block_kernel, rows, lead, spare // 128),
        "own_block", (1,),
        [whole(*params.shape)],
        whole(rows + TILE_ROWS, D),
        shaped(BF, rows + TILE_ROWS, D),
        [pltpu.VMEM((total, 128), F32)],
        (place, params),
        vmem=16 * 1024 * 1024,
    )


def update_kernel(
    rows, lead, shift, rate, place_ref, kept_ref, near_ref, second_ref, ring_ref, params_ref, momentum_ref, average_ref,
    grads_ref, new_params_ref, new_momentum_ref, new_average_ref, low_ref, rows_s,
):
    w = place_ref[0]
    count = params_ref.shape[1] // 128
    block = (
        kept_ref[...].astype(F32) + near_ref[...].astype(F32) + second_ref[...].astype(F32) + ring_ref[...].astype(F32)
    )
    start = lead - shift * w
    third = rows // 3

    @pl.when(w < 2)
    def _():
        for t in range(3):
            for c in range(6):
                rows_s[pl.ds(start + 6 * t + c, third, stride=18), :] = block[
                    third * t : third * (t + 1), 128 * c : 128 * (c + 1)
                ]

    @pl.when(w >= 2)
    def _():
        for c in range(6):
            rows_s[pl.ds(start + c, rows, stride=6), :] = block[0:rows, 128 * c : 128 * (c + 1)]

    for c in range(6):
        rows_s[pl.ds(start + 6 * rows + c, TILE_ROWS, stride=6), :] = block[
            rows : rows + TILE_ROWS, 128 * c : 128 * (c + 1)
        ]
    grads = rows_s[lead : lead + count, :].reshape(params_ref.shape)
    grads_ref[...] = grads
    params = params_ref[...]
    new_momentum = 0.5 * momentum_ref[...] + rate * grads
    new_params = params - (rate * grads + 0.5 * new_momentum)
    new_momentum_ref[...] = new_momentum
    new_params_ref[...] = new_params
    new_average_ref[...] = 0.5 * average_ref[...] + 0.5 * new_params
    low_ref[...] = new_params.astype(BF)


def update_shard(place, parts, params, momentum, average, rate, rows, spare, wide):
    count = params.shape[1] // 128
    lead = spare // 128 * wide
    total = -(-(lead + 6 * (rows + TILE_ROWS)) // 8) * 8
    kept, near, second, ring = parts
    cap = rows + TILE_ROWS
    flat = whole(*params.shape)
    return call(
        functools.partial(update_kernel, rows, lead, spare // 128, rate),
        "update_shard", (1,),
        [whole(cap, D)] * 4 + [flat] * 3,
        [flat] * 5,
        [shaped(F32, *params.shape)] * 4 + [shaped(BF, *params.shape)],
        [pltpu.VMEM((total, 128), F32)],
        (place, kept, near, second, ring, params, momentum, average),
        vmem=32 * 1024 * 1024,
    )


def merge_kernel(rows, at_ref, *refs):
    pieces, (att_ref, ff_ref), (mats, edges, in_sem, out_sem) = refs[:16], refs[16:18], refs[18:]
    copies = {}
    for slot in range(SLOTS):
        for i in range(8):
            w = at_ref[i]
            piece = pieces[8 * slot + i]
            main = pltpu.make_async_copy(
                piece.at[0:rows],
                mats.at[slot, pl.ds(pl.multiple_of(rows * w, TILE_ROWS), rows)],
                in_sem.at[slot, i, 0],
            )
            edge = pltpu.make_async_copy(
                piece.at[rows : rows + TILE_ROWS], edges.at[slot, w], in_sem.at[slot, i, 1]
            )
            main.start()
            edge.start()
            copies[slot, i] = (main, edge)
    outs = []
    for slot in range(SLOTS):
        for i in range(8):
            for c in copies[slot, i]:
                c.wait()
        for w in range(1, 8):
            at = rows * w
            mats[slot, at : at + TILE_ROWS, :] = mats[slot, at : at + TILE_ROWS, :] + edges[slot, w - 1]
        mats[slot, MAT_ROWS:PAD_ROWS, :] = edges[slot, 7]
        for n, (src, dst) in enumerate(
            (
                (mats.at[slot, 0:D], att_ref.at[slot, 0:D]),
                (mats.at[slot, MAT_ROWS:PAD_ROWS], att_ref.at[slot, D:ATT_ROWS]),
                (mats.at[slot, D:MAT_ROWS], ff_ref.at[slot]),
            )
        ):
            copy = pltpu.make_async_copy(src, dst, out_sem.at[slot, n])
            copy.start()
            outs.append(copy)
    for copy in outs:
        copy.wait()


def merge_blocks(at, pieces, rows):
    hbm = pl.BlockSpec(memory_space=pl.ANY)
    return call(
        functools.partial(merge_kernel, rows),
        "merge_weights", (1,),
        [hbm] * 16,
        [hbm] * 2,
        [shaped(BF, SLOTS, ATT_ROWS, D), shaped(BF, SLOTS, FF_ROWS, D)],
        [
            pltpu.VMEM((SLOTS, PAD_ROWS, D), BF),
            pltpu.VMEM((SLOTS, 8, TILE_ROWS, D), BF),
            pltpu.SemaphoreType.DMA((SLOTS, 8, 2)),
            pltpu.SemaphoreType.DMA((SLOTS, 3)),
        ],
        (at, *pieces),
    )


def window_kernel(rows, windows, at_ref, own_att, own_ff, got_att, got_ff, *refs):
    outs, (own_s, got_s, own_sem, got_sem) = refs[:-4], refs[-4:]
    cap = rows + TILE_ROWS

    def fetch(w, slot, att, ff, buf, sem):
        @pl.when(w < 2)
        def _():
            src = att.at[slot, pl.ds(pl.multiple_of(rows * w, TILE_ROWS), cap)]
            pltpu.make_async_copy(src, buf, sem).start()

        @pl.when(w == 2)
        def _():
            pltpu.make_async_copy(att.at[slot, 2 * rows : D], buf.at[0 : D - 2 * rows], sem).start()
            pltpu.make_async_copy(ff.at[slot, 0 : 3 * rows + TILE_ROWS - D], buf.at[D - 2 * rows : cap], sem).start()

        @pl.when((w > 2) & (w < 7))
        def _():
            src = ff.at[slot, pl.ds(pl.multiple_of(rows * w - D, TILE_ROWS), cap)]
            pltpu.make_async_copy(src, buf, sem).start()

        @pl.when(w == 7)
        def _():
            pltpu.make_async_copy(ff.at[slot, 7 * rows - D : FF_ROWS], buf.at[0:rows], sem).start()
            pltpu.make_async_copy(att.at[slot, D:ATT_ROWS], buf.at[rows:cap], sem).start()

    for n, (slot, where) in enumerate(windows):
        w = at_ref[where]
        fetch(w, slot, own_att, own_ff, own_s.at[n], own_sem.at[n])
        fetch(w, slot, got_att, got_ff, got_s.at[n], got_sem.at[n])
    for n in range(len(windows)):
        pltpu.make_async_copy(own_ff.at[0, 0:cap], own_s.at[n], own_sem.at[n]).wait()
        pltpu.make_async_copy(own_ff.at[0, 0:cap], got_s.at[n], got_sem.at[n]).wait()
        outs[n][...] = (own_s[n].astype(F32) + got_s[n].astype(F32)).astype(BF)


def split_windows(at, names, own, got, rows):
    hbm = pl.BlockSpec(memory_space=pl.ANY)
    cap = rows + TILE_ROWS
    n = len(names)
    windows = [(int(name[0] in "YD"), int(name[1]) + 4 * int(name[0] in "XD")) for name in names]
    outs = call(
        functools.partial(window_kernel, rows, windows),
        "split_windows", (1,),
        [hbm] * 4,
        [whole(cap, D)] * n,
        [shaped(BF, cap, D)] * n,
        [
            pltpu.VMEM((n, cap, D), BF),
            pltpu.VMEM((n, cap, D), BF),
            pltpu.SemaphoreType.DMA((n,)),
            pltpu.SemaphoreType.DMA((n,)),
        ],
        (at, *own, *got),
    )
    return dict(zip(names, outs))


def segment_of(pos, len_ref):
    end0 = len_ref[0]
    end1 = end0 + len_ref[1]
    end2 = end1 + len_ref[2]
    return (
        (pos >= end0).astype(jnp.int32)
        + (pos >= end1).astype(jnp.int32)
        + (pos >= end2).astype(jnp.int32)
    )


def att_fwd_kernel(
    scal_ref, x_ref, mq0_ref, wo0_ref, mq1_ref, wo1_ref, tails_ref,
    qkv_ref, wq_ref, mixed_ref, probs_ref, xp_ref, n1_ref, r1_ref,
    table_s, acc_s, wo_s,
):
    s = pl.program_id(0)
    len_ref = scal_ref

    @pl.when(s == 0)
    def _():
        xp_ref[...] = mm(x_ref[...], column_order()).astype(BF)
        acc_s[...] = jnp.zeros_like(acc_s)
        flat = jnp.concatenate(
            [
                jnp.concatenate([tails_ref[k, 1:2, 384:768], tails_ref[k, 2:3, 0:384]], axis=1).astype(F32)
                for k in range(RANKS)
            ]
            + [jnp.zeros((8 - RANKS, D), F32)],
            axis=0,
        ).astype(BF)
        tables = mm(flat, table_order())
        for k in range(RANKS):
            for h in range(HPR):
                row = tables[k : k + 1, BUCKETS * h : BUCKETS * (h + 1)]
                table_s[k, h : h + 1, :] = jnp.concatenate(
                    [
                        row,
                        jnp.broadcast_to(row[:, 255:256], (1, BLK)),
                        jnp.broadcast_to(row[:, 0:1], (1, BLK)),
                    ],
                    axis=1,
                )

    def load(mq_ref, wo_ref):
        for src_row, src_col, dst_row, dst_col in qkv_pieces():
            wq_ref[0, dst_row : dst_row + 96, dst_col : dst_col + PART] = mq_ref[
                0, src_row : src_row + 96, src_col : src_col + PART
            ]
        wo_s[...] = wo_ref[0]

    @pl.when(s < SLOTS)
    def _():
        load(mq0_ref, wo0_ref)

    @pl.when(s >= SLOTS)
    def _():
        load(mq1_ref, wo1_ref)

    first = tails_ref[s, 0:1, :]
    bias = jnp.concatenate(
        [first[:, 0:PART], jnp.zeros((1, PART), BF), first[:, PART : 2 * PART]], axis=1
    ).astype(F32)
    qkv = (mm(xp_ref[...], wq_ref[0]) + bias).astype(BF)
    qkv_ref[0] = qkv

    seg_j = segment_of(lax.broadcasted_iota(jnp.int32, (1, L), 1), len_ref)
    table = table_s[s]
    heads = []
    for h in range(HPR):
        q = qkv[:, HD * h : HD * (h + 1)]
        k = qkv[:, PART + HD * h : PART + HD * (h + 1)]
        v = qkv[:, 2 * PART + HD * h : 2 * PART + HD * (h + 1)]
        row = table[h : h + 1, :]
        near = pltpu.roll(jnp.broadcast_to(row, (BLK, 4 * BLK)), 0, 1, stride=1, stride_axis=0)
        far_right = jnp.broadcast_to(row[:, 255:256], (BLK, BLK))
        far_left = jnp.broadcast_to(row[:, 511:512], (BLK, BLK))
        for i in range(NBLK):
            seg_i = segment_of(
                lax.broadcasted_iota(jnp.int32, (BLK, 1), 0) + BLK * i, len_ref
            )
            parts = []
            for jb in range(NBLK):
                delta = jb - i
                if abs(delta) <= 1:
                    parts.append(near[:, BLK * (delta + 1) : BLK * (delta + 2)])
                else:
                    parts.append(far_right if delta > 0 else far_left)
            logits = mm_nt(q[BLK * i : BLK * (i + 1)], k) * 0.125 + jnp.concatenate(parts, axis=1)
            logits = jnp.where(seg_i == seg_j, logits, NEG)
            top = jnp.max(logits, axis=-1, keepdims=True)
            expo = jnp.exp(logits - top)
            total = jnp.sum(expo, axis=-1, keepdims=True)
            probs_ref[0, h, BLK * i : BLK * (i + 1), :] = (expo * (1.0 / total)).astype(BF)
        heads.append(mm(probs_ref[0, h], v))
    mixed = jnp.concatenate(heads, axis=1).astype(BF)
    mixed_ref[0] = mixed
    acc_s[...] += mm(mixed, wo_s[...])

    @pl.when(s == RANKS - 1)
    def _():
        vec = vector_rows(tails_ref, PlaceView(scal_ref))
        normed, inv = normalize(x_ref[...].astype(F32) + acc_s[...] + vec[0])
        n1_ref[...] = normed
        r1_ref[...] = jnp.broadcast_to(inv, (L, BLK))


class PlaceView:
    def __init__(self, ref):
        self.ref = ref

    def __getitem__(self, i):
        return self.ref[4 + i]


def attention_forward(scalars, x, own_att, got_att, tails):
    per = lambda *shape: pl.BlockSpec((1, *shape), lambda s, n: (s,) + (0,) * len(shape))
    own = lambda rows, at: pl.BlockSpec((1, rows, D), lambda s, n: (jnp.minimum(s, 1), at, 0))
    got = lambda rows, at: pl.BlockSpec((1, rows, D), lambda s, n: (jnp.maximum(s - 2, 0), at, 0))
    return call(
        att_fwd_kernel,
        "attention_forward", (RANKS,),
        [
            whole(L, D),
            own(QKV_ROWS, 0), own(PART, QKV_ROWS // PART),
            got(QKV_ROWS, 0), got(PART, QKV_ROWS // PART),
            whole(RANKS, TILE_ROWS, D),
        ],
        [per(L, QKV_ROWS), per(D, QKV_ROWS), per(L, PART), per(HPR, L, L), whole(L, D), whole(L, D), whole(L, BLK)],
        [
            shaped(BF, RANKS, L, QKV_ROWS),
            shaped(BF, RANKS, D, QKV_ROWS),
            shaped(BF, RANKS, L, PART),
            shaped(BF, RANKS, HPR, L, L),
            shaped(BF, L, D),
            shaped(F32, L, D),
            shaped(F32, L, BLK),
        ],
        [pltpu.VMEM((RANKS, 8, 512), F32), pltpu.VMEM((L, D), F32), pltpu.VMEM((PART, D), BF)],
        (scalars, x, own_att, own_att, got_att, got_att, tails),
        flops=6_000_000_000, moved=24_000_000,
    )


def ffn_kernel(
    place_ref, n1_ref, r1_ref, og_ref, up0_ref, down0_ref, up1_ref, down1_ref, tails_ref,
    block_ref, grad0_ref, grad1_ref, grad_one_ref, ga_ref, vec_ref, bup_ref,
    fn_s, fl_s, slope_s, act_s, down_s, gd_s, gf_s,
):
    step = pl.program_id(0)
    inv_root2 = 1.0 / math.sqrt(2.0)

    @pl.when(step == 0)
    def _():
        vec = vector_rows(tails_ref, place_ref)
        first = n1_ref[...] * vec[2] + vec[3]
        fn_s[...] = first
        fl_s[...] = first.astype(BF)
        down_s[...] = jnp.zeros_like(down_s)

    def forward(slot, up_ref, down_ref):
        bias = jnp.concatenate([tails_ref[slot, 0:1, 384:768], tails_ref[slot, 1:2, 0:384]], axis=1)
        up = mm(fl_s[...], up_ref[0]) + bias.astype(F32)
        half = 0.5 * (1.0 + lax.erf(up * inv_root2))
        act = (up * half).astype(BF)
        slope_s[slot] = half + up * jnp.exp(-0.5 * up * up) * (1.0 / math.sqrt(2.0 * math.pi))
        act_s[slot] = act
        down_s[...] += mm(act, down_ref[0])

    @pl.when(step < 2)
    def _():
        forward(step, up0_ref, down0_ref)

    @pl.when((step == 2) | (step == 3))
    def _():
        forward(step, up1_ref, down1_ref)

    @pl.when(step == RANKS)
    def _():
        vec = vector_rows(tails_ref, place_ref)
        normed, inv = normalize(fn_s[...] + down_s[...] + vec[1])
        block_ref[...] = (normed * vec[4] + vec[5]).astype(BF)
        og = og_ref[...].astype(F32)
        vec_ref[4:5, :] = col_sum(og * normed)
        vec_ref[5:6, :] = col_sum(og)
        grad_two = norm_backward(og * vec[4], normed, inv)
        low = grad_two.astype(BF)
        gd_s[...] = low
        vec_ref[1:2, :] = col_sum(low.astype(F32))
        vec_ref[6:8, :] = jnp.zeros((2, D), F32)
        gf_s[...] = grad_two

    def backward(slot, up_ref, down_ref, grad_ref):
        gd = gd_s[...]
        grad_ref[0, D:FF_ROWS, :] = mm_tn(act_s[slot], gd).astype(BF)
        gu = (mm_nt(gd, down_ref[0]) * slope_s[slot]).astype(BF)
        bup_ref[0, 0:1, :] = col_sum(gu.astype(F32))
        bup_ref[0, 1:8, :] = jnp.zeros((7, D), F32)
        grad_ref[0, 0:D, :] = mm_tn(fl_s[...], gu).astype(BF)
        gf_s[...] += mm_nt(gu, up_ref[0])

    @pl.when((step == 4) | (step == 5))
    def _():
        backward(step - 2, up1_ref, down1_ref, grad1_ref)

    @pl.when(step >= 6)
    def _():
        backward(step - 6, up0_ref, down0_ref, grad0_ref)

    @pl.when(step == 2 * RANKS - 1)
    def _():
        vec = vector_rows(tails_ref, place_ref)
        f = gf_s[...]
        normed = n1_ref[...]
        vec_ref[2:3, :] = col_sum(f * normed)
        vec_ref[3:4, :] = col_sum(f)
        grad_one = norm_backward(f * vec[2], normed, r1_ref[:, 0:1])
        grad_one_ref[...] = grad_one
        low = grad_one.astype(BF)
        ga_ref[...] = low
        vec_ref[0:1, :] = col_sum(low.astype(F32))


def feed_forward(place, n1, r1, out_grad, own_ff, got_ff, tails):
    def own_at(half):
        return lambda s, n: ((((s >= 1) & (s <= 3)) | (s == 7)).astype(jnp.int32), half, 0)

    def got_at(half):
        return lambda s, n: (((s == 3) | (s >= 5)).astype(jnp.int32), half, 0)

    wt = lambda index: pl.BlockSpec((1, D, D), index)
    return call(
        ffn_kernel,
        "feed_forward", (2 * RANKS,),
        [
            whole(L, D), whole(L, BLK), whole(L, D),
            wt(own_at(0)), wt(own_at(1)), wt(got_at(0)), wt(got_at(1)),
            whole(RANKS, TILE_ROWS, D),
        ],
        [
            whole(L, D),
            pl.BlockSpec((1, FF_ROWS, D), lambda s, n: ((s >= 7).astype(jnp.int32), 0, 0)),
            pl.BlockSpec((1, FF_ROWS, D), lambda s, n: ((s >= 5).astype(jnp.int32), 0, 0)),
            whole(L, D), whole(L, D), whole(8, D),
            pl.BlockSpec((1, 8, D), lambda s, n: (lax.rem(jnp.maximum(s, 4) - 2, 4), 0, 0)),
        ],
        [
            shaped(BF, L, D),
            shaped(BF, SLOTS, FF_ROWS, D),
            shaped(BF, SLOTS, FF_ROWS, D),
            shaped(F32, L, D),
            shaped(BF, L, D),
            shaped(F32, 8, D),
            shaped(F32, RANKS, 8, D),
        ],
        [
            pltpu.VMEM((L, D), F32),
            pltpu.VMEM((L, D), BF),
            pltpu.VMEM((RANKS, L, D), F32),
            pltpu.VMEM((RANKS, L, D), BF),
            pltpu.VMEM((L, D), F32),
            pltpu.VMEM((L, D), BF),
            pltpu.VMEM((L, D), F32),
        ],
        (place, n1, r1, out_grad, own_ff, own_ff, got_ff, got_ff, tails),
        flops=14_500_000_000, moved=36_000_000,
    )


def diagonal_sums(block):
    half = block.shape[0] // 2
    while half >= 8:
        block = block[:half] + pltpu.roll(block[half:], 4 * BLK - half, 1)
        half //= 2
    row = lax.broadcasted_iota(jnp.int32, (8, 1), 0)
    for bit in (4, 2, 1):
        block = jnp.where((row & bit) > 0, pltpu.roll(block, 4 * BLK - bit, 1), block)
    return col_sum(block)


def att_bwd_kernel(
    place_ref, ga_ref, wo0_ref, wo1_ref, qkv_ref, probs_ref, mixed_ref, wq_ref, xp_ref, vec_ref, bup_ref, grad_one_ref,
    da0_ref, da1_ref, in_grad_ref,
    ds_s, near_s, sums_s, dx_s, order_s, wo_s, da_s,
):
    s = pl.program_id(0)
    slot = lax.rem(s + SLOTS, RANKS)

    @pl.when(s == 0)
    def _():
        order_s[...] = table_order()
        dx_s[...] = jnp.zeros_like(dx_s)
        sums_s[...] = jnp.zeros_like(sums_s)
        da_s[D:ATT_ROWS, :] = jnp.zeros((TILE_ROWS, D), BF)

    @pl.when(slot < SLOTS)
    def _():
        wo_s[...] = wo0_ref[0]

    @pl.when(slot >= SLOTS)
    def _():
        wo_s[...] = wo1_ref[0]

    ga = ga_ref[...]
    da_s[QKV_ROWS:D, :] = mm_tn(mixed_ref[0], ga).astype(BF)
    dm_all = mm_nt(ga, wo_s[...]).astype(BF)
    qkv = qkv_ref[0]
    dq, dk, dv = [], [], []
    for h in range(HPR):
        q = qkv[:, HD * h : HD * (h + 1)]
        k = qkv[:, PART + HD * h : PART + HD * (h + 1)]
        v = qkv[:, 2 * PART + HD * h : 2 * PART + HD * (h + 1)]
        dm = dm_all[:, HD * h : HD * (h + 1)]
        far_left = jnp.zeros((BLK, BLK), F32)
        far_right = jnp.zeros((BLK, BLK), F32)
        for i in range(NBLK):
            rows = slice(BLK * i, BLK * (i + 1))
            p = probs_ref[0, h, rows, :].astype(F32)
            dp = mm_nt(dm[rows], v)
            ds = (p * (dp - jnp.sum(p * dp, axis=-1, keepdims=True))).astype(BF)
            ds_s[rows, :] = ds
            ds = ds.astype(F32)
            for jb in range(NBLK):
                piece = ds[:, BLK * jb : BLK * (jb + 1)]
                delta = jb - i
                if abs(delta) <= 1:
                    cols = slice(BLK * (delta + 1), BLK * (delta + 2))
                    if i == max(0, -delta):
                        near_s[:, cols] = piece
                    else:
                        near_s[:, cols] += piece
                elif delta > 0:
                    far_right += piece
                else:
                    far_left += piece
        near_s[:, 3 * BLK :] = jnp.zeros((BLK, BLK), F32)
        sums_s[h : h + 1, 0 : 4 * BLK] = diagonal_sums(near_s[...])
        sums_s[h : h + 1, 4 * BLK : 5 * BLK] = col_sum(far_left)
        sums_s[h : h + 1, 5 * BLK : 6 * BLK] = col_sum(far_right)
        dscore = ds_s[...]
        dq.append(mm(dscore, k) * 0.125)
        dk.append(mm_tn(dscore, q) * 0.125)
        dv.append(mm_tn(probs_ref[0, h], dm))
    dqkv = jnp.concatenate(dq + dk + dv, axis=1).astype(BF)

    qv = col_sum(dqkv.astype(F32))
    sums = sums_s[...]
    lane = lax.broadcasted_iota(jnp.int32, (1, 6 * BLK), 1)
    is_left = (lane == 0) | ((lane >= 3 * BLK) & (lane < 5 * BLK))
    is_right = ((lane >= BUCKETS - 1) & (lane < 3 * BLK)) | (lane >= 5 * BLK)
    left = jnp.sum(jnp.where(is_left, sums, 0.0), axis=-1, keepdims=True)
    right = jnp.sum(jnp.where(is_right, sums, 0.0), axis=-1, keepdims=True)
    sums = jnp.where(lane == 0, left, jnp.where(lane == BUCKETS - 1, right, sums))
    table = jnp.concatenate([sums[h : h + 1, :BUCKETS] for h in range(HPR)], axis=1)
    table = jnp.broadcast_to(table, (8, D)).astype(BF)
    table = mm_nt(table, order_s[...])[0:1]
    r = slice_of(slot, place_ref)
    vecs = []
    for i in range(3):
        m = 3 * r + i
        row = vec_ref[pl.ds(m // 2, 1), :]
        vecs.append(jnp.where(m % 2 == 0, row[:, 0:384], row[:, 384:768]))
    bup = bup_ref[0, 0:1, :]
    tail = jnp.concatenate(
        [
            jnp.concatenate([qv[:, 0:PART], qv[:, 2 * PART :], bup[:, 0:384]], axis=1),
            jnp.concatenate([bup[:, 384:768], table[:, 0:384]], axis=1),
            jnp.concatenate([table[:, 384:768], vecs[0]], axis=1),
            jnp.concatenate([vecs[1], vecs[2]], axis=1),
            jnp.zeros((TILE_ROWS - 4, D), F32),
        ],
        axis=0,
    )
    da_s[D:ATT_ROWS, :] = tail.astype(BF)

    dw = mm_tn(xp_ref[...], dqkv).astype(BF)
    for src_row, src_col, dst_row, dst_col in qkv_pieces():
        da_s[src_row : src_row + 96, src_col : src_col + PART] = dw[
            dst_row : dst_row + 96, dst_col : dst_col + PART
        ]
    dx_s[...] += mm_nt(dqkv, wq_ref[0])

    @pl.when(slot < SLOTS)
    def _():
        da0_ref[0] = da_s[...]

    @pl.when(slot >= SLOTS)
    def _():
        da1_ref[0] = da_s[...]

    @pl.when(s == RANKS - 1)
    def _():
        in_grad_ref[...] = grad_one_ref[...] + mm_nt(dx_s[...].astype(BF), column_order())


def attention_backward(place, ga, own_att, got_att, qkv, wq, mixed, probs, xp, vec_g, up_g, grad_one):
    per = lambda *shape: pl.BlockSpec(
        (1, *shape), lambda s, n: (lax.rem(s + SLOTS, RANKS),) + (0,) * len(shape)
    )
    own = lambda s: jnp.maximum(s - 2, 0)
    got = lambda s: jnp.minimum(s, 1)
    return call(
        att_bwd_kernel,
        "attention_backward", (RANKS,),
        [
            whole(L, D),
            pl.BlockSpec((1, PART, D), lambda s, n: (own(s), QKV_ROWS // PART, 0)),
            pl.BlockSpec((1, PART, D), lambda s, n: (got(s), QKV_ROWS // PART, 0)),
            per(L, QKV_ROWS), per(HPR, L, L), per(L, PART), per(D, QKV_ROWS),
            whole(L, D), whole(8, D), per(8, D), whole(L, D),
        ],
        [
            pl.BlockSpec((1, ATT_ROWS, D), lambda s, n: (own(s), 0, 0)),
            pl.BlockSpec((1, ATT_ROWS, D), lambda s, n: (got(s), 0, 0)),
            whole(L, D),
        ],
        [shaped(BF, SLOTS, ATT_ROWS, D), shaped(BF, SLOTS, ATT_ROWS, D), shaped(F32, L, D)],
        [
            pltpu.VMEM((L, L), BF),
            pltpu.VMEM((BLK, 4 * BLK), F32),
            pltpu.VMEM((8, 6 * BLK), F32),
            pltpu.VMEM((L, D), F32),
            pltpu.VMEM((D, D), BF),
            pltpu.VMEM((PART, D), BF),
            pltpu.VMEM((ATT_ROWS, D), BF),
        ],
        (place, ga, own_att, got_att, qkv, probs, mixed, wq, xp, vec_g, up_g, grad_one),
        flops=12_000_000_000, moved=30_000_000,
    )


X_SWAP = [(w, w ^ 1) for w in range(8)]
Z_RING = [(w, (w + 2) % 8) for w in range(8)]
Y_SWAP = [(n, n ^ 2) for n in range(4)]
CORE_SWAP = [(n, n ^ 1) for n in range(4)]


def swap_x(a):
    return lax.ppermute(a, "wide", X_SWAP)


def swap_y(a):
    return lax.ppermute(a, "narrow", Y_SWAP)


def ring_z(a):
    return lax.ppermute(a, "wide", Z_RING)


def ring_back(a):
    return lax.ppermute(a, "wide", [(j, i) for i, j in Z_RING])


def swap_core(a):
    return lax.ppermute(a, "narrow", CORE_SWAP)


def after(value, earlier):
    return lax.optimization_barrier((value, earlier))[0]


def aligned_plan(shard, wide, ranks):
    unit = TILE_ROWS * D
    tiles, spare = divmod(shard, unit)
    rows = tiles * TILE_ROWS
    fits = (
        wide == 8
        and ranks == RANKS
        and spare * wide <= unit
        and spare % 128 == 0
        and rows * wide == MAT_ROWS
        and rows == QKV_ROWS // 2
    )
    return rows, spare, fits


def window_places(z, x):
    planes = jnp.mod(z - jnp.arange(4, dtype=jnp.int32), 4)
    return jnp.concatenate([2 * planes + x, 2 * planes + 1 - x])


def gather_blocks(r0, z, x, rows):
    r1, x0, y0 = ring_z(r0), swap_x(r0), swap_y(r0)
    d0 = swap_y(after(x0, y0))
    r2, x1, y1 = ring_z(r1), swap_x(after(r1, x0)), swap_y(after(r1, y0))
    r3, x2, y2 = ring_z(r2), swap_x(after(r2, x0)), swap_y(after(r2, d0))
    d1 = ring_z(after(d0, y1))
    x3 = swap_x(after(r3, x1))
    y3, d2, d3 = ring_z(after(y2, r3)), swap_x(after(y2, x2)), swap_y(after(x3, y1))
    pieces = [r0, r1, r2, r3, x0, x1, x2, x3, y0, y1, y2, y3, d0, d1, d2, d3]
    return merge_blocks(window_places(z, x), pieces, rows)


def add_low(*terms):
    total = terms[0].astype(F32)
    for term in terms[1:]:
        total = total + term.astype(F32)
    return total.astype(BF)


def reduce_windows(own, got, z, x, rows):
    at = window_places(z, x)
    a = split_windows(at, ("D3", "Y3", "D2", "D1"), own, got, rows)
    y1, z1, x1 = swap_y(a["D3"]), ring_back(a["Y3"]), swap_x(a["D2"])
    a |= split_windows(
        at, ("X3", "Y2", "Y1", "R3", "X2", "R2", "X1", "R1", "D0", "X0", "Y0", "R0"), own, got, rows
    )
    z2 = ring_back(after(a["D1"], x1))
    y3 = swap_y(after(a["Y1"], x1))
    far = add_low(a["X3"], y1)
    x2 = swap_x(far)
    y2 = swap_y(add_low(a["Y2"], z1, x1))
    x3 = swap_x(after(a["X2"], x2))
    z3 = ring_back(add_low(a["R3"], x2))
    x4 = swap_x(after(a["X1"], x3))
    y4 = swap_y(add_low(a["D0"], z2))
    z4 = ring_back(add_low(a["R2"], y2, z3, x3))
    y5 = swap_y(after(a["Y0"], y2))
    z5 = ring_back(add_low(a["R1"], y3, z4, x4))
    x5 = swap_x(add_low(a["X0"], y4))
    return a["R0"], z5, x5, y5


def gather_plain(params):
    flat = lax.all_gather(params.astype(BF)[0], "wide", axis=0, tiled=True)
    flat = jnp.pad(flat, (0, PAD_ROWS * D - flat.shape[0])).reshape(PAD_ROWS, D)
    head = jnp.swapaxes(flat[:QKV_ROWS].reshape(2, 96, 3, D), 1, 2).reshape(QKV_ROWS, D)
    flat = jnp.concatenate([head, flat[QKV_ROWS:]], axis=0)
    mats = lax.all_gather(flat, "narrow", axis=0, tiled=True).reshape(2, 2, PAD_ROWS, D)
    pairs = []
    for core in range(2):
        pair = mats[:, core]
        pairs.append((jnp.concatenate([pair[:, :D], pair[:, MAT_ROWS:]], axis=1), pair[:, D:MAT_ROWS]))
    return pairs


def scatter_plain(pairs, shard, wide):
    mats = [jnp.concatenate([att[:, :D], ff, att[:, D:]], axis=1) for att, ff in pairs]
    grads = jnp.stack(mats, axis=1).reshape(-1, D)
    mine = lax.psum_scatter(grads, "narrow", scatter_dimension=0, tiled=True)
    head = jnp.swapaxes(mine[:QKV_ROWS].reshape(2, 3, 96, D), 1, 2).reshape(QKV_ROWS, D)
    flat = jnp.concatenate([head, mine[QKV_ROWS:]], axis=0).reshape(-1)[: shard * wide]
    return lax.psum_scatter(flat.astype(F32), "wide", scatter_dimension=0, tiled=True).reshape(1, shard)


def body(hidden_in, out_grad, pair_lengths, params, momentum, average):
    wide, ranks = lax.axis_size("wide"), lax.axis_size("narrow")
    shard = params.shape[1]
    rows, spare, fits = aligned_plan(shard, wide, ranks)
    at_wide, at_narrow = lax.axis_index("wide"), lax.axis_index("narrow")
    if fits:
        place = jnp.stack([at_wide, at_narrow // 2, at_narrow % 2]).astype(jnp.int32)
        block = own_block(place, params, rows, spare, wide)
        own_att, own_ff = gather_blocks(block, at_wide // 2, at_wide % 2, rows)
        got_att = swap_core(own_att)
        got_ff = swap_core(after(own_ff, got_att))
    else:
        place = jnp.zeros((3,), jnp.int32)
        (own_att, own_ff), (got_att, got_ff) = gather_plain(params)
    scalars = jnp.concatenate([pair_lengths[0], place])
    tails = jnp.concatenate([own_att[:, D:], got_att[:, D:]], axis=0)

    qkv, wq, mixed, probs, xp, n1, r1 = attention_forward(scalars, hidden_in, own_att, got_att, tails)
    block_out, own_ffg, got_ffg, grad_one, ga, vec_g, up_g = feed_forward(
        place, n1, r1, out_grad, own_ff, got_ff, tails
    )
    own_attg, got_attg, in_grad = attention_backward(
        place, ga, own_att, got_att, qkv, wq, mixed, probs, xp, vec_g, up_g, grad_one
    )

    device_count = wide * ranks
    rate = 1.0 / (32.0 * math.sqrt(hidden_in.shape[0] * device_count))
    if fits:
        got = swap_core(got_attg), swap_core(got_ffg)
        parts = reduce_windows((own_attg, own_ffg), got, at_wide // 2, at_wide % 2, rows)
        grads, new_params, new_momentum, new_average, low = update_shard(
            place, parts, params, momentum, average, rate, rows, spare, wide
        )
    else:
        grads = scatter_plain(((own_attg, own_ffg), (got_attg, got_ffg)), shard, wide)
        new_momentum = 0.5 * momentum + rate * grads
        new_params = params - (rate * grads + 0.5 * new_momentum)
        new_average = 0.5 * average + 0.5 * new_params
        low = new_params.astype(BF)
    return (
        block_out,
        in_grad,
        grads,
        new_params,
        new_momentum,
        new_average,
        low,
    )


def solution(mesh):
    rows = P(("wide", "narrow"), None)
    flat = P("narrow", "wide")
    return jax.shard_map(
        body,
        mesh=mesh,
        in_specs=(rows, rows, rows, flat, flat, flat),
        out_specs=(rows, rows, flat, flat, flat, flat, flat),
        check_vma=False,
    )
```

```python
import functools
import math

import jax
import jax.numpy as jnp
from jax import lax
from jax.experimental import pallas as pl
from jax.experimental.pallas import tpu as pltpu
from jax.sharding import PartitionSpec as P

D = 768
HEADS = 12
FF = 3072
HD = 64
BUCKETS = 256
L = 512
RANKS = 4
PART = D // RANKS
HPR = HEADS // RANKS
SLOTS = 2
QKV_ROWS = 3 * PART
TILE_ROWS = 8
MAT_ROWS = 3 * D
PAD_ROWS = MAT_ROWS + TILE_ROWS
ATT_ROWS = D + TILE_ROWS
FF_ROWS = 2 * D
BLK = 128
NBLK = L // BLK
NEG = -1000000000.0
VMEM_LIMIT = 60 * 1024 * 1024
BF = jnp.bfloat16
F32 = jnp.float32


def mm(a, b):
    return jnp.dot(a, b, preferred_element_type=F32)


def mm_nt(a, b):
    return lax.dot_general(a, b, (((1,), (1,)), ((), ())), preferred_element_type=F32)


def mm_tn(a, b):
    return lax.dot_general(a, b, (((0,), (0,)), ((), ())), preferred_element_type=F32)


def qkv_pieces():
    for b in range(2):
        for j in range(4):
            for c in range(3):
                t, q = divmod(3 * j + c, 4)
                yield 288 * b + 96 * t, PART * q, PART * j + 96 * b, PART * c


def column_order():
    d = lax.broadcasted_iota(jnp.int32, (D, D), 0)
    n = lax.broadcasted_iota(jnp.int32, (D, D), 1)
    j = (n >= PART).astype(jnp.int32) + (n >= 2 * PART).astype(jnp.int32) + (n >= 3 * PART).astype(jnp.int32)
    return (d == 4 * (n - PART * j) + j).astype(F32).astype(BF)


def slot_of(r, place_ref):
    return ((r // 2) ^ place_ref[1]) + 2 * ((r % 2) ^ place_ref[2])


def slice_of(slot, place_ref):
    return 2 * ((slot % 2) ^ place_ref[1]) + ((slot // 2) ^ place_ref[2])


def vector_rows(tails_ref, place_ref):
    chunks = []
    for r in range(RANKS):
        k = slot_of(r, place_ref)
        chunks.append(tails_ref[k, 2:3, 384:768])
        chunks.append(tails_ref[k, 3:4, 0:384])
        chunks.append(tails_ref[k, 3:4, 384:768])
    return [
        jnp.concatenate([chunks[2 * v], chunks[2 * v + 1]], axis=1).astype(F32) for v in range(6)
    ]


def table_order():
    src = lax.broadcasted_iota(jnp.int32, (D, D), 0)
    dst = lax.broadcasted_iota(jnp.int32, (D, D), 1)
    hh = (dst >= BUCKETS).astype(jnp.int32) + (dst >= 2 * BUCKETS).astype(jnp.int32)
    return (src == 3 * (dst - BUCKETS * hh) + hh).astype(F32).astype(BF)


def normalize(values):
    centred = values - jnp.mean(values, axis=-1, keepdims=True)
    inv = lax.rsqrt(jnp.mean(centred * centred, axis=-1, keepdims=True) + 1e-05)
    return centred * inv, inv


def norm_backward(e, normed, inv):
    return inv * (
        e - jnp.mean(e, axis=-1, keepdims=True) - normed * jnp.mean(e * normed, axis=-1, keepdims=True)
    )


def col_sum(values):
    return jnp.sum(values, axis=0, keepdims=True)


def call(kernel, name, grid, in_specs, out_specs, out_shape, scratch, args, vmem=VMEM_LIMIT, flops=0, moved=0, aliases=None):
    return pl.pallas_call(
        kernel,
        grid_spec=pltpu.PrefetchScalarGridSpec(
            num_scalar_prefetch=1,
            grid=grid,
            in_specs=in_specs,
            out_specs=out_specs,
            scratch_shapes=scratch,
        ),
        out_shape=out_shape,
        input_output_aliases=aliases or {},
        compiler_params=pltpu.CompilerParams(vmem_limit_bytes=vmem),
        cost_estimate=pl.CostEstimate(flops=flops, bytes_accessed=moved, transcendentals=0),
        name=name,
    )(*args)


def whole(*shape):
    return pl.BlockSpec(shape, lambda *_: (0,) * len(shape))


def shaped(dtype, *shape):
    return jax.ShapeDtypeStruct(shape, dtype)


class PlaceView:
    def __init__(self, ref):
        self.ref = ref

    def __getitem__(self, i):
        return self.ref[4 + i]


def block_kernel(rows, lead, shift, place_ref, flat_ref, out_ref, rows_s):
    w = place_ref[4]
    count = flat_ref.shape[1] // 128
    rows_s[0:lead, :] = jnp.zeros((lead, 128), F32)
    rows_s[lead : lead + count, :] = flat_ref[...].reshape(count, 128)
    rows_s[lead + count :, :] = jnp.zeros((rows_s.shape[0] - lead - count, 128), F32)
    start = lead - shift * w
    third = rows // 3

    @pl.when(w < 2)
    def _():
        for t in range(3):
            for c in range(6):
                out_ref[third * t : third * (t + 1), 128 * c : 128 * (c + 1)] = rows_s[
                    pl.ds(start + 6 * t + c, third, stride=18), :
                ].astype(BF)

    @pl.when(w >= 2)
    def _():
        for c in range(6):
            out_ref[0:rows, 128 * c : 128 * (c + 1)] = rows_s[
                pl.ds(start + c, rows, stride=6), :
            ].astype(BF)

    for c in range(6):
        out_ref[rows : rows + TILE_ROWS, 128 * c : 128 * (c + 1)] = rows_s[
            pl.ds(start + 6 * rows + c, TILE_ROWS, stride=6), :
        ].astype(BF)


def own_block(place, params, rows, spare, wide):
    count = params.shape[1] // 128
    lead = spare // 128 * wide
    total = -(-(lead + 6 * (rows + TILE_ROWS)) // 8) * 8
    return call(
        functools.partial(block_kernel, rows, lead, spare // 128),
        "own_block", (1,),
        [whole(*params.shape)],
        whole(rows + TILE_ROWS, D),
        shaped(BF, rows + TILE_ROWS, D),
        [pltpu.VMEM((total, 128), F32)],
        (place, params),
        vmem=16 * 1024 * 1024,
    )


def update_kernel(
    rows, lead, shift, rate, place_ref, kept_ref, near_ref, second_ref, ring_ref, params_ref, momentum_ref, average_ref,
    grads_ref, new_params_ref, new_momentum_ref, new_average_ref, low_ref, rows_s,
):
    w = place_ref[4]
    count = params_ref.shape[1] // 128
    block = (
        kept_ref[...].astype(F32) + near_ref[...].astype(F32) + second_ref[...].astype(F32) + ring_ref[...].astype(F32)
    )
    start = lead - shift * w
    third = rows // 3

    @pl.when(w < 2)
    def _():
        for t in range(3):
            for c in range(6):
                rows_s[pl.ds(start + 6 * t + c, third, stride=18), :] = block[
                    third * t : third * (t + 1), 128 * c : 128 * (c + 1)
                ]

    @pl.when(w >= 2)
    def _():
        for c in range(6):
            rows_s[pl.ds(start + c, rows, stride=6), :] = block[0:rows, 128 * c : 128 * (c + 1)]

    for c in range(6):
        rows_s[pl.ds(start + 6 * rows + c, TILE_ROWS, stride=6), :] = block[
            rows : rows + TILE_ROWS, 128 * c : 128 * (c + 1)
        ]
    grads = rows_s[lead : lead + count, :].reshape(params_ref.shape)
    grads_ref[...] = grads
    params = params_ref[...]
    new_momentum = 0.5 * momentum_ref[...] + rate * grads
    new_params = params - (rate * grads + 0.5 * new_momentum)
    new_momentum_ref[...] = new_momentum
    new_params_ref[...] = new_params
    new_average_ref[...] = 0.5 * average_ref[...] + 0.5 * new_params
    low_ref[...] = new_params.astype(BF)


def update_shard(place, parts, params, momentum, average, rate, rows, spare, wide):
    count = params.shape[1] // 128
    lead = spare // 128 * wide
    total = -(-(lead + 6 * (rows + TILE_ROWS)) // 8) * 8
    kept, near, second, ring = parts
    cap = rows + TILE_ROWS
    flat = whole(*params.shape)
    return call(
        functools.partial(update_kernel, rows, lead, spare // 128, rate),
        "update_shard", (1,),
        [whole(cap, D)] * 4 + [flat] * 3,
        [flat] * 5,
        [shaped(F32, *params.shape)] * 4 + [shaped(BF, *params.shape)],
        [pltpu.VMEM((total, 128), F32)],
        (place, kept, near, second, ring, params, momentum, average),
        vmem=32 * 1024 * 1024,
    )


def merge_kernel(rows, slot, at_ref, *refs):
    pieces, (att_ref, ff_ref, mat, edges, in_sem, out_sem) = refs[:8], refs[-6:]
    copies = []
    for i in range(8):
        w = at_ref[i]
        main = pltpu.make_async_copy(
            pieces[i].at[0:rows], mat.at[pl.ds(pl.multiple_of(rows * w, TILE_ROWS), rows)], in_sem.at[i, 0]
        )
        edge = pltpu.make_async_copy(pieces[i].at[rows : rows + TILE_ROWS], edges.at[w], in_sem.at[i, 1])
        main.start()
        edge.start()
        copies += [main, edge]
    for copy in copies:
        copy.wait()
    for w in range(1, 8):
        at = rows * w
        mat[at : at + TILE_ROWS, :] = mat[at : at + TILE_ROWS, :] + edges[w - 1]
    mat[MAT_ROWS:PAD_ROWS, :] = edges[7]
    outs = [
        pltpu.make_async_copy(src, dst, out_sem.at[n])
        for n, (src, dst) in enumerate(
            (
                (mat.at[0:D], att_ref.at[0:D]),
                (mat.at[MAT_ROWS:PAD_ROWS], att_ref.at[D:ATT_ROWS]),
                (mat.at[D:MAT_ROWS], ff_ref.at[slot]),
            )
        )
    ]
    for copy in outs:
        copy.start()
    for copy in outs:
        copy.wait()


def merge_blocks(at, pieces, rows, slot, ff=()):
    hbm = pl.BlockSpec(memory_space=pl.ANY)
    return call(
        functools.partial(merge_kernel, rows, slot),
        "merge_weights", (1,),
        [hbm] * (8 + len(ff)),
        [hbm] * 2,
        [shaped(BF, ATT_ROWS, D), shaped(BF, SLOTS, FF_ROWS, D)],
        [
            pltpu.VMEM((PAD_ROWS, D), BF),
            pltpu.VMEM((8, TILE_ROWS, D), BF),
            pltpu.SemaphoreType.DMA((8, 2)),
            pltpu.SemaphoreType.DMA((3,)),
        ],
        (at, *pieces, *ff),
        aliases={9: 1} if ff else {},
    )


def window_kernel(rows, windows, at_ref, *refs):
    own_att, own_ff, got_att, got_ff = refs[0:2], refs[2], refs[3:5], refs[5]
    outs, (own_s, got_s, own_sem, got_sem) = refs[6:-4], refs[-4:]
    cap = rows + TILE_ROWS

    def fetch(w, slot, att, ff, buf, sem):
        @pl.when(w < 2)
        def _():
            src = att.at[pl.ds(pl.multiple_of(rows * w, TILE_ROWS), cap)]
            pltpu.make_async_copy(src, buf, sem).start()

        @pl.when(w == 2)
        def _():
            pltpu.make_async_copy(att.at[2 * rows : D], buf.at[0 : D - 2 * rows], sem).start()
            pltpu.make_async_copy(ff.at[slot, 0 : 3 * rows + TILE_ROWS - D], buf.at[D - 2 * rows : cap], sem).start()

        @pl.when((w > 2) & (w < 7))
        def _():
            src = ff.at[slot, pl.ds(pl.multiple_of(rows * w - D, TILE_ROWS), cap)]
            pltpu.make_async_copy(src, buf, sem).start()

        @pl.when(w == 7)
        def _():
            pltpu.make_async_copy(ff.at[slot, 7 * rows - D : FF_ROWS], buf.at[0:rows], sem).start()
            pltpu.make_async_copy(att.at[D:ATT_ROWS], buf.at[rows:cap], sem).start()

    for n, (slot, where) in enumerate(windows):
        w = at_ref[where]
        fetch(w, slot, own_att[slot], own_ff, own_s.at[n], own_sem.at[n])
        fetch(w, slot, got_att[slot], got_ff, got_s.at[n], got_sem.at[n])
    for n in range(len(windows)):
        pltpu.make_async_copy(own_ff.at[0, 0:cap], own_s.at[n], own_sem.at[n]).wait()
        pltpu.make_async_copy(own_ff.at[0, 0:cap], got_s.at[n], got_sem.at[n]).wait()
        outs[n][...] = (own_s[n].astype(F32) + got_s[n].astype(F32)).astype(BF)


def split_windows(at, names, own, got, rows):
    hbm = pl.BlockSpec(memory_space=pl.ANY)
    cap = rows + TILE_ROWS
    n = len(names)
    windows = [(int(name[0] in "YD"), int(name[1]) + 4 * int(name[0] in "XD")) for name in names]
    outs = call(
        functools.partial(window_kernel, rows, windows),
        "split_windows", (1,),
        [hbm] * 6,
        [whole(cap, D)] * n,
        [shaped(BF, cap, D)] * n,
        [
            pltpu.VMEM((n, cap, D), BF),
            pltpu.VMEM((n, cap, D), BF),
            pltpu.SemaphoreType.DMA((n,)),
            pltpu.SemaphoreType.DMA((n,)),
        ],
        (at, *own, *got),
    )
    return dict(zip(names, outs))


def segment_of(pos, len_ref):
    end0 = len_ref[0]
    end1 = end0 + len_ref[1]
    end2 = end1 + len_ref[2]
    return (
        (pos >= end0).astype(jnp.int32)
        + (pos >= end1).astype(jnp.int32)
        + (pos >= end2).astype(jnp.int32)
    )


def att_fwd_kernel(
    scal_ref, x_ref, att0_ref, att1_ref, att2_ref, att3_ref,
    qkv_ref, wq_ref, mixed_ref, probs_ref, xp_ref, n1_ref, r1_ref, tails_ref,
    table_s, acc_s, att_s, main_sem, tail_sem,
):
    s = pl.program_id(0)
    len_ref = scal_ref
    atts = (att0_ref, att1_ref, att2_ref, att3_ref)

    @pl.when(s == 0)
    def _():
        tails = [
            pltpu.make_async_copy(att.at[D:ATT_ROWS], tails_ref.at[k], tail_sem.at[k]) for k, att in enumerate(atts)
        ]
        for copy in tails:
            copy.start()
        for k, att in enumerate(atts):
            pltpu.make_async_copy(att.at[0:D], att_s.at[k], main_sem.at[k]).start()
        for copy in tails:
            copy.wait()
        xp_ref[...] = mm(x_ref[...], column_order()).astype(BF)
        acc_s[...] = jnp.zeros_like(acc_s)
        flat = jnp.concatenate(
            [
                jnp.concatenate([tails_ref[k, 1:2, 384:768], tails_ref[k, 2:3, 0:384]], axis=1).astype(F32)
                for k in range(RANKS)
            ]
            + [jnp.zeros((8 - RANKS, D), F32)],
            axis=0,
        ).astype(BF)
        tables = mm(flat, table_order())
        for k in range(RANKS):
            for h in range(HPR):
                row = tables[k : k + 1, BUCKETS * h : BUCKETS * (h + 1)]
                table_s[k, h : h + 1, :] = jnp.concatenate(
                    [
                        row,
                        jnp.broadcast_to(row[:, 255:256], (1, BLK)),
                        jnp.broadcast_to(row[:, 0:1], (1, BLK)),
                    ],
                    axis=1,
                )

    pltpu.make_async_copy(att0_ref.at[0:D], att_s.at[s], main_sem.at[s]).wait()
    for src_row, src_col, dst_row, dst_col in qkv_pieces():
        wq_ref[0, dst_row : dst_row + 96, dst_col : dst_col + PART] = att_s[
            s, src_row : src_row + 96, src_col : src_col + PART
        ]

    first = tails_ref[s, 0:1, :]
    bias = jnp.concatenate(
        [first[:, 0:PART], jnp.zeros((1, PART), BF), first[:, PART : 2 * PART]], axis=1
    ).astype(F32)
    qkv = (mm(xp_ref[...], wq_ref[0]) + bias).astype(BF)
    qkv_ref[0] = qkv

    seg_j = segment_of(lax.broadcasted_iota(jnp.int32, (1, L), 1), len_ref)
    table = table_s[s]
    heads = []
    for h in range(HPR):
        q = qkv[:, HD * h : HD * (h + 1)]
        k = qkv[:, PART + HD * h : PART + HD * (h + 1)]
        v = qkv[:, 2 * PART + HD * h : 2 * PART + HD * (h + 1)]
        row = table[h : h + 1, :]
        near = pltpu.roll(jnp.broadcast_to(row, (BLK, 4 * BLK)), 0, 1, stride=1, stride_axis=0)
        far_right = jnp.broadcast_to(row[:, 255:256], (BLK, BLK))
        far_left = jnp.broadcast_to(row[:, 511:512], (BLK, BLK))
        for i in range(NBLK):
            seg_i = segment_of(
                lax.broadcasted_iota(jnp.int32, (BLK, 1), 0) + BLK * i, len_ref
            )
            parts = []
            for jb in range(NBLK):
                delta = jb - i
                if abs(delta) <= 1:
                    parts.append(near[:, BLK * (delta + 1) : BLK * (delta + 2)])
                else:
                    parts.append(far_right if delta > 0 else far_left)
            logits = mm_nt(q[BLK * i : BLK * (i + 1)], k) * 0.125 + jnp.concatenate(parts, axis=1)
            logits = jnp.where(seg_i == seg_j, logits, NEG)
            top = jnp.max(logits, axis=-1, keepdims=True)
            expo = jnp.exp(logits - top)
            total = jnp.sum(expo, axis=-1, keepdims=True)
            probs_ref[0, h, BLK * i : BLK * (i + 1), :] = (expo * (1.0 / total)).astype(BF)
        heads.append(mm(probs_ref[0, h], v))
    mixed = jnp.concatenate(heads, axis=1).astype(BF)
    mixed_ref[0] = mixed
    acc_s[...] += mm(mixed, att_s[s, QKV_ROWS:D, :])

    @pl.when(s == RANKS - 1)
    def _():
        vec = vector_rows(tails_ref, PlaceView(scal_ref))
        normed, inv = normalize(x_ref[...].astype(F32) + acc_s[...] + vec[0])
        n1_ref[...] = normed
        r1_ref[...] = jnp.broadcast_to(inv, (L, BLK))


def attention_forward(scalars, x, atts):
    per = lambda *shape: pl.BlockSpec((1, *shape), lambda s, n: (s,) + (0,) * len(shape))
    return call(
        att_fwd_kernel,
        "attention_forward", (RANKS,),
        [whole(L, D)] + [pl.BlockSpec(memory_space=pl.ANY)] * RANKS,
        [
            per(L, QKV_ROWS), per(D, QKV_ROWS), per(L, PART), per(HPR, L, L),
            whole(L, D), whole(L, D), whole(L, BLK), whole(RANKS, TILE_ROWS, D),
        ],
        [
            shaped(BF, RANKS, L, QKV_ROWS),
            shaped(BF, RANKS, D, QKV_ROWS),
            shaped(BF, RANKS, L, PART),
            shaped(BF, RANKS, HPR, L, L),
            shaped(BF, L, D),
            shaped(F32, L, D),
            shaped(F32, L, BLK),
            shaped(BF, RANKS, TILE_ROWS, D),
        ],
        [
            pltpu.VMEM((RANKS, 8, 512), F32),
            pltpu.VMEM((L, D), F32),
            pltpu.VMEM((RANKS, D, D), BF),
            pltpu.SemaphoreType.DMA((RANKS,)),
            pltpu.SemaphoreType.DMA((RANKS,)),
        ],
        (scalars, x, *atts),
        flops=6_000_000_000, moved=24_000_000,
    )


def ffn_kernel(
    place_ref, n1_ref, r1_ref, og_ref, up0_ref, down0_ref, up1_ref, down1_ref, tails_ref,
    block_ref, grad0_ref, grad1_ref, grad_one_ref, ga_ref, vec_ref, bup_ref,
    fn_s, fl_s, slope_s, act_s, down_s, gd_s, gf_s,
):
    step = pl.program_id(0)
    inv_root2 = 1.0 / math.sqrt(2.0)

    @pl.when(step == 0)
    def _():
        vec = vector_rows(tails_ref, PlaceView(place_ref))
        first = n1_ref[...] * vec[2] + vec[3]
        fn_s[...] = first
        fl_s[...] = first.astype(BF)
        down_s[...] = jnp.zeros_like(down_s)

    def forward(slot, up_ref, down_ref):
        bias = jnp.concatenate([tails_ref[slot, 0:1, 384:768], tails_ref[slot, 1:2, 0:384]], axis=1)
        up = mm(fl_s[...], up_ref[0]) + bias.astype(F32)
        half = 0.5 * (1.0 + lax.erf(up * inv_root2))
        act = (up * half).astype(BF)
        slope_s[slot] = half + up * jnp.exp(-0.5 * up * up) * (1.0 / math.sqrt(2.0 * math.pi))
        act_s[slot] = act
        down_s[...] += mm(act, down_ref[0])

    @pl.when(step < 2)
    def _():
        forward(step, up0_ref, down0_ref)

    @pl.when((step == 2) | (step == 3))
    def _():
        forward(step, up1_ref, down1_ref)

    @pl.when(step == RANKS)
    def _():
        vec = vector_rows(tails_ref, PlaceView(place_ref))
        normed, inv = normalize(fn_s[...] + down_s[...] + vec[1])
        block_ref[...] = (normed * vec[4] + vec[5]).astype(BF)
        og = og_ref[...].astype(F32)
        vec_ref[4:5, :] = col_sum(og * normed)
        vec_ref[5:6, :] = col_sum(og)
        grad_two = norm_backward(og * vec[4], normed, inv)
        low = grad_two.astype(BF)
        gd_s[...] = low
        vec_ref[1:2, :] = col_sum(low.astype(F32))
        vec_ref[6:8, :] = jnp.zeros((2, D), F32)
        gf_s[...] = grad_two

    def backward(slot, up_ref, down_ref, grad_ref):
        gd = gd_s[...]
        grad_ref[0, D:FF_ROWS, :] = mm_tn(act_s[slot], gd).astype(BF)
        gu = (mm_nt(gd, down_ref[0]) * slope_s[slot]).astype(BF)
        bup_ref[0, 0:1, :] = col_sum(gu.astype(F32))
        bup_ref[0, 1:8, :] = jnp.zeros((7, D), F32)
        grad_ref[0, 0:D, :] = mm_tn(fl_s[...], gu).astype(BF)
        gf_s[...] += mm_nt(gu, up_ref[0])

    @pl.when((step == 4) | (step == 5))
    def _():
        backward(step - 2, up1_ref, down1_ref, grad1_ref)

    @pl.when(step >= 6)
    def _():
        backward(step - 6, up0_ref, down0_ref, grad0_ref)

    @pl.when(step == 2 * RANKS - 1)
    def _():
        vec = vector_rows(tails_ref, PlaceView(place_ref))
        f = gf_s[...]
        normed = n1_ref[...]
        vec_ref[2:3, :] = col_sum(f * normed)
        vec_ref[3:4, :] = col_sum(f)
        grad_one = norm_backward(f * vec[2], normed, r1_ref[:, 0:1])
        grad_one_ref[...] = grad_one
        low = grad_one.astype(BF)
        ga_ref[...] = low
        vec_ref[0:1, :] = col_sum(low.astype(F32))


def feed_forward(place, n1, r1, out_grad, own_ff, got_ff, tails):
    def own_at(half):
        return lambda s, n: ((((s >= 1) & (s <= 3)) | (s == 7)).astype(jnp.int32), half, 0)

    def got_at(half):
        return lambda s, n: (((s == 3) | (s >= 5)).astype(jnp.int32), half, 0)

    wt = lambda index: pl.BlockSpec((1, D, D), index)
    return call(
        ffn_kernel,
        "feed_forward", (2 * RANKS,),
        [
            whole(L, D), whole(L, BLK), whole(L, D),
            wt(own_at(0)), wt(own_at(1)), wt(got_at(0)), wt(got_at(1)),
            whole(RANKS, TILE_ROWS, D),
        ],
        [
            whole(L, D),
            pl.BlockSpec((1, FF_ROWS, D), lambda s, n: ((s >= 7).astype(jnp.int32), 0, 0)),
            pl.BlockSpec((1, FF_ROWS, D), lambda s, n: ((s >= 5).astype(jnp.int32), 0, 0)),
            whole(L, D), whole(L, D), whole(8, D),
            pl.BlockSpec((1, 8, D), lambda s, n: (lax.rem(jnp.maximum(s, 4) - 2, 4), 0, 0)),
        ],
        [
            shaped(BF, L, D),
            shaped(BF, SLOTS, FF_ROWS, D),
            shaped(BF, SLOTS, FF_ROWS, D),
            shaped(F32, L, D),
            shaped(BF, L, D),
            shaped(F32, 8, D),
            shaped(F32, RANKS, 8, D),
        ],
        [
            pltpu.VMEM((L, D), F32),
            pltpu.VMEM((L, D), BF),
            pltpu.VMEM((RANKS, L, D), F32),
            pltpu.VMEM((RANKS, L, D), BF),
            pltpu.VMEM((L, D), F32),
            pltpu.VMEM((L, D), BF),
            pltpu.VMEM((L, D), F32),
        ],
        (place, n1, r1, out_grad, own_ff, own_ff, got_ff, got_ff, tails),
        flops=14_500_000_000, moved=36_000_000,
    )


def diagonal_sums(block):
    half = block.shape[0] // 2
    while half >= 8:
        block = block[:half] + pltpu.roll(block[half:], 4 * BLK - half, 1)
        half //= 2
    row = lax.broadcasted_iota(jnp.int32, (8, 1), 0)
    for bit in (4, 2, 1):
        block = jnp.where((row & bit) > 0, pltpu.roll(block, 4 * BLK - bit, 1), block)
    return col_sum(block)


def att_bwd_kernel(
    place_ref, ga_ref, att0_ref, att1_ref, att2_ref, att3_ref,
    qkv_ref, probs_ref, mixed_ref, wq_ref, xp_ref, vec_ref, bup_ref, grad_one_ref,
    da0_ref, da1_ref, da2_ref, da3_ref, in_grad_ref,
    ds_s, near_s, sums_s, dx_s, order_s, wo_s, das_s, sem, out_sem,
):
    s = pl.program_id(0)
    slot = RANKS - 1 - s
    da_s = das_s.at[lax.rem(s, 2)]

    def leave(k):
        da_ref = (da0_ref, da1_ref, da2_ref, da3_ref)[k]
        return pltpu.make_async_copy(das_s.at[(RANKS - 1 - k) % 2], da_ref, out_sem.at[k])

    for k in range(2):

        @pl.when(slot == k)
        def _(k=k):
            leave(k + 2).wait()

    @pl.when(s == 0)
    def _():
        for k, att in enumerate((att0_ref, att1_ref, att2_ref, att3_ref)):
            pltpu.make_async_copy(att.at[QKV_ROWS:D], wo_s.at[k], sem.at[k]).start()
        order_s[...] = table_order()
        dx_s[...] = jnp.zeros_like(dx_s)
        sums_s[...] = jnp.zeros_like(sums_s)

    ga = ga_ref[...]
    da_s[QKV_ROWS:D, :] = mm_tn(mixed_ref[0], ga).astype(BF)
    pltpu.make_async_copy(att0_ref.at[QKV_ROWS:D], wo_s.at[slot], sem.at[slot]).wait()
    dm_all = mm_nt(ga, wo_s[slot]).astype(BF)
    qkv = qkv_ref[0]
    dq, dk, dv = [], [], []
    for h in range(HPR):
        q = qkv[:, HD * h : HD * (h + 1)]
        k = qkv[:, PART + HD * h : PART + HD * (h + 1)]
        v = qkv[:, 2 * PART + HD * h : 2 * PART + HD * (h + 1)]
        dm = dm_all[:, HD * h : HD * (h + 1)]
        far_left = jnp.zeros((BLK, BLK), F32)
        far_right = jnp.zeros((BLK, BLK), F32)
        for i in range(NBLK):
            rows = slice(BLK * i, BLK * (i + 1))
            p = probs_ref[0, h, rows, :].astype(F32)
            dp = mm_nt(dm[rows], v)
            ds = (p * (dp - jnp.sum(p * dp, axis=-1, keepdims=True))).astype(BF)
            ds_s[rows, :] = ds
            ds = ds.astype(F32)
            for jb in range(NBLK):
                piece = ds[:, BLK * jb : BLK * (jb + 1)]
                delta = jb - i
                if abs(delta) <= 1:
                    cols = slice(BLK * (delta + 1), BLK * (delta + 2))
                    if i == max(0, -delta):
                        near_s[:, cols] = piece
                    else:
                        near_s[:, cols] += piece
                elif delta > 0:
                    far_right += piece
                else:
                    far_left += piece
        near_s[:, 3 * BLK :] = jnp.zeros((BLK, BLK), F32)
        sums_s[h : h + 1, 0 : 4 * BLK] = diagonal_sums(near_s[...])
        sums_s[h : h + 1, 4 * BLK : 5 * BLK] = col_sum(far_left)
        sums_s[h : h + 1, 5 * BLK : 6 * BLK] = col_sum(far_right)
        dscore = ds_s[...]
        dq.append(mm(dscore, k) * 0.125)
        dk.append(mm_tn(dscore, q) * 0.125)
        dv.append(mm_tn(probs_ref[0, h], dm))
    dqkv = jnp.concatenate(dq + dk + dv, axis=1).astype(BF)

    qv = col_sum(dqkv.astype(F32))
    sums = sums_s[...]
    lane = lax.broadcasted_iota(jnp.int32, (1, 6 * BLK), 1)
    is_left = (lane == 0) | ((lane >= 3 * BLK) & (lane < 5 * BLK))
    is_right = ((lane >= BUCKETS - 1) & (lane < 3 * BLK)) | (lane >= 5 * BLK)
    left = jnp.sum(jnp.where(is_left, sums, 0.0), axis=-1, keepdims=True)
    right = jnp.sum(jnp.where(is_right, sums, 0.0), axis=-1, keepdims=True)
    sums = jnp.where(lane == 0, left, jnp.where(lane == BUCKETS - 1, right, sums))
    table = jnp.concatenate([sums[h : h + 1, :BUCKETS] for h in range(HPR)], axis=1)
    table = jnp.broadcast_to(table, (8, D)).astype(BF)
    table = mm_nt(table, order_s[...])[0:1]
    r = slice_of(slot, PlaceView(place_ref))
    vecs = []
    for i in range(3):
        m = 3 * r + i
        row = vec_ref[pl.ds(m // 2, 1), :]
        vecs.append(jnp.where(m % 2 == 0, row[:, 0:384], row[:, 384:768]))
    bup = bup_ref[0, 0:1, :]
    tail = jnp.concatenate(
        [
            jnp.concatenate([qv[:, 0:PART], qv[:, 2 * PART :], bup[:, 0:384]], axis=1),
            jnp.concatenate([bup[:, 384:768], table[:, 0:384]], axis=1),
            jnp.concatenate([table[:, 384:768], vecs[0]], axis=1),
            jnp.concatenate([vecs[1], vecs[2]], axis=1),
            jnp.zeros((TILE_ROWS - 4, D), F32),
        ],
        axis=0,
    )
    da_s[D:ATT_ROWS, :] = tail.astype(BF)

    dw = mm_tn(xp_ref[...], dqkv).astype(BF)
    for src_row, src_col, dst_row, dst_col in qkv_pieces():
        da_s[src_row : src_row + 96, src_col : src_col + PART] = dw[
            dst_row : dst_row + 96, dst_col : dst_col + PART
        ]
    dx_s[...] += mm_nt(dqkv, wq_ref[0])

    for k in range(RANKS):

        @pl.when(slot == k)
        def _(k=k):
            leave(k).start()

    @pl.when(s == RANKS - 1)
    def _():
        in_grad_ref[...] = grad_one_ref[...] + mm_nt(dx_s[...].astype(BF), column_order())
        for k in range(2):
            leave(k).wait()


def attention_backward(scalars, ga, atts, qkv, wq, mixed, probs, xp, vec_g, up_g, grad_one):
    per = lambda *shape: pl.BlockSpec((1, *shape), lambda s, n: (RANKS - 1 - s,) + (0,) * len(shape))
    return call(
        att_bwd_kernel,
        "attention_backward", (RANKS,),
        [whole(L, D)]
        + [pl.BlockSpec(memory_space=pl.ANY)] * RANKS
        + [
            per(L, QKV_ROWS), per(HPR, L, L), per(L, PART), per(D, QKV_ROWS),
            whole(L, D), whole(8, D), per(8, D), whole(L, D),
        ],
        [pl.BlockSpec(memory_space=pl.ANY)] * RANKS + [whole(L, D)],
        [shaped(BF, ATT_ROWS, D)] * RANKS + [shaped(F32, L, D)],
        [
            pltpu.VMEM((L, L), BF),
            pltpu.VMEM((BLK, 4 * BLK), F32),
            pltpu.VMEM((8, 6 * BLK), F32),
            pltpu.VMEM((L, D), F32),
            pltpu.VMEM((D, D), BF),
            pltpu.VMEM((RANKS, PART, D), BF),
            pltpu.VMEM((2, ATT_ROWS, D), BF),
            pltpu.SemaphoreType.DMA((RANKS,)),
            pltpu.SemaphoreType.DMA((RANKS,)),
        ],
        (scalars, ga, *atts, qkv, probs, mixed, wq, xp, vec_g, up_g, grad_one),
        flops=12_000_000_000, moved=30_000_000,
    )


X_SWAP = [(w, w ^ 1) for w in range(8)]
Z_RING = [(w, (w + 2) % 8) for w in range(8)]
Y_SWAP = [(n, n ^ 2) for n in range(4)]
CORE_SWAP = [(n, n ^ 1) for n in range(4)]


def swap_x(a):
    return lax.ppermute(a, "wide", X_SWAP)


def swap_y(a):
    return lax.ppermute(a, "narrow", Y_SWAP)


def ring_z(a):
    return lax.ppermute(a, "wide", Z_RING)


def ring_back(a):
    return lax.ppermute(a, "wide", [(j, i) for i, j in Z_RING])


def swap_core(a):
    return lax.ppermute(a, "narrow", CORE_SWAP)


def after(value, earlier):
    return lax.optimization_barrier((value, earlier))[0]


def aligned_plan(shard, wide, ranks):
    unit = TILE_ROWS * D
    tiles, spare = divmod(shard, unit)
    rows = tiles * TILE_ROWS
    fits = (
        wide == 8
        and ranks == RANKS
        and spare * wide <= unit
        and spare % 128 == 0
        and rows * wide == MAT_ROWS
        and rows == QKV_ROWS // 2
    )
    return rows, spare, fits


def window_places(z, x):
    planes = jnp.mod(z - jnp.arange(4, dtype=jnp.int32), 4)
    return jnp.concatenate([2 * planes + x, 2 * planes + 1 - x])


def gather_blocks(r0, z, x, rows):
    r1, x0, y0 = ring_z(r0), swap_x(r0), swap_y(r0)
    d0 = swap_y(after(x0, y0))
    r2, x1, y1 = ring_z(r1), swap_x(after(r1, x0)), swap_y(after(r1, y0))
    r3, x2, y2 = ring_z(r2), swap_x(after(r2, x0)), swap_y(after(r2, d0))
    d1 = ring_z(after(d0, y1))
    x3 = swap_x(after(r3, x1))
    y3, d2, d3 = ring_z(after(y2, r3)), swap_x(after(y2, x2)), swap_y(after(x3, y1))
    at = window_places(z, x)
    near_att, ff = merge_blocks(at, (r0, r1, r2, r3, x0, x1, x2, x3), rows, 0)
    near_got = swap_core(near_att)
    far_att, ff = merge_blocks(at, (y0, y1, y2, y3, d0, d1, d2, d3), rows, 1, (ff,))
    far_got = swap_core(far_att)
    return ((near_att, far_att), ff), ((near_got, far_got), swap_core(after(ff, (near_got, far_got))))


def add_low(*terms):
    total = terms[0].astype(F32)
    for term in terms[1:]:
        total = total + term.astype(F32)
    return total.astype(BF)


def reduce_windows(own_att, got_att, own_ff, got_ff, z, x, rows):
    at = window_places(z, x)
    far_got = swap_core(got_att[1])
    near_got = swap_core(after(got_att[0], far_got))
    far = (own_att[1], own_att[1], own_ff), (far_got, far_got, got_ff)
    a = split_windows(at, ("D3", "Y3", "D2", "D1"), *far, rows)
    y1, z1, x1 = swap_y(a["D3"]), ring_back(a["Y3"]), swap_x(a["D2"])
    both = (*own_att, own_ff), (near_got, far_got, got_ff)
    a |= split_windows(
        at, ("X3", "Y2", "Y1", "R3", "X2", "R2", "X1", "R1", "D0", "X0", "Y0", "R0"), *both, rows
    )
    z2 = ring_back(after(a["D1"], x1))
    y3 = swap_y(after(a["Y1"], x1))
    far = add_low(a["X3"], y1)
    x2 = swap_x(far)
    y2 = swap_y(add_low(a["Y2"], z1, x1))
    x3 = swap_x(after(a["X2"], x2))
    z3 = ring_back(add_low(a["R3"], x2))
    x4 = swap_x(after(a["X1"], x3))
    y4 = swap_y(add_low(a["D0"], z2))
    z4 = ring_back(add_low(a["R2"], y2, z3, x3))
    y5 = swap_y(after(a["Y0"], y2))
    z5 = ring_back(add_low(a["R1"], y3, z4, x4))
    x5 = swap_x(add_low(a["X0"], y4))
    return a["R0"], z5, x5, y5


def gather_plain(params):
    flat = lax.all_gather(params.astype(BF)[0], "wide", axis=0, tiled=True)
    flat = jnp.pad(flat, (0, PAD_ROWS * D - flat.shape[0])).reshape(PAD_ROWS, D)
    head = jnp.swapaxes(flat[:QKV_ROWS].reshape(2, 96, 3, D), 1, 2).reshape(QKV_ROWS, D)
    flat = jnp.concatenate([head, flat[QKV_ROWS:]], axis=0)
    mats = lax.all_gather(flat, "narrow", axis=0, tiled=True).reshape(2, 2, PAD_ROWS, D)
    pairs = []
    for core in range(2):
        pair = mats[:, core]
        pairs.append((jnp.concatenate([pair[:, :D], pair[:, MAT_ROWS:]], axis=1), pair[:, D:MAT_ROWS]))
    return pairs


def scatter_plain(pairs, shard, wide):
    mats = [jnp.concatenate([att[:, :D], ff, att[:, D:]], axis=1) for att, ff in pairs]
    grads = jnp.stack(mats, axis=1).reshape(-1, D)
    mine = lax.psum_scatter(grads, "narrow", scatter_dimension=0, tiled=True)
    head = jnp.swapaxes(mine[:QKV_ROWS].reshape(2, 3, 96, D), 1, 2).reshape(QKV_ROWS, D)
    flat = jnp.concatenate([head, mine[QKV_ROWS:]], axis=0).reshape(-1)[: shard * wide]
    return lax.psum_scatter(flat.astype(F32), "wide", scatter_dimension=0, tiled=True).reshape(1, shard)


def body(hidden_in, out_grad, pair_lengths, params, momentum, average):
    wide, ranks = lax.axis_size("wide"), lax.axis_size("narrow")
    shard = params.shape[1]
    rows, spare, fits = aligned_plan(shard, wide, ranks)
    at_wide, at_narrow = lax.axis_index("wide"), lax.axis_index("narrow")
    if fits:
        place = jnp.stack([at_wide, at_narrow // 2, at_narrow % 2]).astype(jnp.int32)
        scalars = jnp.concatenate([pair_lengths[0], place])
        block = own_block(scalars, params, rows, spare, wide)
        (own_att, own_ff), (got_att, got_ff) = gather_blocks(block, at_wide // 2, at_wide % 2, rows)
    else:
        scalars = jnp.concatenate([pair_lengths[0], jnp.zeros((3,), jnp.int32)])
        (own_att, own_ff), (got_att, got_ff) = gather_plain(params)
    atts = (own_att[0], own_att[1], got_att[0], got_att[1])

    qkv, wq, mixed, probs, xp, n1, r1, tails = attention_forward(scalars, hidden_in, atts)
    block_out, own_ffg, got_ffg, grad_one, ga, vec_g, up_g = feed_forward(
        scalars, n1, r1, out_grad, own_ff, got_ff, tails
    )
    *attg, in_grad = attention_backward(scalars, ga, atts, qkv, wq, mixed, probs, xp, vec_g, up_g, grad_one)
    own_attg, got_attg = attg[:2], attg[2:]

    device_count = wide * ranks
    rate = 1.0 / (32.0 * math.sqrt(hidden_in.shape[0] * device_count))
    if fits:
        parts = reduce_windows(own_attg, got_attg, own_ffg, swap_core(got_ffg), at_wide // 2, at_wide % 2, rows)
        grads, new_params, new_momentum, new_average, low = update_shard(
            scalars, parts, params, momentum, average, rate, rows, spare, wide
        )
    else:
        grads = scatter_plain(((jnp.stack(own_attg), own_ffg), (jnp.stack(got_attg), got_ffg)), shard, wide)
        new_momentum = 0.5 * momentum + rate * grads
        new_params = params - (rate * grads + 0.5 * new_momentum)
        new_average = 0.5 * average + 0.5 * new_params
        low = new_params.astype(BF)
    return (
        block_out,
        in_grad,
        grads,
        new_params,
        new_momentum,
        new_average,
        low,
    )


def solution(mesh):
    rows = P(("wide", "narrow"), None)
    flat = P("narrow", "wide")
    return jax.shard_map(
        body,
        mesh=mesh,
        in_specs=(rows, rows, rows, flat, flat, flat),
        out_specs=(rows, rows, flat, flat, flat, flat, flat),
        check_vma=False,
    )
```

```python
import functools
import math

import jax
import jax.numpy as jnp
from jax import lax
from jax.experimental import pallas as pl
from jax.experimental.pallas import tpu as pltpu
from jax.sharding import PartitionSpec as P

D = 768
HEADS = 12
FF = 3072
HD = 64
BUCKETS = 256
L = 512
RANKS = 4
PART = D // RANKS
HPR = HEADS // RANKS
SLOTS = 2
QKV_ROWS = 3 * PART
TILE_ROWS = 8
MAT_ROWS = 3 * D
PAD_ROWS = MAT_ROWS + TILE_ROWS
ATT_ROWS = D + TILE_ROWS
FF_ROWS = 2 * D
BLK = 128
NBLK = L // BLK
NEG = -1000000000.0
VMEM_LIMIT = 60 * 1024 * 1024
BF = jnp.bfloat16
F32 = jnp.float32


def mm(a, b):
    return jnp.dot(a, b, preferred_element_type=F32)


def mm_nt(a, b):
    return lax.dot_general(a, b, (((1,), (1,)), ((), ())), preferred_element_type=F32)


def mm_tn(a, b):
    return lax.dot_general(a, b, (((0,), (0,)), ((), ())), preferred_element_type=F32)


def qkv_pieces():
    for b in range(2):
        for j in range(4):
            for c in range(3):
                t, q = divmod(3 * j + c, 4)
                yield 288 * b + 96 * t, PART * q, PART * j + 96 * b, PART * c


def column_order():
    d = lax.broadcasted_iota(jnp.int32, (D, D), 0)
    n = lax.broadcasted_iota(jnp.int32, (D, D), 1)
    j = (n >= PART).astype(jnp.int32) + (n >= 2 * PART).astype(jnp.int32) + (n >= 3 * PART).astype(jnp.int32)
    return (d == 4 * (n - PART * j) + j).astype(F32).astype(BF)


def slot_of(r, place_ref):
    return ((r // 2) ^ place_ref[1]) + 2 * ((r % 2) ^ place_ref[2])


def slice_of(slot, place_ref):
    return 2 * ((slot % 2) ^ place_ref[1]) + ((slot // 2) ^ place_ref[2])


def vector_rows(tails_ref, place_ref):
    chunks = []
    for r in range(RANKS):
        k = slot_of(r, place_ref)
        chunks.append(tails_ref[k, 2:3, 384:768])
        chunks.append(tails_ref[k, 3:4, 0:384])
        chunks.append(tails_ref[k, 3:4, 384:768])
    return [
        jnp.concatenate([chunks[2 * v], chunks[2 * v + 1]], axis=1).astype(F32) for v in range(6)
    ]


def table_order():
    src = lax.broadcasted_iota(jnp.int32, (D, D), 0)
    dst = lax.broadcasted_iota(jnp.int32, (D, D), 1)
    hh = (dst >= BUCKETS).astype(jnp.int32) + (dst >= 2 * BUCKETS).astype(jnp.int32)
    return (src == 3 * (dst - BUCKETS * hh) + hh).astype(F32).astype(BF)


def normalize(values):
    centred = values - jnp.mean(values, axis=-1, keepdims=True)
    inv = lax.rsqrt(jnp.mean(centred * centred, axis=-1, keepdims=True) + 1e-05)
    return centred * inv, inv


def norm_backward(e, normed, inv):
    return inv * (
        e - jnp.mean(e, axis=-1, keepdims=True) - normed * jnp.mean(e * normed, axis=-1, keepdims=True)
    )


def col_sum(values):
    return jnp.sum(values, axis=0, keepdims=True)


def call(kernel, name, grid, in_specs, out_specs, out_shape, scratch, args, vmem=VMEM_LIMIT, flops=0, moved=0, aliases=None):
    return pl.pallas_call(
        kernel,
        grid_spec=pltpu.PrefetchScalarGridSpec(
            num_scalar_prefetch=1,
            grid=grid,
            in_specs=in_specs,
            out_specs=out_specs,
            scratch_shapes=scratch,
        ),
        out_shape=out_shape,
        input_output_aliases=aliases or {},
        compiler_params=pltpu.CompilerParams(vmem_limit_bytes=vmem),
        cost_estimate=pl.CostEstimate(flops=flops, bytes_accessed=moved, transcendentals=0),
        name=name,
    )(*args)


def whole(*shape):
    return pl.BlockSpec(shape, lambda *_: (0,) * len(shape))


def shaped(dtype, *shape):
    return jax.ShapeDtypeStruct(shape, dtype)


class PlaceView:
    def __init__(self, ref):
        self.ref = ref

    def __getitem__(self, i):
        return self.ref[4 + i]


def block_kernel(rows, lead, shift, place_ref, flat_ref, out_ref, rows_s):
    w = place_ref[4]
    count = flat_ref.shape[1] // 128
    rows_s[0:lead, :] = jnp.zeros((lead, 128), F32)
    rows_s[lead : lead + count, :] = flat_ref[...].reshape(count, 128)
    rows_s[lead + count :, :] = jnp.zeros((rows_s.shape[0] - lead - count, 128), F32)
    start = lead - shift * w
    third = rows // 3

    @pl.when(w < 2)
    def _():
        for t in range(3):
            for c in range(6):
                out_ref[third * t : third * (t + 1), 128 * c : 128 * (c + 1)] = rows_s[
                    pl.ds(start + 6 * t + c, third, stride=18), :
                ].astype(BF)

    @pl.when(w >= 2)
    def _():
        for c in range(6):
            out_ref[0:rows, 128 * c : 128 * (c + 1)] = rows_s[
                pl.ds(start + c, rows, stride=6), :
            ].astype(BF)

    for c in range(6):
        out_ref[rows : rows + TILE_ROWS, 128 * c : 128 * (c + 1)] = rows_s[
            pl.ds(start + 6 * rows + c, TILE_ROWS, stride=6), :
        ].astype(BF)


def own_block(place, params, rows, spare, wide):
    count = params.shape[1] // 128
    lead = spare // 128 * wide
    total = -(-(lead + 6 * (rows + TILE_ROWS)) // 8) * 8
    return call(
        functools.partial(block_kernel, rows, lead, spare // 128),
        "own_block", (1,),
        [whole(*params.shape)],
        whole(rows + TILE_ROWS, D),
        shaped(BF, rows + TILE_ROWS, D),
        [pltpu.VMEM((total, 128), F32)],
        (place, params),
        vmem=16 * 1024 * 1024,
    )


def update_kernel(
    rows, lead, shift, rate, place_ref, kept_ref, near_ref, second_ref, ring_ref, params_ref, momentum_ref, average_ref,
    grads_ref, new_params_ref, new_momentum_ref, new_average_ref, low_ref, rows_s,
):
    w = place_ref[4]
    count = params_ref.shape[1] // 128
    block = (
        kept_ref[...].astype(F32) + near_ref[...].astype(F32) + second_ref[...].astype(F32) + ring_ref[...].astype(F32)
    )
    start = lead - shift * w
    third = rows // 3

    @pl.when(w < 2)
    def _():
        for t in range(3):
            for c in range(6):
                rows_s[pl.ds(start + 6 * t + c, third, stride=18), :] = block[
                    third * t : third * (t + 1), 128 * c : 128 * (c + 1)
                ]

    @pl.when(w >= 2)
    def _():
        for c in range(6):
            rows_s[pl.ds(start + c, rows, stride=6), :] = block[0:rows, 128 * c : 128 * (c + 1)]

    for c in range(6):
        rows_s[pl.ds(start + 6 * rows + c, TILE_ROWS, stride=6), :] = block[
            rows : rows + TILE_ROWS, 128 * c : 128 * (c + 1)
        ]
    grads = rows_s[lead : lead + count, :].reshape(params_ref.shape)
    grads_ref[...] = grads
    params = params_ref[...]
    new_momentum = 0.5 * momentum_ref[...] + rate * grads
    new_params = params - (rate * grads + 0.5 * new_momentum)
    new_momentum_ref[...] = new_momentum
    new_params_ref[...] = new_params
    new_average_ref[...] = 0.5 * average_ref[...] + 0.5 * new_params
    low_ref[...] = new_params.astype(BF)


def update_shard(place, parts, params, momentum, average, rate, rows, spare, wide):
    count = params.shape[1] // 128
    lead = spare // 128 * wide
    total = -(-(lead + 6 * (rows + TILE_ROWS)) // 8) * 8
    kept, near, second, ring = parts
    cap = rows + TILE_ROWS
    flat = whole(*params.shape)
    return call(
        functools.partial(update_kernel, rows, lead, spare // 128, rate),
        "update_shard", (1,),
        [whole(cap, D)] * 4 + [flat] * 3,
        [flat] * 5,
        [shaped(F32, *params.shape)] * 4 + [shaped(BF, *params.shape)],
        [pltpu.VMEM((total, 128), F32)],
        (place, kept, near, second, ring, params, momentum, average),
        vmem=32 * 1024 * 1024,
    )


def merge_kernel(rows, slot, at_ref, *refs):
    pieces, (att_ref, ff_ref, mat, edges, in_sem, out_sem) = refs[:8], refs[-6:]
    copies = []
    for i in range(8):
        w = at_ref[i]
        main = pltpu.make_async_copy(
            pieces[i].at[0:rows], mat.at[pl.ds(pl.multiple_of(rows * w, TILE_ROWS), rows)], in_sem.at[i, 0]
        )
        edge = pltpu.make_async_copy(pieces[i].at[rows : rows + TILE_ROWS], edges.at[w], in_sem.at[i, 1])
        main.start()
        edge.start()
        copies += [main, edge]
    for copy in copies:
        copy.wait()
    for w in range(1, 8):
        at = rows * w
        mat[at : at + TILE_ROWS, :] = mat[at : at + TILE_ROWS, :] + edges[w - 1]
    mat[MAT_ROWS:PAD_ROWS, :] = edges[7]
    outs = [
        pltpu.make_async_copy(src, dst, out_sem.at[n])
        for n, (src, dst) in enumerate(
            (
                (mat.at[0:D], att_ref.at[0:D]),
                (mat.at[MAT_ROWS:PAD_ROWS], att_ref.at[D:ATT_ROWS]),
                (mat.at[D:MAT_ROWS], ff_ref.at[slot]),
            )
        )
    ]
    for copy in outs:
        copy.start()
    for copy in outs:
        copy.wait()


def merge_blocks(at, pieces, rows, slot, ff=()):
    hbm = pl.BlockSpec(memory_space=pl.ANY)
    return call(
        functools.partial(merge_kernel, rows, slot),
        "merge_weights", (1,),
        [hbm] * (8 + len(ff)),
        [hbm] * 2,
        [shaped(BF, ATT_ROWS, D), shaped(BF, SLOTS, FF_ROWS, D)],
        [
            pltpu.VMEM((PAD_ROWS, D), BF),
            pltpu.VMEM((8, TILE_ROWS, D), BF),
            pltpu.SemaphoreType.DMA((8, 2)),
            pltpu.SemaphoreType.DMA((3,)),
        ],
        (at, *pieces, *ff),
        aliases={9: 1} if ff else {},
    )


def window_kernel(rows, windows, at_ref, *refs):
    own_att, own_ff, got_att, got_ff = refs[0:2], refs[2], refs[3:5], refs[5]
    outs, (own_s, got_s, own_sem, got_sem) = refs[6:-4], refs[-4:]
    cap = rows + TILE_ROWS

    def fetch(w, slot, att, ff, buf, sem):
        @pl.when(w < 2)
        def _():
            src = att.at[pl.ds(pl.multiple_of(rows * w, TILE_ROWS), cap)]
            pltpu.make_async_copy(src, buf, sem).start()

        @pl.when(w == 2)
        def _():
            pltpu.make_async_copy(att.at[2 * rows : D], buf.at[0 : D - 2 * rows], sem).start()
            pltpu.make_async_copy(ff.at[slot, 0 : 3 * rows + TILE_ROWS - D], buf.at[D - 2 * rows : cap], sem).start()

        @pl.when((w > 2) & (w < 7))
        def _():
            src = ff.at[slot, pl.ds(pl.multiple_of(rows * w - D, TILE_ROWS), cap)]
            pltpu.make_async_copy(src, buf, sem).start()

        @pl.when(w == 7)
        def _():
            pltpu.make_async_copy(ff.at[slot, 7 * rows - D : FF_ROWS], buf.at[0:rows], sem).start()
            pltpu.make_async_copy(att.at[D:ATT_ROWS], buf.at[rows:cap], sem).start()

    for n, (slot, where) in enumerate(windows):
        w = at_ref[where]
        fetch(w, slot, own_att[slot], own_ff, own_s.at[n], own_sem.at[n])
        fetch(w, slot, got_att[slot], got_ff, got_s.at[n], got_sem.at[n])
    for n in range(len(windows)):
        pltpu.make_async_copy(own_ff.at[0, 0:cap], own_s.at[n], own_sem.at[n]).wait()
        pltpu.make_async_copy(own_ff.at[0, 0:cap], got_s.at[n], got_sem.at[n]).wait()
        outs[n][...] = (own_s[n].astype(F32) + got_s[n].astype(F32)).astype(BF)


def split_windows(at, names, own, got, rows):
    hbm = pl.BlockSpec(memory_space=pl.ANY)
    cap = rows + TILE_ROWS
    n = len(names)
    windows = [(int(name[0] in "YD"), int(name[1]) + 4 * int(name[0] in "XD")) for name in names]
    outs = call(
        functools.partial(window_kernel, rows, windows),
        "split_windows", (1,),
        [hbm] * 6,
        [whole(cap, D)] * n,
        [shaped(BF, cap, D)] * n,
        [
            pltpu.VMEM((n, cap, D), BF),
            pltpu.VMEM((n, cap, D), BF),
            pltpu.SemaphoreType.DMA((n,)),
            pltpu.SemaphoreType.DMA((n,)),
        ],
        (at, *own, *got),
    )
    return dict(zip(names, outs))


def segment_of(pos, len_ref):
    end0 = len_ref[0]
    end1 = end0 + len_ref[1]
    end2 = end1 + len_ref[2]
    return (
        (pos >= end0).astype(jnp.int32)
        + (pos >= end1).astype(jnp.int32)
        + (pos >= end2).astype(jnp.int32)
    )


def att_fwd_kernel(
    scal_ref, x_ref, att0_ref, att1_ref, att2_ref, att3_ref,
    qkv_ref, wq_ref, mixed_ref, probs_ref, xp_ref, n1_ref, r1_ref, tails_ref,
    table_s, acc_s, att_s, main_sem, tail_sem,
):
    s = pl.program_id(0)
    len_ref = scal_ref
    atts = (att0_ref, att1_ref, att2_ref, att3_ref)

    @pl.when(s == 0)
    def _():
        tails = [
            pltpu.make_async_copy(att.at[D:ATT_ROWS], tails_ref.at[k], tail_sem.at[k]) for k, att in enumerate(atts)
        ]
        for copy in tails:
            copy.start()
        for k, att in enumerate(atts):
            pltpu.make_async_copy(att.at[0:D], att_s.at[k], main_sem.at[k]).start()
        for copy in tails:
            copy.wait()
        xp_ref[...] = mm(x_ref[...], column_order()).astype(BF)
        acc_s[...] = jnp.zeros_like(acc_s)
        flat = jnp.concatenate(
            [
                jnp.concatenate([tails_ref[k, 1:2, 384:768], tails_ref[k, 2:3, 0:384]], axis=1).astype(F32)
                for k in range(RANKS)
            ]
            + [jnp.zeros((8 - RANKS, D), F32)],
            axis=0,
        ).astype(BF)
        tables = mm(flat, table_order())
        for k in range(RANKS):
            for h in range(HPR):
                row = tables[k : k + 1, BUCKETS * h : BUCKETS * (h + 1)]
                table_s[k, h : h + 1, :] = jnp.concatenate(
                    [
                        row,
                        jnp.broadcast_to(row[:, 255:256], (1, BLK)),
                        jnp.broadcast_to(row[:, 0:1], (1, BLK)),
                    ],
                    axis=1,
                )

    pltpu.make_async_copy(att0_ref.at[0:D], att_s.at[s], main_sem.at[s]).wait()
    for src_row, src_col, dst_row, dst_col in qkv_pieces():
        wq_ref[0, dst_row : dst_row + 96, dst_col : dst_col + PART] = att_s[
            s, src_row : src_row + 96, src_col : src_col + PART
        ]

    first = tails_ref[s, 0:1, :]
    bias = jnp.concatenate(
        [first[:, 0:PART], jnp.zeros((1, PART), BF), first[:, PART : 2 * PART]], axis=1
    ).astype(F32)
    qkv = (mm(xp_ref[...], wq_ref[0]) + bias).astype(BF)
    qkv_ref[0] = qkv

    seg_j = segment_of(lax.broadcasted_iota(jnp.int32, (1, L), 1), len_ref)
    table = table_s[s]
    heads = []
    for h in range(HPR):
        q = qkv[:, HD * h : HD * (h + 1)]
        k = qkv[:, PART + HD * h : PART + HD * (h + 1)]
        v = qkv[:, 2 * PART + HD * h : 2 * PART + HD * (h + 1)]
        row = table[h : h + 1, :]
        near = pltpu.roll(jnp.broadcast_to(row, (BLK, 4 * BLK)), 0, 1, stride=1, stride_axis=0)
        far_right = jnp.broadcast_to(row[:, 255:256], (BLK, BLK))
        far_left = jnp.broadcast_to(row[:, 511:512], (BLK, BLK))
        for i in range(NBLK):
            seg_i = segment_of(
                lax.broadcasted_iota(jnp.int32, (BLK, 1), 0) + BLK * i, len_ref
            )
            parts = []
            for jb in range(NBLK):
                delta = jb - i
                if abs(delta) <= 1:
                    parts.append(near[:, BLK * (delta + 1) : BLK * (delta + 2)])
                else:
                    parts.append(far_right if delta > 0 else far_left)
            logits = mm_nt(q[BLK * i : BLK * (i + 1)], k) * 0.125 + jnp.concatenate(parts, axis=1)
            logits = jnp.where(seg_i == seg_j, logits, NEG)
            top = jnp.max(logits, axis=-1, keepdims=True)
            expo = jnp.exp(logits - top)
            total = jnp.sum(expo, axis=-1, keepdims=True)
            probs_ref[0, h, BLK * i : BLK * (i + 1), :] = (expo * (1.0 / total)).astype(BF)
        heads.append(mm(probs_ref[0, h], v))
    mixed = jnp.concatenate(heads, axis=1).astype(BF)
    mixed_ref[0] = mixed
    acc_s[...] += mm(mixed, att_s[s, QKV_ROWS:D, :])

    @pl.when(s == RANKS - 1)
    def _():
        vec = vector_rows(tails_ref, PlaceView(scal_ref))
        normed, inv = normalize(x_ref[...].astype(F32) + acc_s[...] + vec[0])
        n1_ref[...] = normed
        r1_ref[...] = jnp.broadcast_to(inv, (L, BLK))


def attention_forward(scalars, x, atts):
    per = lambda *shape: pl.BlockSpec((1, *shape), lambda s, n: (s,) + (0,) * len(shape))
    return call(
        att_fwd_kernel,
        "attention_forward", (RANKS,),
        [whole(L, D)] + [pl.BlockSpec(memory_space=pl.ANY)] * RANKS,
        [
            per(L, QKV_ROWS), per(D, QKV_ROWS), per(L, PART), per(HPR, L, L),
            whole(L, D), whole(L, D), whole(L, BLK), whole(RANKS, TILE_ROWS, D),
        ],
        [
            shaped(BF, RANKS, L, QKV_ROWS),
            shaped(BF, RANKS, D, QKV_ROWS),
            shaped(BF, RANKS, L, PART),
            shaped(BF, RANKS, HPR, L, L),
            shaped(BF, L, D),
            shaped(F32, L, D),
            shaped(F32, L, BLK),
            shaped(BF, RANKS, TILE_ROWS, D),
        ],
        [
            pltpu.VMEM((RANKS, 8, 512), F32),
            pltpu.VMEM((L, D), F32),
            pltpu.VMEM((RANKS, D, D), BF),
            pltpu.SemaphoreType.DMA((RANKS,)),
            pltpu.SemaphoreType.DMA((RANKS,)),
        ],
        (scalars, x, *atts),
        flops=6_000_000_000, moved=24_000_000,
    )


def ffn_kernel(
    place_ref, n1_ref, r1_ref, og_ref, up0_ref, down0_ref, up1_ref, down1_ref, tails_ref,
    block_ref, grad0_ref, grad1_ref, grad_one_ref, ga_ref, vec_ref, bup_ref,
    fn_s, fl_s, slope_s, act_s, down_s, gd_s, gf_s, og_s, og_sem,
):
    step = pl.program_id(0)
    inv_root2 = 1.0 / math.sqrt(2.0)

    @pl.when(step == 0)
    def _():
        vec = vector_rows(tails_ref, PlaceView(place_ref))
        first = n1_ref[...] * vec[2] + vec[3]
        pltpu.make_async_copy(og_ref, og_s, og_sem).start()
        fn_s[...] = first
        fl_s[...] = first.astype(BF)
        down_s[...] = jnp.zeros_like(down_s)

    def forward(slot, up_ref, down_ref):
        bias = jnp.concatenate([tails_ref[slot, 0:1, 384:768], tails_ref[slot, 1:2, 0:384]], axis=1)
        up = mm(fl_s[...], up_ref[0]) + bias.astype(F32)
        half = 0.5 * (1.0 + lax.erf(up * inv_root2))
        act = (up * half).astype(BF)
        slope_s[slot] = half + up * jnp.exp(-0.5 * up * up) * (1.0 / math.sqrt(2.0 * math.pi))
        act_s[slot] = act
        down_s[...] += mm(act, down_ref[0])

    @pl.when(step < 2)
    def _():
        forward(step, up0_ref, down0_ref)

    @pl.when((step == 2) | (step == 3))
    def _():
        forward(step, up1_ref, down1_ref)

    @pl.when(step == RANKS)
    def _():
        vec = vector_rows(tails_ref, PlaceView(place_ref))
        normed, inv = normalize(fn_s[...] + down_s[...] + vec[1])
        block_ref[...] = (normed * vec[4] + vec[5]).astype(BF)
        pltpu.make_async_copy(og_ref, og_s, og_sem).wait()
        og = og_s[...].astype(F32)
        vec_ref[4:5, :] = col_sum(og * normed)
        vec_ref[5:6, :] = col_sum(og)
        grad_two = norm_backward(og * vec[4], normed, inv)
        low = grad_two.astype(BF)
        gd_s[...] = low
        vec_ref[1:2, :] = col_sum(low.astype(F32))
        vec_ref[6:8, :] = jnp.zeros((2, D), F32)
        gf_s[...] = grad_two

    def backward(slot, up_ref, down_ref, grad_ref):
        gd = gd_s[...]
        grad_ref[0, D:FF_ROWS, :] = mm_tn(act_s[slot], gd).astype(BF)
        gu = (mm_nt(gd, down_ref[0]) * slope_s[slot]).astype(BF)
        bup_ref[0, 0:1, :] = col_sum(gu.astype(F32))
        bup_ref[0, 1:8, :] = jnp.zeros((7, D), F32)
        grad_ref[0, 0:D, :] = mm_tn(fl_s[...], gu).astype(BF)
        gf_s[...] += mm_nt(gu, up_ref[0])

    @pl.when((step == 4) | (step == 5))
    def _():
        backward(step - 2, up1_ref, down1_ref, grad1_ref)

    @pl.when(step >= 6)
    def _():
        backward(step - 6, up0_ref, down0_ref, grad0_ref)

    @pl.when(step == 2 * RANKS - 1)
    def _():
        vec = vector_rows(tails_ref, PlaceView(place_ref))
        f = gf_s[...]
        normed = n1_ref[...]
        vec_ref[2:3, :] = col_sum(f * normed)
        vec_ref[3:4, :] = col_sum(f)
        grad_one = norm_backward(f * vec[2], normed, r1_ref[:, 0:1])
        grad_one_ref[...] = grad_one
        low = grad_one.astype(BF)
        ga_ref[...] = low
        vec_ref[0:1, :] = col_sum(low.astype(F32))


def feed_forward(place, n1, r1, out_grad, own_ff, got_ff, tails):
    def own_at(half):
        return lambda s, n: ((((s >= 1) & (s <= 3)) | (s == 7)).astype(jnp.int32), half, 0)

    def got_at(half):
        return lambda s, n: (((s == 3) | (s >= 5)).astype(jnp.int32), half, 0)

    wt = lambda index: pl.BlockSpec((1, D, D), index)
    return call(
        ffn_kernel,
        "feed_forward", (2 * RANKS,),
        [
            whole(L, D), whole(L, BLK), pl.BlockSpec(memory_space=pl.ANY),
            wt(own_at(0)), wt(own_at(1)), wt(got_at(0)), wt(got_at(1)),
            whole(RANKS, TILE_ROWS, D),
        ],
        [
            whole(L, D),
            pl.BlockSpec((1, FF_ROWS, D), lambda s, n: ((s >= 7).astype(jnp.int32), 0, 0)),
            pl.BlockSpec((1, FF_ROWS, D), lambda s, n: ((s >= 5).astype(jnp.int32), 0, 0)),
            whole(L, D), whole(L, D), whole(8, D),
            pl.BlockSpec((1, 8, D), lambda s, n: (lax.rem(jnp.maximum(s, 4) - 2, 4), 0, 0)),
        ],
        [
            shaped(BF, L, D),
            shaped(BF, SLOTS, FF_ROWS, D),
            shaped(BF, SLOTS, FF_ROWS, D),
            shaped(F32, L, D),
            shaped(BF, L, D),
            shaped(F32, 8, D),
            shaped(F32, RANKS, 8, D),
        ],
        [
            pltpu.VMEM((L, D), F32),
            pltpu.VMEM((L, D), BF),
            pltpu.VMEM((RANKS, L, D), F32),
            pltpu.VMEM((RANKS, L, D), BF),
            pltpu.VMEM((L, D), F32),
            pltpu.VMEM((L, D), BF),
            pltpu.VMEM((L, D), F32),
            pltpu.VMEM((L, D), BF),
            pltpu.SemaphoreType.DMA,
        ],
        (place, n1, r1, out_grad, own_ff, own_ff, got_ff, got_ff, tails),
        flops=14_500_000_000, moved=36_000_000,
    )


def diagonal_sums(block):
    half = block.shape[0] // 2
    while half >= 8:
        block = block[:half] + pltpu.roll(block[half:], 4 * BLK - half, 1)
        half //= 2
    row = lax.broadcasted_iota(jnp.int32, (8, 1), 0)
    for bit in (4, 2, 1):
        block = jnp.where((row & bit) > 0, pltpu.roll(block, 4 * BLK - bit, 1), block)
    return col_sum(block)


def att_bwd_kernel(
    place_ref, ga_ref, att0_ref, att1_ref, att2_ref, att3_ref,
    qkv_ref, probs_ref, mixed_ref, wq_ref, xp_ref, vec_ref, bup_ref, grad_one_ref,
    da0_ref, da1_ref, da2_ref, da3_ref, in_grad_ref,
    ds_s, near_s, sums_s, dx_s, order_s, wo_s, das_s, xp_s, one_s, sem, out_sem, late_sem,
):
    s = pl.program_id(0)
    slot = RANKS - 1 - s
    da_s = das_s.at[lax.rem(s, 2)]

    def leave(k):
        da_ref = (da0_ref, da1_ref, da2_ref, da3_ref)[k]
        return pltpu.make_async_copy(das_s.at[(RANKS - 1 - k) % 2], da_ref, out_sem.at[k])

    for k in range(2):

        @pl.when(slot == k)
        def _(k=k):
            leave(k + 2).wait()

    @pl.when(s == 0)
    def _():
        for k, att in enumerate((att0_ref, att1_ref, att2_ref, att3_ref)):
            pltpu.make_async_copy(att.at[QKV_ROWS:D], wo_s.at[k], sem.at[k]).start()
        pltpu.make_async_copy(xp_ref, xp_s, late_sem.at[0]).start()
        pltpu.make_async_copy(grad_one_ref, one_s, late_sem.at[1]).start()
        order_s[...] = table_order()
        dx_s[...] = jnp.zeros_like(dx_s)
        sums_s[...] = jnp.zeros_like(sums_s)

    ga = ga_ref[...]
    da_s[QKV_ROWS:D, :] = mm_tn(mixed_ref[0], ga).astype(BF)
    pltpu.make_async_copy(att0_ref.at[QKV_ROWS:D], wo_s.at[slot], sem.at[slot]).wait()
    dm_all = mm_nt(ga, wo_s[slot]).astype(BF)
    qkv = qkv_ref[0]
    dq, dk, dv = [], [], []
    for h in range(HPR):
        q = qkv[:, HD * h : HD * (h + 1)]
        k = qkv[:, PART + HD * h : PART + HD * (h + 1)]
        v = qkv[:, 2 * PART + HD * h : 2 * PART + HD * (h + 1)]
        dm = dm_all[:, HD * h : HD * (h + 1)]
        far_left = jnp.zeros((BLK, BLK), F32)
        far_right = jnp.zeros((BLK, BLK), F32)
        for i in range(NBLK):
            rows = slice(BLK * i, BLK * (i + 1))
            p = probs_ref[0, h, rows, :].astype(F32)
            dp = mm_nt(dm[rows], v)
            ds = (p * (dp - jnp.sum(p * dp, axis=-1, keepdims=True))).astype(BF)
            ds_s[rows, :] = ds
            ds = ds.astype(F32)
            for jb in range(NBLK):
                piece = ds[:, BLK * jb : BLK * (jb + 1)]
                delta = jb - i
                if abs(delta) <= 1:
                    cols = slice(BLK * (delta + 1), BLK * (delta + 2))
                    if i == max(0, -delta):
                        near_s[:, cols] = piece
                    else:
                        near_s[:, cols] += piece
                elif delta > 0:
                    far_right += piece
                else:
                    far_left += piece
        near_s[:, 3 * BLK :] = jnp.zeros((BLK, BLK), F32)
        sums_s[h : h + 1, 0 : 4 * BLK] = diagonal_sums(near_s[...])
        sums_s[h : h + 1, 4 * BLK : 5 * BLK] = col_sum(far_left)
        sums_s[h : h + 1, 5 * BLK : 6 * BLK] = col_sum(far_right)
        dscore = ds_s[...]
        dq.append(mm(dscore, k) * 0.125)
        dk.append(mm_tn(dscore, q) * 0.125)
        dv.append(mm_tn(probs_ref[0, h], dm))
    dqkv = jnp.concatenate(dq + dk + dv, axis=1).astype(BF)

    qv = col_sum(dqkv.astype(F32))
    sums = sums_s[...]
    lane = lax.broadcasted_iota(jnp.int32, (1, 6 * BLK), 1)
    is_left = (lane == 0) | ((lane >= 3 * BLK) & (lane < 5 * BLK))
    is_right = ((lane >= BUCKETS - 1) & (lane < 3 * BLK)) | (lane >= 5 * BLK)
    left = jnp.sum(jnp.where(is_left, sums, 0.0), axis=-1, keepdims=True)
    right = jnp.sum(jnp.where(is_right, sums, 0.0), axis=-1, keepdims=True)
    sums = jnp.where(lane == 0, left, jnp.where(lane == BUCKETS - 1, right, sums))
    table = jnp.concatenate([sums[h : h + 1, :BUCKETS] for h in range(HPR)], axis=1)
    table = jnp.broadcast_to(table, (8, D)).astype(BF)
    table = mm_nt(table, order_s[...])[0:1]
    r = slice_of(slot, PlaceView(place_ref))
    vecs = []
    for i in range(3):
        m = 3 * r + i
        row = vec_ref[pl.ds(m // 2, 1), :]
        vecs.append(jnp.where(m % 2 == 0, row[:, 0:384], row[:, 384:768]))
    bup = bup_ref[0, 0:1, :]
    tail = jnp.concatenate(
        [
            jnp.concatenate([qv[:, 0:PART], qv[:, 2 * PART :], bup[:, 0:384]], axis=1),
            jnp.concatenate([bup[:, 384:768], table[:, 0:384]], axis=1),
            jnp.concatenate([table[:, 384:768], vecs[0]], axis=1),
            jnp.concatenate([vecs[1], vecs[2]], axis=1),
            jnp.zeros((TILE_ROWS - 4, D), F32),
        ],
        axis=0,
    )
    da_s[D:ATT_ROWS, :] = tail.astype(BF)

    @pl.when(s == 0)
    def _():
        pltpu.make_async_copy(xp_ref, xp_s, late_sem.at[0]).wait()

    dw = mm_tn(xp_s[...], dqkv).astype(BF)
    for src_row, src_col, dst_row, dst_col in qkv_pieces():
        da_s[src_row : src_row + 96, src_col : src_col + PART] = dw[
            dst_row : dst_row + 96, dst_col : dst_col + PART
        ]
    dx_s[...] += mm_nt(dqkv, wq_ref[0])

    for k in range(RANKS):

        @pl.when(slot == k)
        def _(k=k):
            leave(k).start()

    @pl.when(s == RANKS - 1)
    def _():
        pltpu.make_async_copy(grad_one_ref, one_s, late_sem.at[1]).wait()
        in_grad_ref[...] = one_s[...] + mm_nt(dx_s[...].astype(BF), column_order())
        for k in range(2):
            leave(k).wait()


def attention_backward(scalars, ga, atts, qkv, wq, mixed, probs, xp, vec_g, up_g, grad_one):
    per = lambda *shape: pl.BlockSpec((1, *shape), lambda s, n: (RANKS - 1 - s,) + (0,) * len(shape))
    return call(
        att_bwd_kernel,
        "attention_backward", (RANKS,),
        [whole(L, D)]
        + [pl.BlockSpec(memory_space=pl.ANY)] * RANKS
        + [
            per(L, QKV_ROWS), per(HPR, L, L), per(L, PART), per(D, QKV_ROWS),
            pl.BlockSpec(memory_space=pl.ANY), whole(8, D), per(8, D), pl.BlockSpec(memory_space=pl.ANY),
        ],
        [pl.BlockSpec(memory_space=pl.ANY)] * RANKS + [whole(L, D)],
        [shaped(BF, ATT_ROWS, D)] * RANKS + [shaped(F32, L, D)],
        [
            pltpu.VMEM((L, L), BF),
            pltpu.VMEM((BLK, 4 * BLK), F32),
            pltpu.VMEM((8, 6 * BLK), F32),
            pltpu.VMEM((L, D), F32),
            pltpu.VMEM((D, D), BF),
            pltpu.VMEM((RANKS, PART, D), BF),
            pltpu.VMEM((2, ATT_ROWS, D), BF),
            pltpu.VMEM((L, D), BF),
            pltpu.VMEM((L, D), F32),
            pltpu.SemaphoreType.DMA((RANKS,)),
            pltpu.SemaphoreType.DMA((RANKS,)),
            pltpu.SemaphoreType.DMA((2,)),
        ],
        (scalars, ga, *atts, qkv, probs, mixed, wq, xp, vec_g, up_g, grad_one),
        flops=12_000_000_000, moved=30_000_000,
    )


X_SWAP = [(w, w ^ 1) for w in range(8)]
Z_RING = [(w, (w + 2) % 8) for w in range(8)]
Y_SWAP = [(n, n ^ 2) for n in range(4)]
CORE_SWAP = [(n, n ^ 1) for n in range(4)]


def swap_x(a):
    return lax.ppermute(a, "wide", X_SWAP)


def swap_y(a):
    return lax.ppermute(a, "narrow", Y_SWAP)


def ring_z(a):
    return lax.ppermute(a, "wide", Z_RING)


def ring_back(a):
    return lax.ppermute(a, "wide", [(j, i) for i, j in Z_RING])


def swap_core(a):
    return lax.ppermute(a, "narrow", CORE_SWAP)


def after(value, earlier):
    return lax.optimization_barrier((value, earlier))[0]


def aligned_plan(shard, wide, ranks):
    unit = TILE_ROWS * D
    tiles, spare = divmod(shard, unit)
    rows = tiles * TILE_ROWS
    fits = (
        wide == 8
        and ranks == RANKS
        and spare * wide <= unit
        and spare % 128 == 0
        and rows * wide == MAT_ROWS
        and rows == QKV_ROWS // 2
    )
    return rows, spare, fits


def window_places(z, x):
    planes = jnp.mod(z - jnp.arange(4, dtype=jnp.int32), 4)
    return jnp.concatenate([2 * planes + x, 2 * planes + 1 - x])


def gather_blocks(r0, z, x, rows):
    r1, x0, y0 = ring_z(r0), swap_x(r0), swap_y(r0)
    d0 = swap_y(after(x0, y0))
    r2, x1, y1 = ring_z(r1), swap_x(after(r1, x0)), swap_y(after(r1, y0))
    r3, x2, y2 = ring_z(r2), swap_x(after(r2, x0)), swap_y(after(r2, d0))
    d1 = ring_z(after(d0, y1))
    x3 = swap_x(after(r3, x1))
    y3, d2, d3 = ring_z(after(y2, r3)), swap_x(after(y2, x2)), swap_y(after(x3, y1))
    at = window_places(z, x)
    near_att, ff = merge_blocks(at, (r0, r1, r2, r3, x0, x1, x2, x3), rows, 0)
    near_got = swap_core(near_att)
    far_att, ff = merge_blocks(at, (y0, y1, y2, y3, d0, d1, d2, d3), rows, 1, (ff,))
    far_got = swap_core(far_att)
    return ((near_att, far_att), ff), ((near_got, far_got), swap_core(after(ff, (near_got, far_got))))


def add_low(*terms):
    total = terms[0].astype(F32)
    for term in terms[1:]:
        total = total + term.astype(F32)
    return total.astype(BF)


def reduce_windows(own_att, got_att, own_ff, got_ff, z, x, rows):
    at = window_places(z, x)
    far_got = swap_core(got_att[1])
    near_got = swap_core(after(got_att[0], far_got))
    far = (own_att[1], own_att[1], own_ff), (far_got, far_got, got_ff)
    a = split_windows(at, ("D3", "Y3", "D2"), *far, rows)
    y1, z1, x1 = swap_y(a["D3"]), ring_back(a["Y3"]), swap_x(a["D2"])
    both = (*own_att, own_ff), (near_got, far_got, got_ff)
    a |= split_windows(
        at, ("X3", "Y2", "Y1", "D1", "R3", "X2", "R2", "X1", "R1", "D0", "X0", "Y0", "R0"), *both, rows
    )
    z2 = ring_back(after(a["D1"], x1))
    y3 = swap_y(after(a["Y1"], x1))
    far = add_low(a["X3"], y1)
    x2 = swap_x(far)
    y2 = swap_y(add_low(a["Y2"], z1, x1))
    x3 = swap_x(after(a["X2"], x2))
    z3 = ring_back(add_low(a["R3"], x2))
    x4 = swap_x(after(a["X1"], x3))
    y4 = swap_y(add_low(a["D0"], z2))
    z4 = ring_back(add_low(a["R2"], y2, z3, x3))
    y5 = swap_y(after(a["Y0"], y2))
    z5 = ring_back(add_low(a["R1"], y3, z4, x4))
    x5 = swap_x(add_low(a["X0"], y4))
    return a["R0"], z5, x5, y5


def gather_plain(params):
    flat = lax.all_gather(params.astype(BF)[0], "wide", axis=0, tiled=True)
    flat = jnp.pad(flat, (0, PAD_ROWS * D - flat.shape[0])).reshape(PAD_ROWS, D)
    head = jnp.swapaxes(flat[:QKV_ROWS].reshape(2, 96, 3, D), 1, 2).reshape(QKV_ROWS, D)
    flat = jnp.concatenate([head, flat[QKV_ROWS:]], axis=0)
    mats = lax.all_gather(flat, "narrow", axis=0, tiled=True).reshape(2, 2, PAD_ROWS, D)
    pairs = []
    for core in range(2):
        pair = mats[:, core]
        pairs.append((jnp.concatenate([pair[:, :D], pair[:, MAT_ROWS:]], axis=1), pair[:, D:MAT_ROWS]))
    return pairs


def scatter_plain(pairs, shard, wide):
    mats = [jnp.concatenate([att[:, :D], ff, att[:, D:]], axis=1) for att, ff in pairs]
    grads = jnp.stack(mats, axis=1).reshape(-1, D)
    mine = lax.psum_scatter(grads, "narrow", scatter_dimension=0, tiled=True)
    head = jnp.swapaxes(mine[:QKV_ROWS].reshape(2, 3, 96, D), 1, 2).reshape(QKV_ROWS, D)
    flat = jnp.concatenate([head, mine[QKV_ROWS:]], axis=0).reshape(-1)[: shard * wide]
    return lax.psum_scatter(flat.astype(F32), "wide", scatter_dimension=0, tiled=True).reshape(1, shard)


def body(hidden_in, out_grad, pair_lengths, params, momentum, average):
    wide, ranks = lax.axis_size("wide"), lax.axis_size("narrow")
    shard = params.shape[1]
    rows, spare, fits = aligned_plan(shard, wide, ranks)
    at_wide, at_narrow = lax.axis_index("wide"), lax.axis_index("narrow")
    if fits:
        place = jnp.stack([at_wide, at_narrow // 2, at_narrow % 2]).astype(jnp.int32)
        scalars = jnp.concatenate([pair_lengths[0], place])
        block = own_block(scalars, params, rows, spare, wide)
        (own_att, own_ff), (got_att, got_ff) = gather_blocks(block, at_wide // 2, at_wide % 2, rows)
    else:
        scalars = jnp.concatenate([pair_lengths[0], jnp.zeros((3,), jnp.int32)])
        (own_att, own_ff), (got_att, got_ff) = gather_plain(params)
    atts = (own_att[0], own_att[1], got_att[0], got_att[1])

    qkv, wq, mixed, probs, xp, n1, r1, tails = attention_forward(scalars, hidden_in, atts)
    block_out, own_ffg, got_ffg, grad_one, ga, vec_g, up_g = feed_forward(
        scalars, n1, r1, out_grad, own_ff, got_ff, tails
    )
    *attg, in_grad = attention_backward(scalars, ga, atts, qkv, wq, mixed, probs, xp, vec_g, up_g, grad_one)
    own_attg, got_attg = attg[:2], attg[2:]

    device_count = wide * ranks
    rate = 1.0 / (32.0 * math.sqrt(hidden_in.shape[0] * device_count))
    if fits:
        parts = reduce_windows(own_attg, got_attg, own_ffg, swap_core(got_ffg), at_wide // 2, at_wide % 2, rows)
        grads, new_params, new_momentum, new_average, low = update_shard(
            scalars, parts, params, momentum, average, rate, rows, spare, wide
        )
    else:
        grads = scatter_plain(((jnp.stack(own_attg), own_ffg), (jnp.stack(got_attg), got_ffg)), shard, wide)
        new_momentum = 0.5 * momentum + rate * grads
        new_params = params - (rate * grads + 0.5 * new_momentum)
        new_average = 0.5 * average + 0.5 * new_params
        low = new_params.astype(BF)
    return (
        block_out,
        in_grad,
        grads,
        new_params,
        new_momentum,
        new_average,
        low,
    )


def solution(mesh):
    rows = P(("wide", "narrow"), None)
    flat = P("narrow", "wide")
    return jax.shard_map(
        body,
        mesh=mesh,
        in_specs=(rows, rows, rows, flat, flat, flat),
        out_specs=(rows, rows, flat, flat, flat, flat, flat),
        check_vma=False,
    )
```

```python
import functools
import math

import jax
import jax.numpy as jnp
from jax import lax
from jax.experimental import pallas as pl
from jax.experimental.pallas import tpu as pltpu
from jax.sharding import PartitionSpec as P

D = 768
HEADS = 12
FF = 3072
HD = 64
BUCKETS = 256
L = 512
RANKS = 4
PART = D // RANKS
HPR = HEADS // RANKS
SLOTS = 2
QKV_ROWS = 3 * PART
TILE_ROWS = 8
MAT_ROWS = 3 * D
PAD_ROWS = MAT_ROWS + TILE_ROWS
ATT_ROWS = D + TILE_ROWS
FF_ROWS = 2 * D
BLK = 128
NBLK = L // BLK
NEG = -1000000000.0
VMEM_LIMIT = 60 * 1024 * 1024
BF = jnp.bfloat16
F32 = jnp.float32


def mm(a, b):
    return jnp.dot(a, b, preferred_element_type=F32)


def mm_nt(a, b):
    return lax.dot_general(a, b, (((1,), (1,)), ((), ())), preferred_element_type=F32)


def mm_tn(a, b):
    return lax.dot_general(a, b, (((0,), (0,)), ((), ())), preferred_element_type=F32)


def qkv_pieces():
    for b in range(2):
        for j in range(4):
            for c in range(3):
                t, q = divmod(3 * j + c, 4)
                yield 288 * b + 96 * t, PART * q, PART * j + 96 * b, PART * c


def column_order():
    d = lax.broadcasted_iota(jnp.int32, (D, D), 0)
    n = lax.broadcasted_iota(jnp.int32, (D, D), 1)
    j = (n >= PART).astype(jnp.int32) + (n >= 2 * PART).astype(jnp.int32) + (n >= 3 * PART).astype(jnp.int32)
    return (d == 4 * (n - PART * j) + j).astype(F32).astype(BF)


def slot_of(r, place_ref):
    return ((r // 2) ^ place_ref[1]) + 2 * ((r % 2) ^ place_ref[2])


def slice_of(slot, place_ref):
    return 2 * ((slot % 2) ^ place_ref[1]) + ((slot // 2) ^ place_ref[2])


def vector_rows(tails_ref, place_ref):
    chunks = []
    for r in range(RANKS):
        k = slot_of(r, place_ref)
        chunks.append(tails_ref[k, 2:3, 384:768])
        chunks.append(tails_ref[k, 3:4, 0:384])
        chunks.append(tails_ref[k, 3:4, 384:768])
    return [
        jnp.concatenate([chunks[2 * v], chunks[2 * v + 1]], axis=1).astype(F32) for v in range(6)
    ]


def table_order():
    src = lax.broadcasted_iota(jnp.int32, (D, D), 0)
    dst = lax.broadcasted_iota(jnp.int32, (D, D), 1)
    hh = (dst >= BUCKETS).astype(jnp.int32) + (dst >= 2 * BUCKETS).astype(jnp.int32)
    return (src == 3 * (dst - BUCKETS * hh) + hh).astype(F32).astype(BF)


def normalize(values):
    centred = values - jnp.mean(values, axis=-1, keepdims=True)
    inv = lax.rsqrt(jnp.mean(centred * centred, axis=-1, keepdims=True) + 1e-05)
    return centred * inv, inv


def norm_backward(e, normed, inv):
    return inv * (
        e - jnp.mean(e, axis=-1, keepdims=True) - normed * jnp.mean(e * normed, axis=-1, keepdims=True)
    )


def col_sum(values):
    return jnp.sum(values, axis=0, keepdims=True)


def call(kernel, name, grid, in_specs, out_specs, out_shape, scratch, args, vmem=VMEM_LIMIT, flops=0, moved=0, aliases=None):
    return pl.pallas_call(
        kernel,
        grid_spec=pltpu.PrefetchScalarGridSpec(
            num_scalar_prefetch=1,
            grid=grid,
            in_specs=in_specs,
            out_specs=out_specs,
            scratch_shapes=scratch,
        ),
        out_shape=out_shape,
        input_output_aliases=aliases or {},
        compiler_params=pltpu.CompilerParams(vmem_limit_bytes=vmem),
        cost_estimate=pl.CostEstimate(flops=flops, bytes_accessed=moved, transcendentals=0),
        name=name,
    )(*args)


def whole(*shape):
    return pl.BlockSpec(shape, lambda *_: (0,) * len(shape))


def shaped(dtype, *shape):
    return jax.ShapeDtypeStruct(shape, dtype)


class PlaceView:
    def __init__(self, ref):
        self.ref = ref

    def __getitem__(self, i):
        return self.ref[4 + i]


def block_kernel(rows, lead, shift, place_ref, flat_ref, out_ref, rows_s):
    w = place_ref[4]
    count = flat_ref.shape[1] // 128
    rows_s[0:lead, :] = jnp.zeros((lead, 128), F32)
    rows_s[lead : lead + count, :] = flat_ref[...].reshape(count, 128)
    rows_s[lead + count :, :] = jnp.zeros((rows_s.shape[0] - lead - count, 128), F32)
    start = lead - shift * w
    third = rows // 3

    @pl.when(w < 2)
    def _():
        for t in range(3):
            for c in range(6):
                out_ref[third * t : third * (t + 1), 128 * c : 128 * (c + 1)] = rows_s[
                    pl.ds(start + 6 * t + c, third, stride=18), :
                ].astype(BF)

    @pl.when(w >= 2)
    def _():
        for c in range(6):
            out_ref[0:rows, 128 * c : 128 * (c + 1)] = rows_s[
                pl.ds(start + c, rows, stride=6), :
            ].astype(BF)

    for c in range(6):
        out_ref[rows : rows + TILE_ROWS, 128 * c : 128 * (c + 1)] = rows_s[
            pl.ds(start + 6 * rows + c, TILE_ROWS, stride=6), :
        ].astype(BF)


def own_block(place, params, rows, spare, wide):
    count = params.shape[1] // 128
    lead = spare // 128 * wide
    total = -(-(lead + 6 * (rows + TILE_ROWS)) // 8) * 8
    return call(
        functools.partial(block_kernel, rows, lead, spare // 128),
        "own_block", (1,),
        [whole(*params.shape)],
        whole(rows + TILE_ROWS, D),
        shaped(BF, rows + TILE_ROWS, D),
        [pltpu.VMEM((total, 128), F32)],
        (place, params),
        vmem=16 * 1024 * 1024,
    )


def update_kernel(
    rows, lead, shift, rate, place_ref, kept_ref, near_ref, second_ref, ring_ref, params_ref, momentum_ref, average_ref,
    grads_ref, new_params_ref, new_momentum_ref, new_average_ref, low_ref, rows_s,
):
    w = place_ref[4]
    count = params_ref.shape[1] // 128
    block = (
        kept_ref[...].astype(F32) + near_ref[...].astype(F32) + second_ref[...].astype(F32) + ring_ref[...].astype(F32)
    )
    start = lead - shift * w
    third = rows // 3

    @pl.when(w < 2)
    def _():
        for t in range(3):
            for c in range(6):
                rows_s[pl.ds(start + 6 * t + c, third, stride=18), :] = block[
                    third * t : third * (t + 1), 128 * c : 128 * (c + 1)
                ]

    @pl.when(w >= 2)
    def _():
        for c in range(6):
            rows_s[pl.ds(start + c, rows, stride=6), :] = block[0:rows, 128 * c : 128 * (c + 1)]

    for c in range(6):
        rows_s[pl.ds(start + 6 * rows + c, TILE_ROWS, stride=6), :] = block[
            rows : rows + TILE_ROWS, 128 * c : 128 * (c + 1)
        ]
    grads = rows_s[lead : lead + count, :].reshape(params_ref.shape)
    grads_ref[...] = grads
    params = params_ref[...]
    new_momentum = 0.5 * momentum_ref[...] + rate * grads
    new_params = params - (rate * grads + 0.5 * new_momentum)
    new_momentum_ref[...] = new_momentum
    new_params_ref[...] = new_params
    new_average_ref[...] = 0.5 * average_ref[...] + 0.5 * new_params
    low_ref[...] = new_params.astype(BF)


def update_shard(place, parts, params, momentum, average, rate, rows, spare, wide):
    count = params.shape[1] // 128
    lead = spare // 128 * wide
    total = -(-(lead + 6 * (rows + TILE_ROWS)) // 8) * 8
    kept, near, second, ring = parts
    cap = rows + TILE_ROWS
    flat = whole(*params.shape)
    return call(
        functools.partial(update_kernel, rows, lead, spare // 128, rate),
        "update_shard", (1,),
        [whole(cap, D)] * 4 + [flat] * 3,
        [flat] * 5,
        [shaped(F32, *params.shape)] * 4 + [shaped(BF, *params.shape)],
        [pltpu.VMEM((total, 128), F32)],
        (place, kept, near, second, ring, params, momentum, average),
        vmem=32 * 1024 * 1024,
    )


def merge_kernel(rows, slot, at_ref, *refs):
    pieces, (att_ref, ff_ref, mat, edges, in_sem, out_sem) = refs[:8], refs[-6:]
    copies = []
    for i in range(8):
        w = at_ref[i]
        main = pltpu.make_async_copy(
            pieces[i].at[0:rows], mat.at[pl.ds(pl.multiple_of(rows * w, TILE_ROWS), rows)], in_sem.at[i, 0]
        )
        edge = pltpu.make_async_copy(pieces[i].at[rows : rows + TILE_ROWS], edges.at[w], in_sem.at[i, 1])
        main.start()
        edge.start()
        copies += [main, edge]
    for copy in copies:
        copy.wait()
    for w in range(1, 8):
        at = rows * w
        mat[at : at + TILE_ROWS, :] = mat[at : at + TILE_ROWS, :] + edges[w - 1]
    mat[MAT_ROWS:PAD_ROWS, :] = edges[7]
    outs = [
        pltpu.make_async_copy(src, dst, out_sem.at[n])
        for n, (src, dst) in enumerate(
            (
                (mat.at[0:D], att_ref.at[0:D]),
                (mat.at[MAT_ROWS:PAD_ROWS], att_ref.at[D:ATT_ROWS]),
                (mat.at[D:MAT_ROWS], ff_ref.at[slot]),
            )
        )
    ]
    for copy in outs:
        copy.start()
    for copy in outs:
        copy.wait()


def merge_blocks(at, pieces, rows, slot, ff=()):
    hbm = pl.BlockSpec(memory_space=pl.ANY)
    return call(
        functools.partial(merge_kernel, rows, slot),
        "merge_weights", (1,),
        [hbm] * (8 + len(ff)),
        [hbm] * 2,
        [shaped(BF, ATT_ROWS, D), shaped(BF, SLOTS, FF_ROWS, D)],
        [
            pltpu.VMEM((PAD_ROWS, D), BF),
            pltpu.VMEM((8, TILE_ROWS, D), BF),
            pltpu.SemaphoreType.DMA((8, 2)),
            pltpu.SemaphoreType.DMA((3,)),
        ],
        (at, *pieces, *ff),
        aliases={9: 1} if ff else {},
    )


def window_kernel(rows, windows, at_ref, *refs):
    own_att, own_ff, got_att, got_ff = refs[0:2], refs[2], refs[3:5], refs[5]
    outs, (own_s, got_s, own_sem, got_sem) = refs[6:-4], refs[-4:]
    cap = rows + TILE_ROWS

    def fetch(w, slot, att, ff, buf, sem):
        @pl.when(w < 2)
        def _():
            src = att.at[pl.ds(pl.multiple_of(rows * w, TILE_ROWS), cap)]
            pltpu.make_async_copy(src, buf, sem).start()

        @pl.when(w == 2)
        def _():
            pltpu.make_async_copy(att.at[2 * rows : D], buf.at[0 : D - 2 * rows], sem).start()
            pltpu.make_async_copy(ff.at[slot, 0 : 3 * rows + TILE_ROWS - D], buf.at[D - 2 * rows : cap], sem).start()

        @pl.when((w > 2) & (w < 7))
        def _():
            src = ff.at[slot, pl.ds(pl.multiple_of(rows * w - D, TILE_ROWS), cap)]
            pltpu.make_async_copy(src, buf, sem).start()

        @pl.when(w == 7)
        def _():
            pltpu.make_async_copy(ff.at[slot, 7 * rows - D : FF_ROWS], buf.at[0:rows], sem).start()
            pltpu.make_async_copy(att.at[D:ATT_ROWS], buf.at[rows:cap], sem).start()

    for n, (slot, where) in enumerate(windows):
        w = at_ref[where]
        fetch(w, slot, own_att[slot], own_ff, own_s.at[n], own_sem.at[n])
        fetch(w, slot, got_att[slot], got_ff, got_s.at[n], got_sem.at[n])
    for n in range(len(windows)):
        pltpu.make_async_copy(own_ff.at[0, 0:cap], own_s.at[n], own_sem.at[n]).wait()
        pltpu.make_async_copy(own_ff.at[0, 0:cap], got_s.at[n], got_sem.at[n]).wait()
        outs[n][...] = (own_s[n].astype(F32) + got_s[n].astype(F32)).astype(BF)


def split_windows(at, names, own, got, rows):
    hbm = pl.BlockSpec(memory_space=pl.ANY)
    cap = rows + TILE_ROWS
    n = len(names)
    windows = [(int(name[0] in "YD"), int(name[1]) + 4 * int(name[0] in "XD")) for name in names]
    outs = call(
        functools.partial(window_kernel, rows, windows),
        "split_windows", (1,),
        [hbm] * 6,
        [whole(cap, D)] * n,
        [shaped(BF, cap, D)] * n,
        [
            pltpu.VMEM((n, cap, D), BF),
            pltpu.VMEM((n, cap, D), BF),
            pltpu.SemaphoreType.DMA((n,)),
            pltpu.SemaphoreType.DMA((n,)),
        ],
        (at, *own, *got),
    )
    return dict(zip(names, outs))


def segment_of(pos, len_ref):
    end0 = len_ref[0]
    end1 = end0 + len_ref[1]
    end2 = end1 + len_ref[2]
    return (
        (pos >= end0).astype(jnp.int32)
        + (pos >= end1).astype(jnp.int32)
        + (pos >= end2).astype(jnp.int32)
    )


def att_fwd_kernel(
    scal_ref, x_ref, att0_ref, att1_ref, att2_ref, att3_ref,
    qkv_ref, wq_ref, mixed_ref, probs_ref, xp_ref, n1_ref, r1_ref, tails_ref,
    table_s, acc_s, att_s, main_sem, tail_sem,
):
    s = pl.program_id(0)
    len_ref = scal_ref
    atts = (att0_ref, att1_ref, att2_ref, att3_ref)

    @pl.when(s == 0)
    def _():
        tails = [
            pltpu.make_async_copy(att.at[D:ATT_ROWS], tails_ref.at[k], tail_sem.at[k]) for k, att in enumerate(atts)
        ]
        for copy in tails:
            copy.start()
        for k, att in enumerate(atts):
            pltpu.make_async_copy(att.at[0:D], att_s.at[k], main_sem.at[k]).start()
        for copy in tails:
            copy.wait()
        xp_ref[...] = mm(x_ref[...], column_order()).astype(BF)
        acc_s[...] = jnp.zeros_like(acc_s)
        flat = jnp.concatenate(
            [
                jnp.concatenate([tails_ref[k, 1:2, 384:768], tails_ref[k, 2:3, 0:384]], axis=1).astype(F32)
                for k in range(RANKS)
            ]
            + [jnp.zeros((8 - RANKS, D), F32)],
            axis=0,
        ).astype(BF)
        tables = mm(flat, table_order())
        for k in range(RANKS):
            for h in range(HPR):
                row = tables[k : k + 1, BUCKETS * h : BUCKETS * (h + 1)]
                table_s[k, h : h + 1, :] = jnp.concatenate(
                    [
                        row,
                        jnp.broadcast_to(row[:, 255:256], (1, BLK)),
                        jnp.broadcast_to(row[:, 0:1], (1, BLK)),
                    ],
                    axis=1,
                )

    pltpu.make_async_copy(att0_ref.at[0:D], att_s.at[s], main_sem.at[s]).wait()
    for src_row, src_col, dst_row, dst_col in qkv_pieces():
        wq_ref[0, dst_row : dst_row + 96, dst_col : dst_col + PART] = att_s[
            s, src_row : src_row + 96, src_col : src_col + PART
        ]

    first = tails_ref[s, 0:1, :]
    bias = jnp.concatenate(
        [first[:, 0:PART], jnp.zeros((1, PART), BF), first[:, PART : 2 * PART]], axis=1
    ).astype(F32)
    qkv = (mm(xp_ref[...], wq_ref[0]) + bias).astype(BF)
    qkv_ref[0] = qkv

    seg_j = segment_of(lax.broadcasted_iota(jnp.int32, (1, L), 1), len_ref)
    table = table_s[s]
    heads = []
    for h in range(HPR):
        q = qkv[:, HD * h : HD * (h + 1)]
        k = qkv[:, PART + HD * h : PART + HD * (h + 1)]
        v = qkv[:, 2 * PART + HD * h : 2 * PART + HD * (h + 1)]
        row = table[h : h + 1, :]
        near = pltpu.roll(jnp.broadcast_to(row, (BLK, 4 * BLK)), 0, 1, stride=1, stride_axis=0)
        far_right = jnp.broadcast_to(row[:, 255:256], (BLK, BLK))
        far_left = jnp.broadcast_to(row[:, 511:512], (BLK, BLK))
        for i in range(NBLK):
            seg_i = segment_of(
                lax.broadcasted_iota(jnp.int32, (BLK, 1), 0) + BLK * i, len_ref
            )
            parts = []
            for jb in range(NBLK):
                delta = jb - i
                if abs(delta) <= 1:
                    parts.append(near[:, BLK * (delta + 1) : BLK * (delta + 2)])
                else:
                    parts.append(far_right if delta > 0 else far_left)
            logits = mm_nt(q[BLK * i : BLK * (i + 1)], k) * 0.125 + jnp.concatenate(parts, axis=1)
            logits = jnp.where(seg_i == seg_j, logits, NEG)
            top = jnp.max(logits, axis=-1, keepdims=True)
            expo = jnp.exp(logits - top)
            total = jnp.sum(expo, axis=-1, keepdims=True)
            probs_ref[0, h, BLK * i : BLK * (i + 1), :] = (expo * (1.0 / total)).astype(BF)
        heads.append(mm(probs_ref[0, h], v))
    mixed = jnp.concatenate(heads, axis=1).astype(BF)
    mixed_ref[0] = mixed
    acc_s[...] += mm(mixed, att_s[s, QKV_ROWS:D, :])

    @pl.when(s == RANKS - 1)
    def _():
        vec = vector_rows(tails_ref, PlaceView(scal_ref))
        normed, inv = normalize(x_ref[...].astype(F32) + acc_s[...] + vec[0])
        n1_ref[...] = normed
        r1_ref[...] = jnp.broadcast_to(inv, (L, BLK))


def attention_forward(scalars, x, atts):
    per = lambda *shape: pl.BlockSpec((1, *shape), lambda s, n: (s,) + (0,) * len(shape))
    return call(
        att_fwd_kernel,
        "attention_forward", (RANKS,),
        [whole(L, D)] + [pl.BlockSpec(memory_space=pl.ANY)] * RANKS,
        [
            per(L, QKV_ROWS), per(D, QKV_ROWS), per(L, PART), per(HPR, L, L),
            whole(L, D), whole(L, D), whole(L, BLK), whole(RANKS, TILE_ROWS, D),
        ],
        [
            shaped(BF, RANKS, L, QKV_ROWS),
            shaped(BF, RANKS, D, QKV_ROWS),
            shaped(BF, RANKS, L, PART),
            shaped(BF, RANKS, HPR, L, L),
            shaped(BF, L, D),
            shaped(F32, L, D),
            shaped(F32, L, BLK),
            shaped(BF, RANKS, TILE_ROWS, D),
        ],
        [
            pltpu.VMEM((RANKS, 8, 512), F32),
            pltpu.VMEM((L, D), F32),
            pltpu.VMEM((RANKS, D, D), BF),
            pltpu.SemaphoreType.DMA((RANKS,)),
            pltpu.SemaphoreType.DMA((RANKS,)),
        ],
        (scalars, x, *atts),
        flops=6_000_000_000, moved=24_000_000,
    )


def ffn_kernel(
    place_ref, n1_ref, r1_ref, og_ref, up0_ref, down0_ref, up1_ref, down1_ref, tails_ref,
    block_ref, grad0_ref, grad1_ref, grad_one_ref, ga_ref, vec_ref, bup_ref,
    fn_s, fl_s, slope_s, act_s, down_s, gd_s, gf_s, og_s, og_sem,
):
    step = pl.program_id(0)
    inv_root2 = 1.0 / math.sqrt(2.0)

    @pl.when(step == 0)
    def _():
        vec = vector_rows(tails_ref, PlaceView(place_ref))
        first = n1_ref[...] * vec[2] + vec[3]
        pltpu.make_async_copy(og_ref, og_s, og_sem).start()
        fn_s[...] = first
        fl_s[...] = first.astype(BF)
        down_s[...] = jnp.zeros_like(down_s)

    def forward(slot, up_ref, down_ref):
        bias = jnp.concatenate([tails_ref[slot, 0:1, 384:768], tails_ref[slot, 1:2, 0:384]], axis=1)
        up = mm(fl_s[...], up_ref[0]) + bias.astype(F32)
        half = 0.5 * (1.0 + lax.erf(up * inv_root2))
        act = (up * half).astype(BF)
        slope_s[slot] = half + up * jnp.exp(-0.5 * up * up) * (1.0 / math.sqrt(2.0 * math.pi))
        act_s[slot] = act
        down_s[...] += mm(act, down_ref[0])

    @pl.when(step < 2)
    def _():
        forward(step, up0_ref, down0_ref)

    @pl.when((step == 2) | (step == 3))
    def _():
        forward(step, up1_ref, down1_ref)

    @pl.when(step == RANKS)
    def _():
        vec = vector_rows(tails_ref, PlaceView(place_ref))
        normed, inv = normalize(fn_s[...] + down_s[...] + vec[1])
        block_ref[...] = (normed * vec[4] + vec[5]).astype(BF)
        pltpu.make_async_copy(og_ref, og_s, og_sem).wait()
        og = og_s[...].astype(F32)
        vec_ref[4:5, :] = col_sum(og * normed)
        vec_ref[5:6, :] = col_sum(og)
        grad_two = norm_backward(og * vec[4], normed, inv)
        low = grad_two.astype(BF)
        gd_s[...] = low
        vec_ref[1:2, :] = col_sum(low.astype(F32))
        vec_ref[6:8, :] = jnp.zeros((2, D), F32)
        gf_s[...] = grad_two

    def backward(slot, up_ref, down_ref, grad_ref):
        gd = gd_s[...]
        grad_ref[0, D:FF_ROWS, :] = mm_tn(act_s[slot], gd).astype(BF)
        gu = (mm_nt(gd, down_ref[0]) * slope_s[slot]).astype(BF)
        bup_ref[0, 0:1, :] = col_sum(gu.astype(F32))
        bup_ref[0, 1:8, :] = jnp.zeros((7, D), F32)
        grad_ref[0, 0:D, :] = mm_tn(fl_s[...], gu).astype(BF)
        gf_s[...] += mm_nt(gu, up_ref[0])

    @pl.when((step == 4) | (step == 5))
    def _():
        backward(step - 2, up1_ref, down1_ref, grad1_ref)

    @pl.when(step >= 6)
    def _():
        backward(step - 6, up0_ref, down0_ref, grad0_ref)

    @pl.when(step == 2 * RANKS - 1)
    def _():
        vec = vector_rows(tails_ref, PlaceView(place_ref))
        f = gf_s[...]
        normed = n1_ref[...]
        vec_ref[2:3, :] = col_sum(f * normed)
        vec_ref[3:4, :] = col_sum(f)
        grad_one = norm_backward(f * vec[2], normed, r1_ref[:, 0:1])
        grad_one_ref[...] = grad_one
        low = grad_one.astype(BF)
        ga_ref[...] = low
        vec_ref[0:1, :] = col_sum(low.astype(F32))


def feed_forward(place, n1, r1, out_grad, own_ff, got_ff, tails):
    def own_at(half):
        return lambda s, n: ((((s >= 1) & (s <= 3)) | (s == 7)).astype(jnp.int32), half, 0)

    def got_at(half):
        return lambda s, n: (((s == 3) | (s >= 5)).astype(jnp.int32), half, 0)

    wt = lambda index: pl.BlockSpec((1, D, D), index)
    return call(
        ffn_kernel,
        "feed_forward", (2 * RANKS,),
        [
            whole(L, D), whole(L, BLK), pl.BlockSpec(memory_space=pl.ANY),
            wt(own_at(0)), wt(own_at(1)), wt(got_at(0)), wt(got_at(1)),
            whole(RANKS, TILE_ROWS, D),
        ],
        [
            whole(L, D),
            pl.BlockSpec((1, FF_ROWS, D), lambda s, n: ((s >= 7).astype(jnp.int32), 0, 0)),
            pl.BlockSpec((1, FF_ROWS, D), lambda s, n: ((s >= 5).astype(jnp.int32), 0, 0)),
            whole(L, D), whole(L, D), whole(8, D),
            pl.BlockSpec((1, 8, D), lambda s, n: (lax.rem(jnp.maximum(s, 4) - 2, 4), 0, 0)),
        ],
        [
            shaped(BF, L, D),
            shaped(BF, SLOTS, FF_ROWS, D),
            shaped(BF, SLOTS, FF_ROWS, D),
            shaped(F32, L, D),
            shaped(BF, L, D),
            shaped(F32, 8, D),
            shaped(F32, RANKS, 8, D),
        ],
        [
            pltpu.VMEM((L, D), F32),
            pltpu.VMEM((L, D), BF),
            pltpu.VMEM((RANKS, L, D), F32),
            pltpu.VMEM((RANKS, L, D), BF),
            pltpu.VMEM((L, D), F32),
            pltpu.VMEM((L, D), BF),
            pltpu.VMEM((L, D), F32),
            pltpu.VMEM((L, D), BF),
            pltpu.SemaphoreType.DMA,
        ],
        (place, n1, r1, out_grad, own_ff, own_ff, got_ff, got_ff, tails),
        flops=14_500_000_000, moved=36_000_000,
    )


def diagonal_sums(block):
    half = block.shape[0] // 2
    while half >= 8:
        block = block[:half] + pltpu.roll(block[half:], 4 * BLK - half, 1)
        half //= 2
    row = lax.broadcasted_iota(jnp.int32, (8, 1), 0)
    for bit in (4, 2, 1):
        block = jnp.where((row & bit) > 0, pltpu.roll(block, 4 * BLK - bit, 1), block)
    return col_sum(block)


def att_bwd_kernel(
    place_ref, ga_ref, att0_ref, att1_ref, att2_ref, att3_ref,
    qkv_ref, probs_ref, mixed_ref, wq_ref, xp_ref, vec_ref, bup_ref, grad_one_ref,
    da0_ref, da1_ref, da2_ref, da3_ref, in_grad_ref,
    ds_s, near_s, sums_s, dx_s, order_s, wo_s, das_s, xp_s, one_s, sem, out_sem, late_sem,
):
    s = pl.program_id(0)
    slot = RANKS - 1 - s
    da_s = das_s.at[lax.rem(s, 2)]

    def leave(k):
        da_ref = (da0_ref, da1_ref, da2_ref, da3_ref)[k]
        return pltpu.make_async_copy(das_s.at[(RANKS - 1 - k) % 2], da_ref, out_sem.at[k])

    for k in range(2):

        @pl.when(slot == k)
        def _(k=k):
            leave(k + 2).wait()

    @pl.when(s == 0)
    def _():
        for k, att in enumerate((att0_ref, att1_ref, att2_ref, att3_ref)):
            pltpu.make_async_copy(att.at[QKV_ROWS:D], wo_s.at[k], sem.at[k]).start()
        pltpu.make_async_copy(xp_ref, xp_s, late_sem.at[0]).start()
        pltpu.make_async_copy(grad_one_ref, one_s, late_sem.at[1]).start()
        order_s[...] = table_order()
        dx_s[...] = jnp.zeros_like(dx_s)
        sums_s[...] = jnp.zeros_like(sums_s)

    ga = ga_ref[...]
    da_s[QKV_ROWS:D, :] = mm_tn(mixed_ref[0], ga).astype(BF)
    pltpu.make_async_copy(att0_ref.at[QKV_ROWS:D], wo_s.at[slot], sem.at[slot]).wait()
    dm_all = mm_nt(ga, wo_s[slot]).astype(BF)
    qkv = qkv_ref[0]
    dq, dk, dv = [], [], []
    for h in range(HPR):
        q = qkv[:, HD * h : HD * (h + 1)]
        k = qkv[:, PART + HD * h : PART + HD * (h + 1)]
        v = qkv[:, 2 * PART + HD * h : 2 * PART + HD * (h + 1)]
        dm = dm_all[:, HD * h : HD * (h + 1)]
        far_left = jnp.zeros((BLK, BLK), F32)
        far_right = jnp.zeros((BLK, BLK), F32)
        for i in range(NBLK):
            rows = slice(BLK * i, BLK * (i + 1))
            p = probs_ref[0, h, rows, :].astype(F32)
            dp = mm_nt(dm[rows], v)
            ds = (p * (dp - jnp.sum(p * dp, axis=-1, keepdims=True))).astype(BF)
            ds_s[rows, :] = ds
            ds = ds.astype(F32)
            for jb in range(NBLK):
                piece = ds[:, BLK * jb : BLK * (jb + 1)]
                delta = jb - i
                if abs(delta) <= 1:
                    cols = slice(BLK * (delta + 1), BLK * (delta + 2))
                    if i == max(0, -delta):
                        near_s[:, cols] = piece
                    else:
                        near_s[:, cols] += piece
                elif delta > 0:
                    far_right += piece
                else:
                    far_left += piece
        near_s[:, 3 * BLK :] = jnp.zeros((BLK, BLK), F32)
        sums_s[h : h + 1, 0 : 4 * BLK] = diagonal_sums(near_s[...])
        sums_s[h : h + 1, 4 * BLK : 5 * BLK] = col_sum(far_left)
        sums_s[h : h + 1, 5 * BLK : 6 * BLK] = col_sum(far_right)
        dscore = ds_s[...]
        dq.append(mm(dscore, k) * 0.125)
        dk.append(mm_tn(dscore, q) * 0.125)
        dv.append(mm_tn(probs_ref[0, h], dm))
    dqkv = jnp.concatenate(dq + dk + dv, axis=1).astype(BF)

    qv = col_sum(dqkv.astype(F32))
    sums = sums_s[...]
    lane = lax.broadcasted_iota(jnp.int32, (1, 6 * BLK), 1)
    is_left = (lane == 0) | ((lane >= 3 * BLK) & (lane < 5 * BLK))
    is_right = ((lane >= BUCKETS - 1) & (lane < 3 * BLK)) | (lane >= 5 * BLK)
    left = jnp.sum(jnp.where(is_left, sums, 0.0), axis=-1, keepdims=True)
    right = jnp.sum(jnp.where(is_right, sums, 0.0), axis=-1, keepdims=True)
    sums = jnp.where(lane == 0, left, jnp.where(lane == BUCKETS - 1, right, sums))
    table = jnp.concatenate([sums[h : h + 1, :BUCKETS] for h in range(HPR)], axis=1)
    table = jnp.broadcast_to(table, (8, D)).astype(BF)
    table = mm_nt(table, order_s[...])[0:1]
    r = slice_of(slot, PlaceView(place_ref))
    vecs = []
    for i in range(3):
        m = 3 * r + i
        row = vec_ref[pl.ds(m // 2, 1), :]
        vecs.append(jnp.where(m % 2 == 0, row[:, 0:384], row[:, 384:768]))
    bup = bup_ref[0, 0:1, :]
    tail = jnp.concatenate(
        [
            jnp.concatenate([qv[:, 0:PART], qv[:, 2 * PART :], bup[:, 0:384]], axis=1),
            jnp.concatenate([bup[:, 384:768], table[:, 0:384]], axis=1),
            jnp.concatenate([table[:, 384:768], vecs[0]], axis=1),
            jnp.concatenate([vecs[1], vecs[2]], axis=1),
            jnp.zeros((TILE_ROWS - 4, D), F32),
        ],
        axis=0,
    )
    da_s[D:ATT_ROWS, :] = tail.astype(BF)

    @pl.when(s == 0)
    def _():
        pltpu.make_async_copy(xp_ref, xp_s, late_sem.at[0]).wait()

    dw = mm_tn(xp_s[...], dqkv).astype(BF)
    for src_row, src_col, dst_row, dst_col in qkv_pieces():
        da_s[src_row : src_row + 96, src_col : src_col + PART] = dw[
            dst_row : dst_row + 96, dst_col : dst_col + PART
        ]
    dx_s[...] += mm_nt(dqkv, wq_ref[0])

    for k in range(RANKS):

        @pl.when(slot == k)
        def _(k=k):
            leave(k).start()

    @pl.when(s == RANKS - 1)
    def _():
        pltpu.make_async_copy(grad_one_ref, one_s, late_sem.at[1]).wait()
        in_grad_ref[...] = one_s[...] + mm_nt(dx_s[...].astype(BF), column_order())
        for k in range(2):
            leave(k).wait()


def attention_backward(scalars, ga, atts, qkv, wq, mixed, probs, xp, vec_g, up_g, grad_one):
    per = lambda *shape: pl.BlockSpec((1, *shape), lambda s, n: (RANKS - 1 - s,) + (0,) * len(shape))
    return call(
        att_bwd_kernel,
        "attention_backward", (RANKS,),
        [whole(L, D)]
        + [pl.BlockSpec(memory_space=pl.ANY)] * RANKS
        + [
            per(L, QKV_ROWS), per(HPR, L, L), per(L, PART), per(D, QKV_ROWS),
            pl.BlockSpec(memory_space=pl.ANY), whole(8, D), per(8, D), pl.BlockSpec(memory_space=pl.ANY),
        ],
        [pl.BlockSpec(memory_space=pl.ANY)] * RANKS + [whole(L, D)],
        [shaped(BF, ATT_ROWS, D)] * RANKS + [shaped(F32, L, D)],
        [
            pltpu.VMEM((L, L), BF),
            pltpu.VMEM((BLK, 4 * BLK), F32),
            pltpu.VMEM((8, 6 * BLK), F32),
            pltpu.VMEM((L, D), F32),
            pltpu.VMEM((D, D), BF),
            pltpu.VMEM((RANKS, PART, D), BF),
            pltpu.VMEM((2, ATT_ROWS, D), BF),
            pltpu.VMEM((L, D), BF),
            pltpu.VMEM((L, D), F32),
            pltpu.SemaphoreType.DMA((RANKS,)),
            pltpu.SemaphoreType.DMA((RANKS,)),
            pltpu.SemaphoreType.DMA((2,)),
        ],
        (scalars, ga, *atts, qkv, probs, mixed, wq, xp, vec_g, up_g, grad_one),
        flops=12_000_000_000, moved=30_000_000,
    )


X_SWAP = [(w, w ^ 1) for w in range(8)]
Z_RING = [(w, (w + 2) % 8) for w in range(8)]
Y_SWAP = [(n, n ^ 2) for n in range(4)]
CORE_SWAP = [(n, n ^ 1) for n in range(4)]


def swap_x(a):
    return lax.ppermute(a, "wide", X_SWAP)


def swap_y(a):
    return lax.ppermute(a, "narrow", Y_SWAP)


def ring_z(a):
    return lax.ppermute(a, "wide", Z_RING)


def ring_back(a):
    return lax.ppermute(a, "wide", [(j, i) for i, j in Z_RING])


def swap_core(a):
    return lax.ppermute(a, "narrow", CORE_SWAP)


def after(value, earlier):
    return lax.optimization_barrier((value, earlier))[0]


def aligned_plan(shard, wide, ranks):
    unit = TILE_ROWS * D
    tiles, spare = divmod(shard, unit)
    rows = tiles * TILE_ROWS
    fits = (
        wide == 8
        and ranks == RANKS
        and spare * wide <= unit
        and spare % 128 == 0
        and rows * wide == MAT_ROWS
        and rows == QKV_ROWS // 2
    )
    return rows, spare, fits


def window_places(z, x):
    planes = jnp.mod(z - jnp.arange(4, dtype=jnp.int32), 4)
    return jnp.concatenate([2 * planes + x, 2 * planes + 1 - x])


def gather_blocks(r0, z, x, rows):
    r1, x0, y0 = ring_z(r0), swap_x(r0), swap_y(r0)
    d0 = swap_y(after(x0, y0))
    r2, x1, y1 = ring_z(r1), swap_x(after(r1, x0)), swap_y(after(r1, y0))
    r3, x2, y2 = ring_z(r2), swap_x(after(r2, x0)), swap_y(after(r2, d0))
    d1 = ring_z(after(d0, y1))
    x3 = swap_x(after(r3, x1))
    y3, d2, d3 = ring_z(after(y2, r3)), swap_x(after(y2, x2)), swap_y(after(x3, y1))
    at = window_places(z, x)
    near_att, ff = merge_blocks(at, (r0, r1, r2, r3, x0, x1, x2, x3), rows, 0)
    near_got = swap_core(near_att)
    far_att, ff = merge_blocks(at, (y0, y1, y2, y3, d0, d1, d2, d3), rows, 1, (ff,))
    far_got = swap_core(far_att)
    return ((near_att, far_att), ff), ((near_got, far_got), swap_core(after(ff, (near_got, far_got))))


def add_low(*terms):
    total = terms[0].astype(F32)
    for term in terms[1:]:
        total = total + term.astype(F32)
    return total.astype(BF)


def reduce_windows(own_att, got_att, own_ff, got_ff, z, x, rows):
    at = window_places(z, x)
    far_got = swap_core(got_att[1])
    near_got = swap_core(after(got_att[0], far_got))
    far = (own_att[1], own_att[1], own_ff), (far_got, far_got, got_ff)
    a = split_windows(at, ("D3", "Y3", "D2"), *far, rows)
    y1, z1, x1 = swap_y(a["D3"]), ring_back(a["Y3"]), swap_x(a["D2"])
    both = (*own_att, own_ff), (near_got, far_got, got_ff)
    a |= split_windows(
        at, ("X3", "Y2", "Y1", "D1", "R3", "X2", "R2", "X1", "R1", "D0", "X0", "Y0", "R0"), *both, rows
    )
    z2 = ring_back(after(a["D1"], x1))
    y3 = swap_y(after(a["Y1"], x1))
    far = add_low(a["X3"], y1)
    x2 = swap_x(far)
    y2 = swap_y(add_low(a["Y2"], z1, x1))
    x3 = swap_x(after(a["X2"], x2))
    z3 = ring_back(add_low(a["R3"], x2))
    x4 = swap_x(after(a["X1"], x2))
    y4 = swap_y(add_low(a["D0"], z2))
    z4 = ring_back(add_low(a["R2"], y2, z3, x3))
    y5 = swap_y(after(a["Y0"], y2))
    z5 = ring_back(add_low(a["R1"], y3, z4, x4))
    x5 = swap_x(add_low(a["X0"], y4))
    return a["R0"], z5, x5, y5


def gather_plain(params):
    flat = lax.all_gather(params.astype(BF)[0], "wide", axis=0, tiled=True)
    flat = jnp.pad(flat, (0, PAD_ROWS * D - flat.shape[0])).reshape(PAD_ROWS, D)
    head = jnp.swapaxes(flat[:QKV_ROWS].reshape(2, 96, 3, D), 1, 2).reshape(QKV_ROWS, D)
    flat = jnp.concatenate([head, flat[QKV_ROWS:]], axis=0)
    mats = lax.all_gather(flat, "narrow", axis=0, tiled=True).reshape(2, 2, PAD_ROWS, D)
    pairs = []
    for core in range(2):
        pair = mats[:, core]
        pairs.append((jnp.concatenate([pair[:, :D], pair[:, MAT_ROWS:]], axis=1), pair[:, D:MAT_ROWS]))
    return pairs


def scatter_plain(pairs, shard, wide):
    mats = [jnp.concatenate([att[:, :D], ff, att[:, D:]], axis=1) for att, ff in pairs]
    grads = jnp.stack(mats, axis=1).reshape(-1, D)
    mine = lax.psum_scatter(grads, "narrow", scatter_dimension=0, tiled=True)
    head = jnp.swapaxes(mine[:QKV_ROWS].reshape(2, 3, 96, D), 1, 2).reshape(QKV_ROWS, D)
    flat = jnp.concatenate([head, mine[QKV_ROWS:]], axis=0).reshape(-1)[: shard * wide]
    return lax.psum_scatter(flat.astype(F32), "wide", scatter_dimension=0, tiled=True).reshape(1, shard)


def body(hidden_in, out_grad, pair_lengths, params, momentum, average):
    wide, ranks = lax.axis_size("wide"), lax.axis_size("narrow")
    shard = params.shape[1]
    rows, spare, fits = aligned_plan(shard, wide, ranks)
    at_wide, at_narrow = lax.axis_index("wide"), lax.axis_index("narrow")
    if fits:
        place = jnp.stack([at_wide, at_narrow // 2, at_narrow % 2]).astype(jnp.int32)
        scalars = jnp.concatenate([pair_lengths[0], place])
        block = own_block(scalars, params, rows, spare, wide)
        (own_att, own_ff), (got_att, got_ff) = gather_blocks(block, at_wide // 2, at_wide % 2, rows)
    else:
        scalars = jnp.concatenate([pair_lengths[0], jnp.zeros((3,), jnp.int32)])
        (own_att, own_ff), (got_att, got_ff) = gather_plain(params)
    atts = (own_att[0], own_att[1], got_att[0], got_att[1])

    qkv, wq, mixed, probs, xp, n1, r1, tails = attention_forward(scalars, hidden_in, atts)
    block_out, own_ffg, got_ffg, grad_one, ga, vec_g, up_g = feed_forward(
        scalars, n1, r1, out_grad, own_ff, got_ff, tails
    )
    *attg, in_grad = attention_backward(scalars, ga, atts, qkv, wq, mixed, probs, xp, vec_g, up_g, grad_one)
    own_attg, got_attg = attg[:2], attg[2:]

    device_count = wide * ranks
    rate = 1.0 / (32.0 * math.sqrt(hidden_in.shape[0] * device_count))
    if fits:
        parts = reduce_windows(own_attg, got_attg, own_ffg, swap_core(got_ffg), at_wide // 2, at_wide % 2, rows)
        grads, new_params, new_momentum, new_average, low = update_shard(
            scalars, parts, params, momentum, average, rate, rows, spare, wide
        )
    else:
        grads = scatter_plain(((jnp.stack(own_attg), own_ffg), (jnp.stack(got_attg), got_ffg)), shard, wide)
        new_momentum = 0.5 * momentum + rate * grads
        new_params = params - (rate * grads + 0.5 * new_momentum)
        new_average = 0.5 * average + 0.5 * new_params
        low = new_params.astype(BF)
    return (
        block_out,
        in_grad,
        grads,
        new_params,
        new_momentum,
        new_average,
        low,
    )


def solution(mesh):
    rows = P(("wide", "narrow"), None)
    flat = P("narrow", "wide")
    return jax.shard_map(
        body,
        mesh=mesh,
        in_specs=(rows, rows, rows, flat, flat, flat),
        out_specs=(rows, rows, flat, flat, flat, flat, flat),
        check_vma=False,
    )
```
